32 devices in a mesh: rep: 8 (over z, y), shard: 4 (over x, core).
Axes of the slice: x: 2, y: 2, z: 4, core: 2. Of those that a mesh axis runs over, the one named last changes fastest.
Arguments:
- tokens: bfloat16 [4096, 1024], P(('rep', 'shard')), may hold values from -6 to 6
- cotangent: bfloat16 [4096, 1024], P(('rep', 'shard')), may hold values from -6 to 6
- doc_ids: int32 [4096], P(('rep', 'shard')), may hold values from -1 to 15, as said below
- w_query: bfloat16 [1024, 1024], P('shard'), may hold values from -0.1875 to 0.1875
- w_key: bfloat16 [1024, 512], P('shard'), may hold values from -0.1875 to 0.1875
- w_value: bfloat16 [1024, 512], P('shard'), may hold values from -0.1875 to 0.1875
- w_out: bfloat16 [1024, 1024], P('shard'), may hold values from -0.5 to 0.5
- w_gate: bfloat16 [1024, 4608], P('shard'), may hold values from -0.1875 to 0.1875
- w_up: bfloat16 [1024, 4608], P('shard'), may hold values from -0.1875 to 0.1875
- w_down: bfloat16 [4608, 1024], P('shard'), may hold values from -0.09375 to 0.09375
- gain_attn: bfloat16 [1024], P('shard'), may hold values from 0.5 to 1.5
- gain_ffn: bfloat16 [1024], P('shard'), may hold values from 0.5 to 1.5
- gain_query: bfloat16 [64], P('shard'), may hold values from 0.5 to 1.5
- gain_key: bfloat16 [64], P('shard'), may hold values from 0.5 to 1.5
Outputs:
- block_out: bfloat16 [4096, 1024], P(('rep', 'shard'))
- grad_tokens: float32 [4096, 1024], P(('rep', 'shard'))
- grad_w_query: float32 [1024, 1024], P('shard')
- grad_w_key: float32 [1024, 512], P('shard')
- grad_w_value: float32 [1024, 512], P('shard')
- grad_w_out: float32 [1024, 1024], P('shard')
- grad_w_gate: float32 [1024, 4608], P('shard')
- grad_w_up: float32 [1024, 4608], P('shard')
- grad_w_down: float32 [4608, 1024], P('shard')
- grad_gain_attn: float32 [1024], P('shard')
- grad_gain_ffn: float32 [1024], P('shard')
- grad_gain_query: float32 [64], P('shard')
- grad_gain_key: float32 [64], P('shard')
The draws below stay inside these ranges and needn't reach their ends.
Inputs may be any that keep to these rules, and one draw needn't show every extreme that they name: `doc_ids`: each device's 128 slots hold its sequences one after another, numbered from 0 upward without gaps, followed by its empty slots marked -1; at least one device has no empty slot and holds 16 sequences.
All inputs are finite; a program needn't handle non-finite values.
Results may differ from the reference program's by a relative error of at most 0.02.
Values may be sent and summed in bfloat16 or wider, within the bound.
A program may use at most 192 MiB of HBM per device.

```python
import math
import jax
import jax.numpy as jnp
from jax import lax

D = 1024
QH = 16
KVH = 8
HEAD_DIM = 64
FF = 4608
TOK_DEV = 128
QW = 1024
KW = 512
TOKENS = 4096
N_REP = 8
N_SHARD = 4


def draw_doc_ids(key, part):
    dev_count = TOKENS // TOK_DEV
    top_seq = TOK_DEV // 8 - 1
    key_live, key_full, key_cuts = jax.random.split(key, 3)
    live_count = jax.random.randint(key_live, (dev_count,), TOK_DEV // 4, TOK_DEV)
    full_device = jax.random.randint(key_full, (), 0, dev_count)
    is_full = jnp.arange(dev_count) == full_device
    live_count = jnp.where(is_full, TOK_DEV, live_count)
    cut_marks = (jax.random.randint(key_cuts, (dev_count, TOK_DEV), 0, 32) == 0).astype(jnp.int32)
    slot_index = jnp.arange(TOK_DEV)[None, :]
    even_cuts = (slot_index % 8 == 0).astype(jnp.int32)
    cut_marks = jnp.where(is_full[:, None], even_cuts, cut_marks)
    cut_marks = cut_marks.at[:, 0].set(0)
    seq_index = jnp.minimum(jnp.cumsum(cut_marks, axis=1), top_seq)
    seq_index = jnp.where(slot_index < live_count[:, None], seq_index, -1)
    return seq_index.reshape(-1).astype(jnp.int32)


def shard_levels(key, dims, cuts, least, high):
    factor_of = 1.0
    for dim, blocks in cuts:
        steps = jax.random.uniform(jax.random.fold_in(jax.random.fold_in(key, 6), dim), (blocks,), jnp.float32, least / len(cuts), high / len(cuts))
        factor_of = factor_of * jnp.repeat(jnp.exp(steps), dims[dim] // blocks).reshape((-1,) + (1,) * (len(dims) - 1 - dim))
    return factor_of


def noise(key, dims, scale, limit, cuts=(), kind=jnp.bfloat16):
    loudness = shard_levels(key, dims, cuts, -0.22, 0.18) if cuts else 1.0
    values = jax.random.normal(key, dims, jnp.float32) * scale * loudness
    return jnp.minimum(jnp.maximum(values, -limit), limit).astype(kind)


def setup_inputs(seed: int = 0) -> dict:
    key_list = jax.random.split(jax.random.key(seed), 15)
    tokens = noise(key_list[0], (TOKENS, D), 1.0, 6.0, ((0, 32),))
    cotangent = noise(key_list[1], (TOKENS, D), 1.0, 6.0, ((0, 32),))
    doc_ids = draw_doc_ids(jax.random.fold_in(key_list[14], 71), 0)
    w_query = noise(key_list[3], (D, QW), D ** -0.5, 0.1875, ((0, 4),))
    w_key = noise(key_list[4], (D, KW), D ** -0.5, 0.1875, ((0, 4),))
    w_value = noise(key_list[5], (D, KW), D ** -0.5, 0.1875, ((0, 4),))
    w_out = noise(key_list[6], (QW, D), (QW // 8) ** -0.5, 0.5, ((0, 4),))
    w_gate = noise(key_list[7], (D, FF), D ** -0.5, 0.1875, ((0, 4),))
    w_up = noise(key_list[8], (D, FF), D ** -0.5, 0.1875, ((0, 4),))
    w_down = noise(key_list[9], (FF, D), FF ** -0.5, 0.09375, ((0, 4),))
    gain_attn = jnp.clip(1.0 + 0.1 * jax.random.normal(key_list[10], (D,), jnp.float32), 0.5, 1.5).astype(jnp.bfloat16)
    gain_ffn = jnp.clip(1.0 + 0.1 * jax.random.normal(key_list[11], (D,), jnp.float32), 0.5, 1.5).astype(jnp.bfloat16)
    gain_query = jnp.clip(1.0 + 0.1 * jax.random.normal(key_list[12], (HEAD_DIM,), jnp.float32), 0.5, 1.5).astype(jnp.bfloat16)
    gain_key = jnp.clip(1.0 + 0.1 * jax.random.normal(key_list[13], (HEAD_DIM,), jnp.float32), 0.5, 1.5).astype(jnp.bfloat16)
    return {"tokens": tokens, "cotangent": cotangent, "doc_ids": doc_ids, "w_query": w_query, "w_key": w_key, "w_value": w_value, "w_out": w_out, "w_gate": w_gate, "w_up": w_up, "w_down": w_down, "gain_attn": gain_attn, "gain_ffn": gain_ffn, "gain_query": gain_query, "gain_key": gain_key}


NORM_EPSILON = 1e-05
ROPE_BASE = 1000000.0

def matmul(left, right):
    return jnp.dot(left, right, preferred_element_type=jnp.float32)

def norm_rows(values, gain_vec):
    inv_rms = lax.rsqrt(lax.optimization_barrier(jnp.mean(values * values, axis=-1, keepdims=True)) + NORM_EPSILON)
    normed = values * inv_rms
    return (normed * gain_vec.astype(jnp.float32), normed, inv_rms)

def norm_back(grad_out, normed, inv_rms, gain_vec):
    scaled = grad_out * gain_vec.astype(jnp.float32)
    grad_in = inv_rms * (scaled - normed * lax.optimization_barrier(jnp.mean(scaled * normed, axis=-1, keepdims=True)))
    return grad_in

def round_total(batched):
    rounded = lax.optimization_barrier(batched.astype(jnp.bfloat16))
    return lax.optimization_barrier(jnp.sum(rounded.astype(jnp.float32), axis=0))

def device_product(left, right, dev_group):
    left_dev = left.reshape(dev_group, -1, left.shape[-1]).astype(jnp.float32)
    right_dev = right.reshape(dev_group, -1, right.shape[-1]).astype(jnp.float32)
    return round_total(jnp.einsum('gta,gtb->gab', left_dev, right_dev))

def device_gain(grad_out, normed, dev_group):
    product = (grad_out * normed).reshape(dev_group, -1, grad_out.shape[-1])
    return round_total(lax.optimization_barrier(jnp.sum(product, axis=1)))

def doc_tables(doc_rows):
    block_len = doc_rows.shape[-1]
    row_index = jnp.arange(block_len)[:, None]
    col_index = jnp.arange(block_len)[None, :]
    same_doc = doc_rows[:, :, None] == doc_rows[:, None, :]
    allowed = same_doc & (row_index >= col_index)[None]
    earlier = same_doc & (row_index > col_index)[None]
    positions = lax.optimization_barrier(jnp.sum(earlier.astype(jnp.int32), axis=2))
    return (allowed, positions)

def rope_tables(positions, head_dim):
    half_dim = head_dim // 2
    inv_freq = jnp.exp(jnp.arange(half_dim).astype(jnp.float32) * (-2.0 * math.log(ROPE_BASE) / head_dim))
    angles = positions.astype(jnp.float32)[:, :, None, None] * inv_freq
    return (jnp.cos(angles), jnp.sin(angles))

def rotate(values, cos_tab, sin_tab):
    half_dim = values.shape[-1] // 2
    part_one = values[..., :half_dim]
    part_two = values[..., half_dim:]
    return jnp.concatenate([part_one * cos_tab - part_two * sin_tab, part_two * cos_tab + part_one * sin_tab], axis=-1)

def rotate_back(values, cos_tab, sin_tab):
    half_dim = values.shape[-1] // 2
    part_one = values[..., :half_dim]
    part_two = values[..., half_dim:]
    return jnp.concatenate([part_one * cos_tab + part_two * sin_tab, part_two * cos_tab - part_one * sin_tab], axis=-1)

def reference(tokens, cotangent, doc_ids, w_query, w_key, w_value, w_out, w_gate, w_up, w_down, gain_attn, gain_ffn, gain_query, gain_key):
    devices = N_REP * N_SHARD
    dev_group = math.gcd(devices, max(1, 1024 // TOK_DEV))
    blocks = devices // dev_group
    block_rows = dev_group * TOK_DEV
    head_share = QH // KVH
    score_scale = 1.0 / math.sqrt(HEAD_DIM)

    def block_step(totals, pieces):
        block_tokens, block_cot, doc_rows = pieces
        allowed, positions = doc_tables(doc_rows)
        key_mask = allowed[:, None, None]
        cos_tab, sin_tab = rope_tables(positions, HEAD_DIM)
        resid_in = block_tokens.astype(jnp.float32)
        normed_in, unit_in, rms_in = norm_rows(resid_in, gain_attn)
        normed_bf = normed_in.astype(jnp.bfloat16)
        query_raw = matmul(normed_bf, w_query).reshape(dev_group, TOK_DEV, QH, HEAD_DIM)
        key_raw = matmul(normed_bf, w_key).reshape(dev_group, TOK_DEV, KVH, HEAD_DIM)
        value_bf = matmul(normed_bf, w_value).astype(jnp.bfloat16).reshape(dev_group, TOK_DEV, KVH, HEAD_DIM)
        query_normed, query_unit, query_rms = norm_rows(query_raw, gain_query)
        key_normed, key_unit, key_rms = norm_rows(key_raw, gain_key)
        query_bf = rotate(query_normed, cos_tab, sin_tab).astype(jnp.bfloat16).reshape(dev_group, TOK_DEV, KVH, head_share, HEAD_DIM)
        key_bf = rotate(key_normed, cos_tab, sin_tab).astype(jnp.bfloat16)
        scores = jnp.einsum('gqkrd,gskd->gkrqs', query_bf.astype(jnp.float32), key_bf.astype(jnp.float32)) * score_scale
        log_total = jnp.log(lax.optimization_barrier(jnp.sum(jnp.where(key_mask, jnp.exp(scores), 0.0), axis=-1, keepdims=True)))
        attn_probs = jnp.where(key_mask, jnp.exp(scores - log_total), 0.0)
        probs_bf = attn_probs.astype(jnp.bfloat16)
        mixed_bf = jnp.einsum('gkrqs,gskd->gqkrd', probs_bf.astype(jnp.float32), value_bf.astype(jnp.float32)).astype(jnp.bfloat16).reshape(block_rows, QH * HEAD_DIM)
        resid_mid = resid_in + matmul(mixed_bf, w_out)
        normed_mid, unit_mid, rms_mid = norm_rows(resid_mid, gain_ffn)
        hidden_in = normed_mid.astype(jnp.bfloat16)
        gate_proj = matmul(hidden_in, w_gate)
        up_proj = matmul(hidden_in, w_up)
        gate_sig = jax.nn.sigmoid(gate_proj)
        gate_act = gate_proj * gate_sig
        hidden_bf = (gate_act * up_proj).astype(jnp.bfloat16)
        block_out = (resid_mid + matmul(hidden_bf, w_down)).astype(jnp.bfloat16)
        live_rows = (doc_rows.reshape(block_rows) >= 0).astype(jnp.float32)[:, None]
        grad_y = block_cot.astype(jnp.float32) * live_rows
        grad_y_bf = grad_y.astype(jnp.bfloat16)
        part_down = device_product(hidden_bf, grad_y_bf, dev_group)
        grad_hidden = matmul(grad_y_bf, w_down.T)
        grad_gate_bf = (grad_hidden * up_proj * gate_sig * (1.0 + gate_proj * (1.0 - gate_sig))).astype(jnp.bfloat16)
        grad_up_bf = (grad_hidden * gate_act).astype(jnp.bfloat16)
        part_gate = device_product(hidden_in, grad_gate_bf, dev_group)
        part_up = device_product(hidden_in, grad_up_bf, dev_group)
        grad_norm_mid = matmul(grad_gate_bf, w_gate.T) + matmul(grad_up_bf, w_up.T)
        back_mid = norm_back(grad_norm_mid, unit_mid, rms_mid, gain_ffn)
        part_gffn = device_gain(grad_norm_mid, unit_mid, dev_group)
        grad_mid = grad_y + back_mid
        grad_mid_bf = grad_mid.astype(jnp.bfloat16)
        part_out = device_product(mixed_bf, grad_mid_bf, dev_group)
        grad_mixed_bf = matmul(grad_mid_bf, w_out.T).astype(jnp.bfloat16).reshape(dev_group, TOK_DEV, KVH, head_share, HEAD_DIM)
        grad_scores = jnp.einsum('gqkrd,gskd->gkrqs', grad_mixed_bf.astype(jnp.float32), value_bf.astype(jnp.float32))
        grad_value_bf = jnp.einsum('gkrqs,gqkrd->gskd', probs_bf.astype(jnp.float32), grad_mixed_bf.astype(jnp.float32)).astype(jnp.bfloat16).reshape(block_rows, KVH * HEAD_DIM)
        row_dot = lax.optimization_barrier(jnp.sum(attn_probs * grad_scores, axis=-1, keepdims=True))
        grad_logits = (attn_probs * (grad_scores - row_dot) * score_scale).astype(jnp.bfloat16)
        grad_query_rot = jnp.einsum('gkrqs,gskd->gqkrd', grad_logits.astype(jnp.float32), key_bf.astype(jnp.float32)).reshape(dev_group, TOK_DEV, QH, HEAD_DIM)
        grad_key_rot = jnp.einsum('gkrqs,gqkrd->gskd', grad_logits.astype(jnp.float32), query_bf.astype(jnp.float32))
        query_back = rotate_back(grad_query_rot, cos_tab, sin_tab)
        key_back = rotate_back(grad_key_rot, cos_tab, sin_tab)
        grad_query_raw = norm_back(query_back, query_unit, query_rms, gain_query)
        grad_key_raw = norm_back(key_back, key_unit, key_rms, gain_key)
        part_gquery = device_gain(query_back, query_unit, dev_group)
        part_gkey = device_gain(key_back, key_unit, dev_group)
        grad_query_bf = grad_query_raw.astype(jnp.bfloat16).reshape(block_rows, QH * HEAD_DIM)
        grad_key_bf = grad_key_raw.astype(jnp.bfloat16).reshape(block_rows, KVH * HEAD_DIM)
        part_query = device_product(normed_bf, grad_query_bf, dev_group)
        part_key = device_product(normed_bf, grad_key_bf, dev_group)
        part_value = device_product(normed_bf, grad_value_bf, dev_group)
        grad_norm_in = matmul(grad_query_bf, w_query.T) + matmul(grad_key_bf, w_key.T) + matmul(grad_value_bf, w_value.T)
        back_in = norm_back(grad_norm_in, unit_in, rms_in, gain_attn)
        part_gattn = device_gain(grad_norm_in, unit_in, dev_group)
        grad_input = grad_mid + back_in
        parts = (part_query, part_key, part_value, part_out, part_gate, part_up, part_down, part_gattn, part_gffn, part_gquery, part_gkey)
        totals = tuple((total_one + part_one for total_one, part_one in zip(totals, parts)))
        return (totals, (block_out, grad_input))
    shapes = [w_query.shape, w_key.shape, w_value.shape, w_out.shape, w_gate.shape, w_up.shape, w_down.shape, gain_attn.shape, gain_ffn.shape, gain_query.shape, gain_key.shape]
    start = tuple((jnp.zeros(shape_one, jnp.float32) for shape_one in shapes))
    inputs = (tokens.reshape(blocks, block_rows, D), cotangent.reshape(blocks, block_rows, D), doc_ids.reshape(blocks, dev_group, TOK_DEV))
    totals, stacked = lax.scan(block_step, start, inputs)
    block_out = stacked[0].reshape(TOKENS, D)
    grad_tokens = stacked[1].reshape(TOKENS, D)
    return (block_out, grad_tokens, totals[0], totals[1], totals[2], totals[3], totals[4], totals[5], totals[6], totals[7], totals[8], totals[9], totals[10])
```

```python
import functools
import math

import jax
import jax.numpy as jnp
from jax import lax
from jax.experimental import pallas as pl
from jax.experimental.pallas import tpu as pltpu
from jax.sharding import PartitionSpec as P

MESH = pl.DeviceIdType.MESH

QH = 16
KVH = 8
HEAD_DIM = 64


NORM_EPSILON = 1e-05
ROPE_BASE = 1000000.0


def matmul(left, right):
    return jnp.dot(left, right, preferred_element_type=jnp.float32)


def norm_rows(values, gain_vec):
    inv_rms = lax.rsqrt(jnp.mean(values * values, axis=-1, keepdims=True) + NORM_EPSILON)
    normed = values * inv_rms
    return (normed * gain_vec.astype(jnp.float32), normed, inv_rms)


def norm_back(grad_out, normed, inv_rms, gain_vec):
    scaled = grad_out * gain_vec.astype(jnp.float32)
    grad_in = inv_rms * (scaled - normed * jnp.mean(scaled * normed, axis=-1, keepdims=True))
    lead_axes = tuple(range(grad_out.ndim - 1))
    return (grad_in, jnp.sum(grad_out * normed, axis=lead_axes))


def doc_tables(doc_rows):
    block_len = doc_rows.shape[-1]
    row_index = jnp.arange(block_len)[:, None]
    col_index = jnp.arange(block_len)[None, :]
    same_doc = doc_rows[:, :, None] == doc_rows[:, None, :]
    allowed = same_doc & (row_index >= col_index)[None]
    earlier = same_doc & (row_index > col_index)[None]
    positions = jnp.sum(earlier.astype(jnp.int32), axis=2)
    return (allowed, positions)


def rope_tables(positions, head_dim):
    half_dim = head_dim // 2
    inv_freq = jnp.exp(
        jnp.arange(half_dim).astype(jnp.float32) * (-2.0 * math.log(ROPE_BASE) / head_dim)
    )
    angles = positions.astype(jnp.float32)[:, :, None, None] * inv_freq
    return (jnp.cos(angles), jnp.sin(angles))


def rotate(values, cos_tab, sin_tab):
    half_dim = values.shape[-1] // 2
    part_one = values[..., :half_dim]
    part_two = values[..., half_dim:]
    return jnp.concatenate(
        [part_one * cos_tab - part_two * sin_tab, part_two * cos_tab + part_one * sin_tab], axis=-1
    )


def rotate_back(values, cos_tab, sin_tab):
    half_dim = values.shape[-1] // 2
    part_one = values[..., :half_dim]
    part_two = values[..., half_dim:]
    return jnp.concatenate(
        [part_one * cos_tab + part_two * sin_tab, part_two * cos_tab - part_one * sin_tab], axis=-1
    )


def attn_probs_of(query_bf, key_bf, key_mask, log_total, score_scale):
    scores = (
        jnp.einsum("gqkrd,gskd->gkrqs", query_bf, key_bf, preferred_element_type=jnp.float32)
        * score_scale
    )
    if log_total is None:
        log_total = jnp.log(
            jnp.sum(jnp.where(key_mask, jnp.exp(scores), 0.0), axis=-1, keepdims=True)
        )
    return (jnp.where(key_mask, jnp.exp(scores - log_total), 0.0), log_total)


def bit_count(size):
    return size.bit_length() - 1


def swap(values, axis_name, axis_size, bit):
    return lax.ppermute(values, axis_name, [(i, i ^ (1 << bit)) for i in range(axis_size)])


def after(values, earlier):
    if earlier is None:
        return values
    return lax.optimization_barrier((values, earlier))[0]


def gather_small(values, n_shard):
    rows = [values] + [
        lax.ppermute(values, "shard", [(i, i ^ j) for i in range(n_shard)]) for j in range(1, n_shard)
    ]
    got = jnp.stack(rows)
    me = lax.axis_index("shard")
    for bit in range(bit_count(n_shard)):
        pairs = got.reshape(-1, 2, 1 << bit, got.shape[-1])
        got = jnp.where((me >> bit) & 1 == 1, jnp.flip(pairs, axis=1), pairs).reshape(got.shape)
    return got


def gather_pieces(weight, n_shard, n_rep, earlier):
    rows = weight.shape[0]
    me = lax.axis_index("shard")
    split = n_rep > 1 and rows % 2 == 0
    first = weight
    if split:
        half = rows // 2
        lane = lax.axis_index("rep") & 1
        first = lax.dynamic_slice_in_dim(weight, lane * half, half, axis=0)
    mine = [(0, first)]
    for bit in reversed(range(1, bit_count(n_shard))):
        sent = [(j, after(w, earlier)) for j, w in mine]
        got = [(j ^ (1 << bit), swap(w, "shard", n_shard, bit)) for j, w in sent]
        mine, earlier = mine + got, got[-1][1]
    near = [(0, weight)]
    for j, w in mine[1:]:
        if split:
            other = swap(w, "rep", n_rep, 0)
            whole = jnp.zeros_like(weight)
            whole = lax.dynamic_update_slice_in_dim(whole, w, lane * half, axis=0)
            w = lax.dynamic_update_slice_in_dim(whole, other, (1 - lane) * half, axis=0)
        near.append((j, w))
    pieces = []
    for j, w in near:
        pieces.append(((me ^ j) * rows, w))
        if n_shard > 1:
            pieces.append(((me ^ j ^ 1) * rows, swap(w, "shard", n_shard, 0)))
    return pieces, earlier


def times(left, pieces):
    total = None
    for start, w in pieces:
        part = matmul(lax.dynamic_slice_in_dim(left, start, w.shape[0], axis=1), w)
        total = part if total is None else total + part
    return total


def times_t(left, pieces, depth):
    total = jnp.zeros((left.shape[0], depth), jnp.float32)
    for start, w in pieces:
        part = lax.dot_general(left, w, (((1,), (1,)), ((), ())), preferred_element_type=jnp.float32)
        total = lax.dynamic_update_slice_in_dim(total, part, start, axis=1)
    return total


def sum_kernel(cfg, lt_ref, r_ref, g_ref, out_ref, gout_ref, *scratch):
    n_rep, n_shard, tok = cfg["n_rep"], cfg["n_shard"], cfg["tok"]
    sub, cols, pr, pc = cfg["sub"], cfg["cols"], cfg["pr"], cfg["pc"]
    depth, n_down, n_mid, n_qkv, n_all = (cfg[k] for k in ("depth", "n_down", "n_mid", "n_qkv", "n_all"))
    lsegs, rsegs = cfg["lsegs"], cfg["rsegs"]
    s_bits, r_bits = bit_count(n_shard), bit_count(n_rep)
    n_half = n_shard // 2
    steps = [("shard", i) for i in reversed(range(1, s_bits))] + [("rep", i) for i in range(r_bits)]
    back = [("rep", i) for i in reversed(range(r_bits))]
    n_down_steps, n_back = len(steps), len(back)
    ltf, rf, dsend = scratch[:3]
    recv = scratch[3 : 3 + n_down_steps]
    outb, gacc, grecv = scratch[3 + n_down_steps : 6 + n_down_steps]
    (ex_send, ex_recv, ex_own, send_sem, recv_sem, out_sem, g_send, g_recv, g_out) = scratch[6 + n_down_steps :]
    slots = dsend.shape[0]

    me_s, me_r = lax.axis_index("shard"), lax.axis_index("rep")
    core = me_s & 1

    def bit_of(axis, bit):
        return ((me_s if axis == "shard" else me_r) >> bit) & 1

    def peer(axis, bit):
        return {axis: (me_s if axis == "shard" else me_r) ^ (1 << bit)}

    everyone = [("shard", i) for i in range(s_bits)] + [("rep", i) for i in range(r_bits)]
    barrier = pltpu.get_barrier_semaphore()
    for axis, bit in everyone:
        pl.semaphore_signal(barrier, inc=1, device_id=peer(axis, bit), device_id_type=MESH)
    pl.semaphore_wait(barrier, len(everyone))

    def exchange(i):
        (l0, l1), (r0, r1) = lsegs[i], rsegs[i]
        remote = [
            pltpu.make_async_remote_copy(
                src_ref=lt_ref.at[1 - core, :, pl.ds(l0, l1 - l0)],
                dst_ref=ltf.at[:, pl.ds(l0, l1 - l0), pl.ds(tok, tok)],
                send_sem=ex_send.at[i, 0], recv_sem=ex_recv.at[i, 0],
                device_id=peer("shard", 0), device_id_type=MESH),
            pltpu.make_async_remote_copy(
                src_ref=r_ref.at[:, pl.ds(r0, r1 - r0)],
                dst_ref=rf.at[pl.ds(tok, tok), pl.ds(r0, r1 - r0)],
                send_sem=ex_send.at[i, 1], recv_sem=ex_recv.at[i, 1],
                device_id=peer("shard", 0), device_id_type=MESH),
        ]
        local = [
            pltpu.make_async_copy(
                lt_ref.at[core, :, pl.ds(l0, l1 - l0)],
                ltf.at[:, pl.ds(l0, l1 - l0), pl.ds(0, tok)], ex_own.at[i, 0]),
            pltpu.make_async_copy(
                r_ref.at[:, pl.ds(r0, r1 - r0)], rf.at[pl.ds(0, tok), pl.ds(r0, r1 - r0)], ex_own.at[i, 1]),
        ]
        return remote + local

    for i in range(3):
        for cp in exchange(i):
            cp.start()

    gacc[0] = g_ref[...]

    def gain_copy(i):
        axis, bit = everyone[i]
        return pltpu.make_async_remote_copy(
            src_ref=gacc.at[i], dst_ref=grecv.at[i], send_sem=g_send.at[i], recv_sem=g_recv.at[i],
            device_id=peer(axis, bit), device_id_type=MESH)

    def place(k, j):
        kk = k - n_down
        down = k < n_down
        off = jnp.where(kk < n_mid, lsegs[1][0], jnp.where(kk < n_mid + n_qkv, lsegs[2][0], cfg["lout"]))
        lrow = jnp.where(down, k * sub, off + j * sub)
        rcol = jnp.where(down, j * cols, depth + kk * cols)
        return pl.multiple_of(lrow, sub), pl.multiple_of(rcol, cols)

    def product(blk, k, j):
        lrow, rcol = place(k, j)
        return jnp.dot(
            ltf[blk, pl.ds(lrow, sub), :], rf[:, pl.ds(rcol, cols)], preferred_element_type=jnp.float32)

    rows_p, cols_p = sub // pr, cols // pc

    def pieces(j):
        for a in range(rows_p):
            for b in range(cols_p):
                yield (j * rows_p + a) * cols_p + b, a * pr, b * pc

    nb = n_half // 2
    top = bit_of(*steps[0])

    def rs_copy(i, k):
        axis, bit = steps[i]
        if i == 0:
            src = dsend.at[k % slots]
        else:
            half = recv[i - 1].shape[1] // 2
            src = recv[i - 1].at[k, pl.ds((1 - bit_of(axis, bit)) * half, half)]
        return pltpu.make_async_remote_copy(
            src_ref=src, dst_ref=recv[i].at[k], send_sem=send_sem.at[i, k], recv_sem=recv_sem.at[i, k],
            device_id=peer(axis, bit), device_id_type=MESH)

    def own_start(size):
        at = 0
        for n, (axis, bit) in enumerate(steps[s_bits - 1 :]):
            block = n_rep >> (n + 1)
            if block >= size:
                at = at + bit_of(axis, bit) * block
        return at

    def ag_copy(i, k):
        axis, bit = back[i]
        size = 1 << i
        at = pl.ds(own_start(size), size)
        n = n_down_steps + i
        return pltpu.make_async_remote_copy(
            src_ref=outb.at[k, at], dst_ref=outb.at[k, at], send_sem=send_sem.at[n, k], recv_sem=recv_sem.at[n, k],
            device_id=peer(axis, bit), device_id_type=MESH)

    def out_copy(k):
        return pltpu.make_async_copy(outb.at[k], out_ref.at[k], out_sem.at[k])

    def first(k):
        for i in range(nb):
            for j in range(2):
                part = product((1 - top) * nb + i, k, j).astype(jnp.bfloat16)
                for p, a, b in pieces(j):
                    dsend[k % slots, i * n_rep + p] = part[a : a + pr, b : b + pc]

    def join(i, k):
        rs_copy(i, k).wait()
        if i == 0:
            for n in range(nb):
                for j in range(2):
                    part = product(top * nb + n, k, j)
                    for p, a, b in pieces(j):
                        q = n * n_rep + p
                        got = recv[0][k, q].astype(jnp.float32)
                        recv[0][k, q] = (part[a : a + pr, b : b + pc] + got).astype(jnp.bfloat16)
            return
        half = recv[i].shape[1]
        base = bit_of(*steps[i]) * half
        for q in range(half):
            kept = recv[i - 1][k, base + q].astype(jnp.float32)
            both = (kept + recv[i][k, q].astype(jnp.float32)).astype(jnp.bfloat16)
            if i == n_down_steps - 1:
                outb[k, own_start(1)] = both
            else:
                recv[i][k, q] = both

    lag = [0, 2]
    for _ in range(n_down_steps - 1 + n_back):
        lag.append(lag[-1] + 1)
    last = lag[-1]

    def during(t, n, do):
        k = t - lag[n]

        @pl.when((k >= 0) & (k < n_all))
        def _():
            do(k)

    def body(t, carry):
        for i, when in ((0, 0), (1, n_down), (2, n_down + n_mid)):
            @pl.when(t == when)
            def _(i=i):
                for n, cp in enumerate(exchange(i)):
                    cp.wait()

        during(t, 0, first)
        for i in range(n_down_steps):
            during(t, 1 + i, functools.partial(join, i))
        for i in range(n_back):
            during(t, 1 + n_down_steps + i, lambda k, i=i: ag_copy(i, k).wait())
        for g in range(len(everyone)):
            @pl.when(t == 3 + 2 * g)
            def _(g=g):
                gain_copy(g).wait()
                gacc[g + 1] = gacc[g] + grecv[g]

        for i in range(n_down_steps):
            during(t, i, lambda k, i=i: rs_copy(i, k).start())
        for i in range(n_back):
            during(t, n_down_steps + i, lambda k, i=i: ag_copy(i, k).start())
        during(t, n_down_steps + n_back, lambda k: out_copy(k).start())
        for g in range(len(everyone)):
            @pl.when(t == 1 + 2 * g)
            def _(g=g):
                gain_copy(g).start()

        return carry

    lax.fori_loop(0, n_all + last, body, 0)
    gout = pltpu.make_async_copy(gacc.at[len(everyone)], gout_ref, g_out)
    gout.start()

    def finish(k, carry):
        out_copy(k).wait()
        return carry

    lax.fori_loop(0, n_all, finish, 0)
    gout.wait()


def reduce_grads(hid, h2, h1, ob, dyb, dgate, dup, dqkv, dx2b, gains, n_rep, n_shard):
    tok, ff = hid.shape
    depth = h1.shape[1]
    qkv = dqkv.shape[1]
    n_half = n_shard // 2
    sub = depth // n_shard // 2
    cols = depth // 2
    pr = max(16, 2 * sub // n_rep)
    pc = cols * (2 * sub // pr) // n_rep
    n_down, n_mid, n_qkv, n_out = ff // cols, 2 * ff // cols, qkv // cols, depth // cols
    n_all = n_down + n_mid + n_qkv + n_out
    fs, ds = ff // n_shard, depth // n_shard
    lt = jnp.concatenate([v.T.reshape(n_shard, -1, tok) for v in (hid, h2, h1, ob)], axis=1)
    lt = lt.reshape(n_half, 2, -1, tok).transpose(1, 0, 2, 3)
    right = jnp.concatenate([dyb, dgate, dup, dqkv, dx2b], axis=1)
    lrows, rcols = lt.shape[2], right.shape[1]
    cfg = dict(
        n_rep=n_rep, n_shard=n_shard, tok=tok, sub=sub, cols=cols, pr=pr, pc=pc, depth=depth,
        n_down=n_down, n_mid=n_mid, n_qkv=n_qkv, n_all=n_all, lout=fs + 2 * ds,
        lsegs=((0, fs), (fs, fs + ds), (fs + ds, lrows)),
        rsegs=((0, depth), (depth, depth + 2 * ff), (depth + 2 * ff, rcols)),
    )
    g_rows = gains.shape[0]
    s_bits, r_bits = bit_count(n_shard), bit_count(n_rep)
    n_hops = s_bits + r_bits
    n_steps = s_bits - 1 + r_bits
    slots = 4
    sizes = [n_half * n_rep >> (i + 1) for i in range(n_steps)]
    bf = jnp.bfloat16
    dma = pltpu.SemaphoreType.DMA
    out, gsum = pl.pallas_call(
        functools.partial(sum_kernel, cfg),
        name="sum_grads",
        out_shape=(
            jax.ShapeDtypeStruct((n_all, n_rep, pr, pc), bf),
            jax.ShapeDtypeStruct((g_rows, 128), jnp.float32),
        ),
        in_specs=[pl.BlockSpec(memory_space=pltpu.VMEM)] * 3,
        out_specs=[pl.BlockSpec(memory_space=pl.ANY)] * 2,
        scratch_shapes=[
            pltpu.VMEM((n_half, lrows, 2 * tok), bf),
            pltpu.VMEM((2 * tok, rcols), bf),
            pltpu.VMEM((slots, sizes[0], pr, pc), bf),
            *[pltpu.VMEM((n_all, size, pr, pc), bf) for size in sizes],
            pltpu.VMEM((n_all, n_rep, pr, pc), bf),
            pltpu.VMEM((n_hops + 1, g_rows, 128), jnp.float32),
            pltpu.VMEM((n_hops, g_rows, 128), jnp.float32),
            dma((3, 2)), dma((3, 2)), dma((3, 2)),
            dma((n_steps + r_bits, n_all)), dma((n_steps + r_bits, n_all)), dma((n_all,)),
            dma((n_hops,)), dma((n_hops,)), dma,
        ],
        compiler_params=pltpu.CompilerParams(
            collective_id=0, has_side_effects=True, vmem_limit_bytes=60_000_000),
    )(lt, right, gains)

    rp, cp = sub // pr, cols // pc

    def unpack(lo, n, down):
        v = out[lo : lo + n].reshape(n, 2, rp, cp, pr, pc)
        order = (0, 2, 4, 1, 3, 5) if down else (1, 2, 4, 0, 3, 5)
        rows = n * sub if down else 2 * sub
        return v.transpose(order).reshape(rows, -1).astype(jnp.float32)

    got, lo = [], 0
    for n, down in ((n_down, True), (n_mid // 2, False), (n_mid // 2, False), (n_qkv, False), (n_out, False)):
        got.append(unpack(lo, n, down))
        lo += n
    return got, gsum


def local(
    n_rep,
    n_shard,
    tokens,
    cotangent,
    doc_ids,
    w_query,
    w_key,
    w_value,
    w_out,
    w_gate,
    w_up,
    w_down,
    gain_attn,
    gain_ffn,
    gain_query,
    gain_key,
):
    tok_rows, width = tokens.shape
    ff = w_gate.shape[1]
    q_width, k_width = w_query.shape[1], w_key.shape[1]
    head_share = QH // KVH
    score_scale = 1.0 / math.sqrt(HEAD_DIM)
    gains = (gain_attn, gain_ffn, gain_query, gain_key)
    gain_sizes = [g.shape[0] for g in gains]
    gain_ends = [sum(gain_sizes[: i + 1]) for i in range(len(gains))]
    all_gains = gather_small(jnp.concatenate(gains), n_shard)
    full_gattn, full_gffn, full_gquery, full_gkey = (
        all_gains[:, end - size : end].reshape(-1) for size, end in zip(gain_sizes, gain_ends)
    )
    w_qkv = jnp.concatenate([w_query, w_key, w_value], axis=1)
    qkv_set, last = gather_pieces(w_qkv, n_shard, n_rep, all_gains)
    out_set, last = gather_pieces(w_out, n_shard, n_rep, last)
    gate_set, last = gather_pieces(w_gate, n_shard, n_rep, last)
    up_set, last = gather_pieces(w_up, n_shard, n_rep, last)
    down_set, last = gather_pieces(w_down, n_shard, n_rep, last)

    doc_rows = doc_ids[None, :]
    allowed, positions = doc_tables(doc_rows)
    key_mask = allowed[:, None, None]
    cos_tab, sin_tab = rope_tables(positions, HEAD_DIM)
    resid_in = tokens.astype(jnp.float32)
    normed_in, unit_in, rms_in = norm_rows(resid_in, full_gattn)
    normed_bf = normed_in.astype(jnp.bfloat16)
    qkv = times(normed_bf, qkv_set)
    query_raw = qkv[:, :q_width].reshape(1, tok_rows, QH, HEAD_DIM)
    key_raw = qkv[:, q_width : q_width + k_width].reshape(1, tok_rows, KVH, HEAD_DIM)
    value_bf = qkv[:, q_width + k_width :].astype(jnp.bfloat16).reshape(1, tok_rows, KVH, HEAD_DIM)
    query_normed, query_unit, query_rms = norm_rows(query_raw, full_gquery)
    key_normed, key_unit, key_rms = norm_rows(key_raw, full_gkey)
    query_bf = (
        rotate(query_normed, cos_tab, sin_tab)
        .astype(jnp.bfloat16)
        .reshape(1, tok_rows, KVH, head_share, HEAD_DIM)
    )
    key_bf = rotate(key_normed, cos_tab, sin_tab).astype(jnp.bfloat16)
    attn_probs, log_total = attn_probs_of(query_bf, key_bf, key_mask, None, score_scale)
    probs_bf = attn_probs.astype(jnp.bfloat16)
    mixed_bf = (
        jnp.einsum("gkrqs,gskd->gqkrd", probs_bf, value_bf, preferred_element_type=jnp.float32)
        .astype(jnp.bfloat16)
        .reshape(tok_rows, QH * HEAD_DIM)
    )
    resid_mid = resid_in + times(mixed_bf, out_set)
    normed_mid, unit_mid, rms_mid = norm_rows(resid_mid, full_gffn)
    hidden_in = normed_mid.astype(jnp.bfloat16)
    gate_proj = times(hidden_in, gate_set)
    up_proj = times(hidden_in, up_set)
    gate_sig = jax.nn.sigmoid(gate_proj)
    gate_act = gate_proj * gate_sig
    hidden_bf = (gate_act * up_proj).astype(jnp.bfloat16)

    live_rows = (doc_ids >= 0).astype(jnp.float32)[:, None]
    grad_y = cotangent.astype(jnp.float32) * live_rows
    grad_y_bf = grad_y.astype(jnp.bfloat16)
    block_out = (resid_mid + times(hidden_bf, down_set)).astype(jnp.bfloat16)

    grad_hidden = times_t(grad_y_bf, down_set, ff)
    grad_gate_bf = (grad_hidden * up_proj * gate_sig * (1.0 + gate_proj * (1.0 - gate_sig))).astype(
        jnp.bfloat16
    )
    grad_up_bf = (grad_hidden * gate_act).astype(jnp.bfloat16)
    grad_norm_mid = times_t(grad_gate_bf, gate_set, width) + times_t(grad_up_bf, up_set, width)
    back_mid, part_gffn = norm_back(grad_norm_mid, unit_mid, rms_mid, full_gffn)
    grad_mid = grad_y + back_mid
    grad_mid_bf = grad_mid.astype(jnp.bfloat16)
    grad_mixed_bf = (
        times_t(grad_mid_bf, out_set, q_width)
        .astype(jnp.bfloat16)
        .reshape(1, tok_rows, KVH, head_share, HEAD_DIM)
    )
    grad_scores = jnp.einsum(
        "gqkrd,gskd->gkrqs", grad_mixed_bf, value_bf, preferred_element_type=jnp.float32
    )
    grad_value_bf = (
        jnp.einsum("gkrqs,gqkrd->gskd", probs_bf, grad_mixed_bf, preferred_element_type=jnp.float32)
        .astype(jnp.bfloat16)
        .reshape(tok_rows, KVH * HEAD_DIM)
    )
    row_dot = jnp.sum(attn_probs * grad_scores, axis=-1, keepdims=True)
    grad_logits = (attn_probs * (grad_scores - row_dot) * score_scale).astype(jnp.bfloat16)
    grad_query_rot = jnp.einsum(
        "gkrqs,gskd->gqkrd", grad_logits, key_bf, preferred_element_type=jnp.float32
    ).reshape(1, tok_rows, QH, HEAD_DIM)
    grad_key_rot = jnp.einsum(
        "gkrqs,gqkrd->gskd", grad_logits, query_bf, preferred_element_type=jnp.float32
    )
    grad_query_raw, part_gquery = norm_back(
        rotate_back(grad_query_rot, cos_tab, sin_tab), query_unit, query_rms, full_gquery
    )
    grad_key_raw, part_gkey = norm_back(
        rotate_back(grad_key_rot, cos_tab, sin_tab), key_unit, key_rms, full_gkey
    )
    grad_query_bf = grad_query_raw.astype(jnp.bfloat16).reshape(tok_rows, QH * HEAD_DIM)
    grad_key_bf = grad_key_raw.astype(jnp.bfloat16).reshape(tok_rows, KVH * HEAD_DIM)
    grad_qkv_bf = jnp.concatenate([grad_query_bf, grad_key_bf, grad_value_bf], axis=1)
    grad_norm_in = times_t(grad_qkv_bf, qkv_set, width)
    back_in, part_gattn = norm_back(grad_norm_in, unit_in, rms_in, full_gattn)
    grad_tokens = grad_mid + back_in
    part_gains = jnp.concatenate(
        [
            p.reshape(n_shard, -1)
            for p in (part_gattn, part_gffn, part_gquery, part_gkey)
        ],
        axis=1,
    )
    part_gains = part_gains.astype(jnp.bfloat16).astype(jnp.float32)
    flat = part_gains.reshape(-1)
    flat = jnp.pad(flat, (0, -flat.shape[0] % 1024)).reshape(-1, 128)
    (grad_down, grad_gate, grad_up, grad_qkv, grad_out), sum_gains = reduce_grads(
        hidden_bf, hidden_in, normed_bf, mixed_bf,
        grad_y_bf, grad_gate_bf, grad_up_bf, grad_qkv_bf, grad_mid_bf,
        flat, n_rep, n_shard,
    )
    ends = [q_width, q_width + k_width]
    grad_query, grad_key, grad_value = jnp.split(grad_qkv, ends, axis=1)
    sum_gains = sum_gains.reshape(-1)[: part_gains.size].reshape(part_gains.shape)
    own_gains = lax.dynamic_index_in_dim(sum_gains, lax.axis_index("shard"), axis=0, keepdims=False)
    grad_gattn, grad_gffn, grad_gquery, grad_gkey = (
        own_gains[end - size : end] for size, end in zip(gain_sizes, gain_ends)
    )
    return (
        block_out,
        grad_tokens,
        grad_query,
        grad_key,
        grad_value,
        grad_out,
        grad_gate,
        grad_up,
        grad_down,
        grad_gattn,
        grad_gffn,
        grad_gquery,
        grad_gkey,
    )


def solution(mesh):
    return jax.shard_map(
        functools.partial(local, mesh.shape["rep"], mesh.shape["shard"]),
        mesh=mesh,
        in_specs=(
            P(("rep", "shard"), None),
            P(("rep", "shard"), None),
            P(("rep", "shard")),
            P("shard", None),
            P("shard", None),
            P("shard", None),
            P("shard", None),
            P("shard", None),
            P("shard", None),
            P("shard", None),
            P("shard"),
            P("shard"),
            P("shard"),
            P("shard"),
        ),
        out_specs=(
            P(("rep", "shard"), None),
            P(("rep", "shard"), None),
            P("shard", None),
            P("shard", None),
            P("shard", None),
            P("shard", None),
            P("shard", None),
            P("shard", None),
            P("shard", None),
            P("shard"),
            P("shard"),
            P("shard"),
            P("shard"),
        ),
        check_vma=False,
    )
```

```python
import functools
import math

import jax
import jax.numpy as jnp
from jax import lax
from jax.experimental import pallas as pl
from jax.experimental.pallas import tpu as pltpu
from jax.sharding import PartitionSpec as P

MESH = pl.DeviceIdType.MESH

QH = 16
KVH = 8
HEAD_DIM = 64


NORM_EPSILON = 1e-05
ROPE_BASE = 1000000.0


def matmul(left, right):
    return jnp.dot(left, right, preferred_element_type=jnp.float32)


def matmul_t(left, right):
    return lax.dot_general(left, right, (((1,), (1,)), ((), ())), preferred_element_type=jnp.float32)


def norm_rows(values, gain_vec):
    inv_rms = lax.rsqrt(jnp.mean(values * values, axis=-1, keepdims=True) + NORM_EPSILON)
    normed = values * inv_rms
    return (normed * gain_vec.astype(jnp.float32), normed, inv_rms)


def norm_back(grad_out, normed, inv_rms, gain_vec):
    scaled = grad_out * gain_vec.astype(jnp.float32)
    grad_in = inv_rms * (scaled - normed * jnp.mean(scaled * normed, axis=-1, keepdims=True))
    lead_axes = tuple(range(grad_out.ndim - 1))
    return (grad_in, jnp.sum(grad_out * normed, axis=lead_axes))


def doc_tables(doc_rows):
    block_len = doc_rows.shape[-1]
    row_index = jnp.arange(block_len)[:, None]
    col_index = jnp.arange(block_len)[None, :]
    same_doc = doc_rows[:, :, None] == doc_rows[:, None, :]
    allowed = same_doc & (row_index >= col_index)[None]
    earlier = same_doc & (row_index > col_index)[None]
    positions = jnp.sum(earlier.astype(jnp.int32), axis=2)
    return (allowed, positions)


def rope_tables(positions, head_dim):
    half_dim = head_dim // 2
    inv_freq = jnp.exp(
        jnp.arange(half_dim).astype(jnp.float32) * (-2.0 * math.log(ROPE_BASE) / head_dim)
    )
    angles = positions.astype(jnp.float32)[:, :, None, None] * inv_freq
    return (jnp.cos(angles), jnp.sin(angles))


def rotate(values, cos_tab, sin_tab):
    half_dim = values.shape[-1] // 2
    part_one = values[..., :half_dim]
    part_two = values[..., half_dim:]
    return jnp.concatenate(
        [part_one * cos_tab - part_two * sin_tab, part_two * cos_tab + part_one * sin_tab], axis=-1
    )


def rotate_back(values, cos_tab, sin_tab):
    half_dim = values.shape[-1] // 2
    part_one = values[..., :half_dim]
    part_two = values[..., half_dim:]
    return jnp.concatenate(
        [part_one * cos_tab + part_two * sin_tab, part_two * cos_tab - part_one * sin_tab], axis=-1
    )


def attn_probs_of(query_bf, key_bf, key_mask, log_total, score_scale):
    scores = (
        jnp.einsum("gqkrd,gskd->gkrqs", query_bf, key_bf, preferred_element_type=jnp.float32)
        * score_scale
    )
    if log_total is None:
        log_total = jnp.log(
            jnp.sum(jnp.where(key_mask, jnp.exp(scores), 0.0), axis=-1, keepdims=True)
        )
    return (jnp.where(key_mask, jnp.exp(scores - log_total), 0.0), log_total)


def bit_count(size):
    return size.bit_length() - 1


def gather_kernel(cfg, *refs):
    items, n_in, n_out = cfg["items"], cfg["n_in"], cfg["n_out"]
    ins, outs = refs[:n_in], refs[n_in : n_in + n_out]
    gain_in, gain_out = ins[-1], outs[-1]
    send_sem, recv_sem, own_sem, gs_sem, gr_sem, go_sem = refs[n_in + n_out :]
    me_s, me_r = lax.axis_index("shard"), lax.axis_index("rep")
    core, y, z = me_s & 1, me_r & 1, (me_r >> 1) & 1
    peers = [{"shard": me_s ^ 1}, {"shard": me_s ^ 2}, {"rep": me_r ^ 1}, {"rep": me_r ^ 2}]
    to_core, to_x, to_y, to_z = peers
    barrier = pltpu.get_barrier_semaphore()
    for p in peers:
        pl.semaphore_signal(barrier, inc=1, device_id=p, device_id_type=MESH)
    pl.semaphore_wait(barrier, len(peers))

    other = me_s ^ 2
    mine = z * 2 + y
    from_y, from_z, diag = mine ^ 1, mine ^ 2, mine ^ 3

    def place(n, shard, row, size):
        it = items[n]
        return outs[it["out"]].at[shard, pl.ds(it["row"] + row, size), pl.ds(it["dst"], it["cols"])]

    def fresh(n, row, size):
        it = items[n]
        return ins[it["in"]].at[pl.ds(it["row"] + row, size), pl.ds(it["src"], it["cols"])]

    def send(n, i, src, dst, to):
        return pltpu.make_async_remote_copy(
            src_ref=src, dst_ref=dst, send_sem=send_sem.at[n, i], recv_sem=recv_sem.at[n, i],
            device_id=to, device_id_type=MESH)

    def relay(n, i, row, size, to):
        ref = place(n, other, row, size)
        return send(n, i, ref, ref, to)

    def copies(n):
        it = items[n]
        rows, quarter = it["rows"], it["rows"] // 4
        dx, dy, dz = it["parts"]
        at = lambda q: pl.multiple_of(q * quarter, quarter)
        whole = lambda i, row, size, to: send(n, i, fresh(n, row, size), place(n, me_s, row, size), to)
        return dict(
            x=whole(0, at(mine), quarter, to_x),
            xd=whole(1, at(diag), dx, to_x),
            own=whole(2, 0, rows, to_core),
            y=relay(n, 3, at(mine), quarter, to_y),
            z=relay(n, 4, at(mine), quarter, to_z),
            c0=relay(n, 5, at(mine), quarter, to_core),
            fz=relay(n, 6, at(from_y) + dx + dy, dz, to_z),
            c1=relay(n, 7, at(from_y), quarter, to_core),
            fy=relay(n, 8, at(from_z) + dx, dy, to_y),
            c2=relay(n, 9, at(from_z), quarter, to_core),
            c3=relay(n, 10, at(diag), quarter, to_core),
            keep=pltpu.make_async_copy(fresh(n, 0, rows), place(n, me_s, 0, rows), own_sem.at[n]),
        )

    gain_send = lambda i, shard, src, to: pltpu.make_async_remote_copy(
        src_ref=src, dst_ref=gain_out.at[shard], send_sem=gs_sem.at[i], recv_sem=gr_sem.at[i],
        device_id=to, device_id_type=MESH)
    gains = [
        gain_send(0, me_s, gain_in, to_x),
        gain_send(1, me_s, gain_in, to_core),
        gain_send(2, other, gain_out.at[other], to_core),
    ]
    gain_keep = pltpu.make_async_copy(gain_in, gain_out.at[me_s], go_sem)
    gain_keep.start()
    gains[0].start()
    gains[1].start()
    todo = [copies(n) for n in range(len(items))]
    for c in todo:
        for k in ("x", "xd", "own", "keep"):
            c[k].start()
    gains[0].wait_recv()
    gains[2].start()

    def near(c):
        c["x"].wait_recv()
        for k in ("y", "z", "c0"):
            c[k].start()

    def far(c):
        c["y"].wait_recv()
        c["fz"].start()
        c["c1"].start()
        c["z"].wait_recv()
        c["fy"].start()
        c["c2"].start()

    def end(c):
        for k in ("xd", "fy", "fz"):
            c[k].wait_recv()
        c["c3"].start()

    count = len(todo)
    for t in range(count + 2):
        if t < count:
            near(todo[t])
        if 0 <= t - 1 < count:
            far(todo[t - 1])
        if 0 <= t - 2 < count:
            end(todo[t - 2])
    for c in todo:
        for k in ("own", "c0", "c1", "c2", "c3"):
            c[k].wait_recv()
        for k in ("x", "xd", "own", "y", "z", "c0", "fz", "c1", "fy", "c2", "c3"):
            c[k].wait_send()
        c["keep"].wait()
    gains[1].wait_recv()
    gains[2].wait_recv()
    for g in gains:
        g.wait_send()
    gain_keep.wait()


def gather_all(groups, gains, n_rep, n_shard):
    tile = 16
    fits = n_shard == 4 and n_rep >= 4 and all(w.shape[0] % (4 * tile) == 0 for g in groups for w in g)
    if not fits:
        full = [lax.all_gather(jnp.concatenate(g, axis=1), "shard", axis=0, tiled=True) for g in groups]
        return full, lax.all_gather(gains, "shard", axis=0)
    items, ins = [], []
    for o, group in enumerate(groups):
        dst = 0
        for w in group:
            rows, cols = w.shape
            big = w.size > 2 * 256 * 1024
            row_cut = 3 if big and rows > cols and rows % (12 * tile) == 0 else 1
            col_cut = 3 if big and row_cut == 1 and cols % 384 == 0 else 1
            step, width = rows // row_cut, cols // col_cut
            for a in range(row_cut):
                for b in range(col_cut):
                    units = step // 4 // tile
                    third = units // 3
                    rest = units - 3 * third
                    turn = len(items) % 2
                    parts = [third, third + (rest > turn), third + (rest > 1 - turn)]
                    parts[0] = units - parts[1] - parts[2]
                    items.append({
                        "in": len(ins), "out": o, "row": a * step, "rows": step, "src": b * width,
                        "dst": dst + b * width, "cols": width, "parts": tuple(p * tile for p in parts)})
            ins.append(w)
            dst += cols
    outs = [
        jax.ShapeDtypeStruct((n_shard, g[0].shape[0], sum(w.shape[1] for w in g)), g[0].dtype) for g in groups]
    outs.append(jax.ShapeDtypeStruct((n_shard,) + gains.shape, gains.dtype))
    n = len(items)
    dma = pltpu.SemaphoreType.DMA
    hbm = pl.BlockSpec(memory_space=pltpu.HBM)
    got = pl.pallas_call(
        functools.partial(gather_kernel, {"items": items, "n_in": len(ins) + 1, "n_out": len(outs)}),
        name="gather_weights",
        out_shape=tuple(outs),
        in_specs=[hbm] * (len(ins) + 1),
        out_specs=[hbm] * len(outs),
        scratch_shapes=[dma((n, 11)), dma((n, 11)), dma((n,)), dma((3,)), dma((3,)), dma],
        compiler_params=pltpu.CompilerParams(collective_id=1, has_side_effects=True),
    )(*ins, gains)
    return [g.reshape(-1, g.shape[-1]) for g in got[:-1]], got[-1]


def sum_kernel(cfg, lt_ref, r_ref, g_ref, *refs):
    n_sets = len(cfg["sets"])
    out_refs, gout_ref, scratch = refs[:n_sets], refs[n_sets], refs[n_sets + 1 :]
    n_rep, n_shard, tok = cfg["n_rep"], cfg["n_shard"], cfg["tok"]
    sub, cols, pr, pc = cfg["sub"], cfg["cols"], cfg["pr"], cfg["pc"]
    depth, n_down, n_mid, n_qkv, n_all = (cfg[k] for k in ("depth", "n_down", "n_mid", "n_qkv", "n_all"))
    lsegs, rsegs = cfg["lsegs"], cfg["rsegs"]
    s_bits, r_bits = bit_count(n_shard), bit_count(n_rep)
    n_half = n_shard // 2
    steps = [("shard", i) for i in reversed(range(1, s_bits))] + [("rep", i) for i in range(r_bits)]
    back = [("rep", i) for i in reversed(range(r_bits))]
    n_down_steps, n_back = len(steps), len(back)
    ltf, rf, dsend = scratch[:3]
    recv = scratch[3 : 3 + n_down_steps]
    outb, gacc, grecv = scratch[3 + n_down_steps : 6 + n_down_steps]
    (ex_send, ex_recv, ex_own, send_sem, recv_sem, out_sem, g_send, g_recv, g_out) = scratch[6 + n_down_steps :]
    slots = dsend.shape[0]

    me_s, me_r = lax.axis_index("shard"), lax.axis_index("rep")
    core = me_s & 1

    def bit_of(axis, bit):
        return ((me_s if axis == "shard" else me_r) >> bit) & 1

    def peer(axis, bit):
        return {axis: (me_s if axis == "shard" else me_r) ^ (1 << bit)}

    everyone = [("shard", i) for i in range(s_bits)] + [("rep", i) for i in range(r_bits)]
    barrier = pltpu.get_barrier_semaphore()
    for axis, bit in everyone:
        pl.semaphore_signal(barrier, inc=1, device_id=peer(axis, bit), device_id_type=MESH)
    pl.semaphore_wait(barrier, len(everyone))

    def exchange(i):
        (l0, l1), (r0, r1) = lsegs[i], rsegs[i]
        remote = [
            pltpu.make_async_remote_copy(
                src_ref=lt_ref.at[1 - core, :, pl.ds(l0, l1 - l0)],
                dst_ref=ltf.at[:, pl.ds(l0, l1 - l0), pl.ds(tok, tok)],
                send_sem=ex_send.at[i, 0], recv_sem=ex_recv.at[i, 0],
                device_id=peer("shard", 0), device_id_type=MESH),
            pltpu.make_async_remote_copy(
                src_ref=r_ref.at[:, pl.ds(r0, r1 - r0)],
                dst_ref=rf.at[pl.ds(tok, tok), pl.ds(r0, r1 - r0)],
                send_sem=ex_send.at[i, 1], recv_sem=ex_recv.at[i, 1],
                device_id=peer("shard", 0), device_id_type=MESH),
        ]
        local = [
            pltpu.make_async_copy(
                lt_ref.at[core, :, pl.ds(l0, l1 - l0)],
                ltf.at[:, pl.ds(l0, l1 - l0), pl.ds(0, tok)], ex_own.at[i, 0]),
            pltpu.make_async_copy(
                r_ref.at[:, pl.ds(r0, r1 - r0)], rf.at[pl.ds(0, tok), pl.ds(r0, r1 - r0)], ex_own.at[i, 1]),
        ]
        return remote + local

    for i in range(3):
        for cp in exchange(i):
            cp.start()

    gacc[0] = g_ref[...]

    def gain_copy(i):
        axis, bit = everyone[i]
        return pltpu.make_async_remote_copy(
            src_ref=gacc.at[i], dst_ref=grecv.at[i], send_sem=g_send.at[i], recv_sem=g_recv.at[i],
            device_id=peer(axis, bit), device_id_type=MESH)

    def place(k, j):
        kk = k - n_down
        down = k < n_down
        off = jnp.where(kk < n_mid, lsegs[1][0], jnp.where(kk < n_mid + n_qkv, lsegs[2][0], cfg["lout"]))
        lrow = jnp.where(down, k * sub, off + j * sub)
        rcol = jnp.where(down, j * cols, depth + kk * cols)
        return pl.multiple_of(lrow, sub), pl.multiple_of(rcol, cols)

    def product(blk, k, j):
        lrow, rcol = place(k, j)
        return jnp.dot(
            ltf[blk, pl.ds(lrow, sub), :], rf[:, pl.ds(rcol, cols)], preferred_element_type=jnp.float32)

    rows_p, cols_p = sub // pr, cols // pc

    def pieces(j):
        for a in range(rows_p):
            for b in range(cols_p):
                yield (j * rows_p + a) * cols_p + b, a * pr, b * pc

    nb = n_half // 2
    top = bit_of(*steps[0])

    def rs_copy(i, k):
        axis, bit = steps[i]
        if i == 0:
            src = dsend.at[k % slots]
        else:
            half = recv[i - 1].shape[1] // 2
            src = recv[i - 1].at[k, pl.ds((1 - bit_of(axis, bit)) * half, half)]
        return pltpu.make_async_remote_copy(
            src_ref=src, dst_ref=recv[i].at[k], send_sem=send_sem.at[i, k], recv_sem=recv_sem.at[i, k],
            device_id=peer(axis, bit), device_id_type=MESH)

    def own_start(size):
        at = 0
        for n, (axis, bit) in enumerate(steps[s_bits - 1 :]):
            block = n_rep >> (n + 1)
            if block >= size:
                at = at + bit_of(axis, bit) * block
        return at

    def ag_copy(i, k):
        axis, bit = back[i]
        size = 1 << i
        at = pl.ds(own_start(size), size)
        n = n_down_steps + i
        return pltpu.make_async_remote_copy(
            src_ref=outb.at[k, at], dst_ref=outb.at[k, at], send_sem=send_sem.at[n, k], recv_sem=recv_sem.at[n, k],
            device_id=peer(axis, bit), device_id_type=MESH)

    def out_copies(n, k):
        lo = cfg["sets"][n][0]
        made = []
        for j in range(2):
            for b in range(cols_p):
                if n == 0:
                    dst = out_refs[n].at[k, :, :, pl.ds(j * cols + b * pc, pc)]
                else:
                    at = pl.multiple_of((k - lo) * cols, cols) + b * pc
                    dst = out_refs[n].at[pl.ds(j * rows_p, rows_p), :, pl.ds(at, pc)]
                if cols_p == 1:
                    made.append((outb.at[k, pl.ds(j * rows_p, rows_p)], dst))
                else:
                    made += [
                        (outb.at[k, (j * rows_p + a) * cols_p + b], dst.at[a]) for a in range(rows_p)]
        return [pltpu.make_async_copy(src, dst, out_sem.at[k, i]) for i, (src, dst) in enumerate(made)]

    def each_set(k, act):
        for n, (lo, hi) in enumerate(cfg["sets"]):
            @pl.when((k >= lo) & (k < hi))
            def _(n=n):
                for cp in out_copies(n, k):
                    act(cp)

    def first(k):
        for i in range(nb):
            for j in range(2):
                part = product((1 - top) * nb + i, k, j).astype(jnp.bfloat16)
                for p, a, b in pieces(j):
                    dsend[k % slots, i * n_rep + p] = part[a : a + pr, b : b + pc]

    def join(i, k):
        rs_copy(i, k).wait()
        if i == 0:
            for n in range(nb):
                for j in range(2):
                    part = product(top * nb + n, k, j)
                    for p, a, b in pieces(j):
                        q = n * n_rep + p
                        got = recv[0][k, q].astype(jnp.float32)
                        recv[0][k, q] = (part[a : a + pr, b : b + pc] + got).astype(jnp.bfloat16)
            return
        half = recv[i].shape[1]
        base = bit_of(*steps[i]) * half
        for q in range(half):
            kept = recv[i - 1][k, base + q].astype(jnp.float32)
            both = (kept + recv[i][k, q].astype(jnp.float32)).astype(jnp.bfloat16)
            if i == n_down_steps - 1:
                outb[k, own_start(1)] = both
            else:
                recv[i][k, q] = both

    lag = [0, 2]
    for _ in range(n_down_steps - 1 + n_back):
        lag.append(lag[-1] + 2)
    last = lag[-1]

    def during(t, n, do):
        k = t - lag[n]

        @pl.when((k >= 0) & (k < n_all))
        def _():
            do(k)

    def body(t, carry):
        for i, when in ((0, 0), (1, n_down), (2, n_down + n_mid)):
            @pl.when(t == when)
            def _(i=i):
                for n, cp in enumerate(exchange(i)):
                    cp.wait()

        during(t, 0, first)
        for i in range(n_down_steps):
            during(t, 1 + i, functools.partial(join, i))
        for i in range(n_back):
            during(t, 1 + n_down_steps + i, lambda k, i=i: ag_copy(i, k).wait())
        for g in range(len(everyone)):
            @pl.when(t == 3 + 2 * g)
            def _(g=g):
                gain_copy(g).wait()
                gacc[g + 1] = gacc[g] + grecv[g]

        for i in range(n_down_steps):
            during(t, i, lambda k, i=i: rs_copy(i, k).start())
        for i in range(n_back):
            during(t, n_down_steps + i, lambda k, i=i: ag_copy(i, k).start())
        during(t, n_down_steps + n_back, lambda k: each_set(k, lambda cp: cp.start()))
        for g in range(len(everyone)):
            @pl.when(t == 1 + 2 * g)
            def _(g=g):
                gain_copy(g).start()

        return carry

    lax.fori_loop(0, n_all + last, body, 0)
    gout = pltpu.make_async_copy(gacc.at[len(everyone)], gout_ref, g_out)
    gout.start()

    def finish(k, carry):
        each_set(k, lambda cp: cp.wait())
        return carry

    lax.fori_loop(0, n_all, finish, 0)
    gout.wait()


def reduce_grads(hid, h2, h1, ob, dyb, dgate, dup, dqkv, dx2b, gains, n_rep, n_shard):
    tok, ff = hid.shape
    depth = h1.shape[1]
    qkv = dqkv.shape[1]
    n_half = n_shard // 2
    sub = depth // n_shard // 2
    cols = depth // 2
    pr = max(16, 2 * sub // n_rep)
    pc = cols * (2 * sub // pr) // n_rep
    n_down, n_mid, n_qkv, n_out = ff // cols, 2 * ff // cols, qkv // cols, depth // cols
    n_all = n_down + n_mid + n_qkv + n_out
    fs, ds = ff // n_shard, depth // n_shard
    lt = jnp.concatenate([v.T.reshape(n_shard, -1, tok) for v in (hid, h2, h1, ob)], axis=1)
    lt = lt.reshape(n_half, 2, -1, tok).transpose(1, 0, 2, 3)
    right = jnp.concatenate([dyb, dgate, dup, dqkv, dx2b], axis=1)
    lrows, rcols = lt.shape[2], right.shape[1]
    cfg = dict(
        n_rep=n_rep, n_shard=n_shard, tok=tok, sub=sub, cols=cols, pr=pr, pc=pc, depth=depth,
        n_down=n_down, n_mid=n_mid, n_qkv=n_qkv, n_all=n_all, lout=fs + 2 * ds,
        lsegs=((0, fs), (fs, fs + ds), (fs + ds, lrows)),
        rsegs=((0, depth), (depth, depth + 2 * ff), (depth + 2 * ff, rcols)),
    )
    g_rows = gains.shape[0]
    ends = [n_down, n_down + n_mid // 2, n_down + n_mid, n_down + n_mid + n_qkv, n_all]
    cfg["sets"] = tuple(zip([0] + ends[:-1], ends))
    rp, cp = sub // pr, cols // pc
    shapes = [(n_down, rp, pr, depth)] + [(2 * rp, pr, n) for n in (ff, ff, qkv, depth)]
    s_bits, r_bits = bit_count(n_shard), bit_count(n_rep)
    n_hops = s_bits + r_bits
    n_steps = s_bits - 1 + r_bits
    slots = 4
    sizes = [n_half * n_rep >> (i + 1) for i in range(n_steps)]
    bf = jnp.bfloat16
    dma = pltpu.SemaphoreType.DMA
    *outs, gsum = pl.pallas_call(
        functools.partial(sum_kernel, cfg),
        name="sum_grads",
        out_shape=(
            *[jax.ShapeDtypeStruct(shape, bf) for shape in shapes],
            jax.ShapeDtypeStruct((g_rows, 128), jnp.float32),
        ),
        in_specs=[pl.BlockSpec(memory_space=pltpu.VMEM)] * 3,
        out_specs=[pl.BlockSpec(memory_space=pltpu.HBM)] * (len(shapes) + 1),
        scratch_shapes=[
            pltpu.VMEM((n_half, lrows, 2 * tok), bf),
            pltpu.VMEM((2 * tok, rcols), bf),
            pltpu.VMEM((slots, sizes[0], pr, pc), bf),
            *[pltpu.VMEM((n_all, size, pr, pc), bf) for size in sizes],
            pltpu.VMEM((n_all, n_rep, pr, pc), bf),
            pltpu.VMEM((n_hops + 1, g_rows, 128), jnp.float32),
            pltpu.VMEM((n_hops, g_rows, 128), jnp.float32),
            dma((3, 2)), dma((3, 2)), dma((3, 2)),
            dma((n_steps + r_bits, n_all)), dma((n_steps + r_bits, n_all)), dma((n_all, 2 if cp == 1 else n_rep)),
            dma((n_hops,)), dma((n_hops,)), dma,
        ],
        compiler_params=pltpu.CompilerParams(
            collective_id=0, has_side_effects=True, vmem_limit_bytes=60_000_000),
    )(lt, right, gains)

    return [v.reshape(-1, v.shape[-1]).astype(jnp.float32) for v in outs], gsum


def local(
    n_rep,
    n_shard,
    tokens,
    cotangent,
    doc_ids,
    w_query,
    w_key,
    w_value,
    w_out,
    w_gate,
    w_up,
    w_down,
    gain_attn,
    gain_ffn,
    gain_query,
    gain_key,
):
    tok_rows, width = tokens.shape
    ff = w_gate.shape[1]
    q_width, k_width = w_query.shape[1], w_key.shape[1]
    head_share = QH // KVH
    score_scale = 1.0 / math.sqrt(HEAD_DIM)
    gains = (gain_attn, gain_ffn, gain_query, gain_key)
    gain_sizes = [g.shape[0] for g in gains]
    gain_ends = [sum(gain_sizes[: i + 1]) for i in range(len(gains))]
    flat_gains = jnp.concatenate(gains)
    n_gain = flat_gains.shape[0]
    flat_gains = jnp.pad(flat_gains, (0, -n_gain % 2048)).reshape(-1, 128)
    (qkv_set, out_set, gate_set, up_set, down_set), all_gains = gather_all(
        [[w_query, w_key, w_value], [w_out], [w_gate], [w_up], [w_down]], flat_gains, n_rep, n_shard
    )
    all_gains = all_gains.reshape(n_shard, -1)
    full_gattn, full_gffn, full_gquery, full_gkey = (
        all_gains[:, end - size : end].reshape(-1) for size, end in zip(gain_sizes, gain_ends)
    )

    doc_rows = doc_ids[None, :]
    allowed, positions = doc_tables(doc_rows)
    key_mask = allowed[:, None, None]
    cos_tab, sin_tab = rope_tables(positions, HEAD_DIM)
    resid_in = tokens.astype(jnp.float32)
    normed_in, unit_in, rms_in = norm_rows(resid_in, full_gattn)
    normed_bf = normed_in.astype(jnp.bfloat16)
    qkv = matmul(normed_bf, qkv_set)
    query_raw = qkv[:, :q_width].reshape(1, tok_rows, QH, HEAD_DIM)
    key_raw = qkv[:, q_width : q_width + k_width].reshape(1, tok_rows, KVH, HEAD_DIM)
    value_bf = qkv[:, q_width + k_width :].astype(jnp.bfloat16).reshape(1, tok_rows, KVH, HEAD_DIM)
    query_normed, query_unit, query_rms = norm_rows(query_raw, full_gquery)
    key_normed, key_unit, key_rms = norm_rows(key_raw, full_gkey)
    query_bf = (
        rotate(query_normed, cos_tab, sin_tab)
        .astype(jnp.bfloat16)
        .reshape(1, tok_rows, KVH, head_share, HEAD_DIM)
    )
    key_bf = rotate(key_normed, cos_tab, sin_tab).astype(jnp.bfloat16)
    attn_probs, log_total = attn_probs_of(query_bf, key_bf, key_mask, None, score_scale)
    probs_bf = attn_probs.astype(jnp.bfloat16)
    mixed_bf = (
        jnp.einsum("gkrqs,gskd->gqkrd", probs_bf, value_bf, preferred_element_type=jnp.float32)
        .astype(jnp.bfloat16)
        .reshape(tok_rows, QH * HEAD_DIM)
    )
    resid_mid = resid_in + matmul(mixed_bf, out_set)
    normed_mid, unit_mid, rms_mid = norm_rows(resid_mid, full_gffn)
    hidden_in = normed_mid.astype(jnp.bfloat16)
    gate_proj = matmul(hidden_in, gate_set)
    up_proj = matmul(hidden_in, up_set)
    gate_sig = jax.nn.sigmoid(gate_proj)
    gate_act = gate_proj * gate_sig
    hidden_bf = (gate_act * up_proj).astype(jnp.bfloat16)

    live_rows = (doc_ids >= 0).astype(jnp.float32)[:, None]
    grad_y = cotangent.astype(jnp.float32) * live_rows
    grad_y_bf = grad_y.astype(jnp.bfloat16)
    block_out = (resid_mid + matmul(hidden_bf, down_set)).astype(jnp.bfloat16)

    grad_hidden = matmul_t(grad_y_bf, down_set)
    grad_gate_bf = (grad_hidden * up_proj * gate_sig * (1.0 + gate_proj * (1.0 - gate_sig))).astype(
        jnp.bfloat16
    )
    grad_up_bf = (grad_hidden * gate_act).astype(jnp.bfloat16)
    grad_norm_mid = matmul_t(grad_gate_bf, gate_set) + matmul_t(grad_up_bf, up_set)
    back_mid, part_gffn = norm_back(grad_norm_mid, unit_mid, rms_mid, full_gffn)
    grad_mid = grad_y + back_mid
    grad_mid_bf = grad_mid.astype(jnp.bfloat16)
    grad_mixed_bf = (
        matmul_t(grad_mid_bf, out_set)
        .astype(jnp.bfloat16)
        .reshape(1, tok_rows, KVH, head_share, HEAD_DIM)
    )
    grad_scores = jnp.einsum(
        "gqkrd,gskd->gkrqs", grad_mixed_bf, value_bf, preferred_element_type=jnp.float32
    )
    grad_value_bf = (
        jnp.einsum("gkrqs,gqkrd->gskd", probs_bf, grad_mixed_bf, preferred_element_type=jnp.float32)
        .astype(jnp.bfloat16)
        .reshape(tok_rows, KVH * HEAD_DIM)
    )
    row_dot = jnp.sum(attn_probs * grad_scores, axis=-1, keepdims=True)
    grad_logits = (attn_probs * (grad_scores - row_dot) * score_scale).astype(jnp.bfloat16)
    grad_query_rot = jnp.einsum(
        "gkrqs,gskd->gqkrd", grad_logits, key_bf, preferred_element_type=jnp.float32
    ).reshape(1, tok_rows, QH, HEAD_DIM)
    grad_key_rot = jnp.einsum(
        "gkrqs,gqkrd->gskd", grad_logits, query_bf, preferred_element_type=jnp.float32
    )
    grad_query_raw, part_gquery = norm_back(
        rotate_back(grad_query_rot, cos_tab, sin_tab), query_unit, query_rms, full_gquery
    )
    grad_key_raw, part_gkey = norm_back(
        rotate_back(grad_key_rot, cos_tab, sin_tab), key_unit, key_rms, full_gkey
    )
    grad_query_bf = grad_query_raw.astype(jnp.bfloat16).reshape(tok_rows, QH * HEAD_DIM)
    grad_key_bf = grad_key_raw.astype(jnp.bfloat16).reshape(tok_rows, KVH * HEAD_DIM)
    grad_qkv_bf = jnp.concatenate([grad_query_bf, grad_key_bf, grad_value_bf], axis=1)
    grad_norm_in = matmul_t(grad_qkv_bf, qkv_set)
    back_in, part_gattn = norm_back(grad_norm_in, unit_in, rms_in, full_gattn)
    grad_tokens = grad_mid + back_in
    part_gains = jnp.concatenate(
        [
            p.reshape(n_shard, -1)
            for p in (part_gattn, part_gffn, part_gquery, part_gkey)
        ],
        axis=1,
    )
    part_gains = part_gains.astype(jnp.bfloat16).astype(jnp.float32)
    flat = part_gains.reshape(-1)
    flat = jnp.pad(flat, (0, -flat.shape[0] % 1024)).reshape(-1, 128)
    (grad_down, grad_gate, grad_up, grad_qkv, grad_out), sum_gains = reduce_grads(
        hidden_bf, hidden_in, normed_bf, mixed_bf,
        grad_y_bf, grad_gate_bf, grad_up_bf, grad_qkv_bf, grad_mid_bf,
        flat, n_rep, n_shard,
    )
    ends = [q_width, q_width + k_width]
    grad_query, grad_key, grad_value = jnp.split(grad_qkv, ends, axis=1)
    sum_gains = sum_gains.reshape(-1)[: part_gains.size].reshape(part_gains.shape)
    own_gains = lax.dynamic_index_in_dim(sum_gains, lax.axis_index("shard"), axis=0, keepdims=False)
    grad_gattn, grad_gffn, grad_gquery, grad_gkey = (
        own_gains[end - size : end] for size, end in zip(gain_sizes, gain_ends)
    )
    return (
        block_out,
        grad_tokens,
        grad_query,
        grad_key,
        grad_value,
        grad_out,
        grad_gate,
        grad_up,
        grad_down,
        grad_gattn,
        grad_gffn,
        grad_gquery,
        grad_gkey,
    )


def solution(mesh):
    return jax.shard_map(
        functools.partial(local, mesh.shape["rep"], mesh.shape["shard"]),
        mesh=mesh,
        in_specs=(
            P(("rep", "shard"), None),
            P(("rep", "shard"), None),
            P(("rep", "shard")),
            P("shard", None),
            P("shard", None),
            P("shard", None),
            P("shard", None),
            P("shard", None),
            P("shard", None),
            P("shard", None),
            P("shard"),
            P("shard"),
            P("shard"),
            P("shard"),
        ),
        out_specs=(
            P(("rep", "shard"), None),
            P(("rep", "shard"), None),
            P("shard", None),
            P("shard", None),
            P("shard", None),
            P("shard", None),
            P("shard", None),
            P("shard", None),
            P("shard", None),
            P("shard"),
            P("shard"),
            P("shard"),
            P("shard"),
        ),
        check_vma=False,
    )
```

```python
import functools
import math

import jax
import jax.numpy as jnp
from jax import lax
from jax.experimental import pallas as pl
from jax.experimental.pallas import tpu as pltpu
from jax.sharding import PartitionSpec as P

MESH = pl.DeviceIdType.MESH

QH = 16
KVH = 8
HEAD_DIM = 64


NORM_EPSILON = 1e-05
ROPE_BASE = 1000000.0


def matmul(left, right):
    return jnp.dot(left, right, preferred_element_type=jnp.float32)


def matmul_t(left, right):
    return lax.dot_general(left, right, (((1,), (1,)), ((), ())), preferred_element_type=jnp.float32)


def norm_rows(values, gain_vec):
    inv_rms = lax.rsqrt(jnp.mean(values * values, axis=-1, keepdims=True) + NORM_EPSILON)
    normed = values * inv_rms
    return (normed * gain_vec.astype(jnp.float32), normed, inv_rms)


def norm_back(grad_out, normed, inv_rms, gain_vec):
    scaled = grad_out * gain_vec.astype(jnp.float32)
    grad_in = inv_rms * (scaled - normed * jnp.mean(scaled * normed, axis=-1, keepdims=True))
    lead_axes = tuple(range(grad_out.ndim - 1))
    return (grad_in, jnp.sum(grad_out * normed, axis=lead_axes))


def doc_tables(doc_rows):
    block_len = doc_rows.shape[-1]
    row_index = jnp.arange(block_len)[:, None]
    col_index = jnp.arange(block_len)[None, :]
    same_doc = doc_rows[:, :, None] == doc_rows[:, None, :]
    allowed = same_doc & (row_index >= col_index)[None]
    earlier = same_doc & (row_index > col_index)[None]
    positions = jnp.sum(earlier.astype(jnp.int32), axis=2)
    return (allowed, positions)


def rope_tables(positions, head_dim):
    half_dim = head_dim // 2
    inv_freq = jnp.exp(
        jnp.arange(half_dim).astype(jnp.float32) * (-2.0 * math.log(ROPE_BASE) / head_dim)
    )
    angles = positions.astype(jnp.float32)[:, :, None, None] * inv_freq
    return (jnp.cos(angles), jnp.sin(angles))


def rotate(values, cos_tab, sin_tab):
    half_dim = values.shape[-1] // 2
    part_one = values[..., :half_dim]
    part_two = values[..., half_dim:]
    return jnp.concatenate(
        [part_one * cos_tab - part_two * sin_tab, part_two * cos_tab + part_one * sin_tab], axis=-1
    )


def rotate_back(values, cos_tab, sin_tab):
    half_dim = values.shape[-1] // 2
    part_one = values[..., :half_dim]
    part_two = values[..., half_dim:]
    return jnp.concatenate(
        [part_one * cos_tab + part_two * sin_tab, part_two * cos_tab - part_one * sin_tab], axis=-1
    )


def attn_probs_of(query_bf, key_bf, key_mask, log_total, score_scale):
    scores = (
        jnp.einsum("gqkrd,gskd->gkrqs", query_bf, key_bf, preferred_element_type=jnp.float32)
        * score_scale
    )
    if log_total is None:
        log_total = jnp.log(
            jnp.sum(jnp.where(key_mask, jnp.exp(scores), 0.0), axis=-1, keepdims=True)
        )
    return (jnp.where(key_mask, jnp.exp(scores - log_total), 0.0), log_total)


def bit_count(size):
    return size.bit_length() - 1


def gather_kernel(cfg, *refs):
    items, n_in, n_out = cfg["items"], cfg["n_in"], cfg["n_out"]
    ins, outs = refs[:n_in], refs[n_in : n_in + n_out]
    gain_in, gain_out = ins[-1], outs[-1]
    held = refs[n_in + n_out : n_in + 2 * n_out - 1]
    send_sem, recv_sem, own_sem, out_sem, gs_sem, gr_sem, go_sem = refs[n_in + 2 * n_out - 1 :]
    me_s, me_r = lax.axis_index("shard"), lax.axis_index("rep")
    core, y, z = me_s & 1, me_r & 1, (me_r >> 1) & 1
    peers = [{"shard": me_s ^ 1}, {"shard": me_s ^ 2}, {"rep": me_r ^ 1}, {"rep": me_r ^ 2}]
    to_core, to_x, to_y, to_z = peers
    barrier = pltpu.get_barrier_semaphore()
    for p in peers:
        pl.semaphore_signal(barrier, inc=1, device_id=p, device_id_type=MESH)
    pl.semaphore_wait(barrier, len(peers))

    other = me_s ^ 2
    mine = z * 2 + y
    from_y, from_z, diag = mine ^ 1, mine ^ 2, mine ^ 3

    def place(n, shard, row, size):
        it = items[n]
        return held[it["out"]].at[shard, pl.ds(it["row"] + row, size), pl.ds(it["dst"], it["cols"])]

    def result(n, shard, row, size):
        it = items[n]
        return outs[it["out"]].at[shard, pl.ds(it["row"] + row, size), pl.ds(it["dst"], it["cols"])]

    def fresh(n, row, size):
        it = items[n]
        return ins[it["in"]].at[pl.ds(it["row"] + row, size), pl.ds(it["src"], it["cols"])]

    def send(n, i, src, dst, to):
        return pltpu.make_async_remote_copy(
            src_ref=src, dst_ref=dst, send_sem=send_sem.at[n, i], recv_sem=recv_sem.at[n, i],
            device_id=to, device_id_type=MESH)

    def relay(n, i, row, size, to):
        ref = place(n, other, row, size)
        return send(n, i, ref, ref, to)

    def copies(n):
        it = items[n]
        rows, quarter = it["rows"], it["rows"] // 4
        dx, dy, dz = it["parts"]
        at = lambda q: pl.multiple_of(q * quarter, quarter)
        whole = lambda i, row, size, to: send(
            n, i, place(n, me_s, row, size), place(n, me_s, row, size), to)
        return dict(
            x=whole(0, at(mine), quarter, to_x),
            xd=whole(1, at(diag), dx, to_x),
            own=whole(2, 0, rows, to_core),
            y=relay(n, 3, at(mine), quarter, to_y),
            z=relay(n, 4, at(mine), quarter, to_z),
            c0=relay(n, 5, at(mine), quarter, to_core),
            fz=relay(n, 6, at(from_y) + dx + dy, dz, to_z),
            c1=relay(n, 7, at(from_y), quarter, to_core),
            fy=relay(n, 8, at(from_z) + dx, dy, to_y),
            c2=relay(n, 9, at(from_z), quarter, to_core),
            c3=relay(n, 10, at(diag), quarter, to_core),
            out=[
                pltpu.make_async_copy(
                    place(n, me_s ^ d, 0, rows), result(n, me_s ^ d, 0, rows), out_sem.at[n, d])
                for d in range(4)],
            keep=pltpu.make_async_copy(fresh(n, 0, rows), place(n, me_s, 0, rows), own_sem.at[n]),
        )

    gain_send = lambda i, shard, src, to: pltpu.make_async_remote_copy(
        src_ref=src, dst_ref=gain_out.at[shard], send_sem=gs_sem.at[i], recv_sem=gr_sem.at[i],
        device_id=to, device_id_type=MESH)
    gains = [
        gain_send(0, me_s, gain_in, to_x),
        gain_send(1, me_s, gain_in, to_core),
        gain_send(2, other, gain_out.at[other], to_core),
    ]
    gain_keep = pltpu.make_async_copy(gain_in, gain_out.at[me_s], go_sem)
    gain_keep.start()
    gains[0].start()
    gains[1].start()
    todo = [copies(n) for n in range(len(items))]
    for c in todo:
        c["keep"].start()
    for c in todo:
        c["keep"].wait()
        for k in ("x", "xd", "own"):
            c[k].start()
        c["out"][0].start()
    gains[0].wait_recv()
    gains[2].start()

    def near(c):
        c["x"].wait_recv()
        for k in ("y", "z", "c0"):
            c[k].start()

    def far(c):
        c["y"].wait_recv()
        c["fz"].start()
        c["c1"].start()
        c["z"].wait_recv()
        c["fy"].start()
        c["c2"].start()

    def end(c):
        for k in ("xd", "fy", "fz"):
            c[k].wait_recv()
        c["c3"].start()
        c["out"][2].start()
        c["own"].wait_recv()
        c["out"][1].start()

    def pair(c):
        for k in ("c0", "c1", "c2", "c3"):
            c[k].wait_recv()
        c["out"][3].start()

    count = len(todo)
    for t in range(count + 3):
        if t < count:
            near(todo[t])
        if 0 <= t - 1 < count:
            far(todo[t - 1])
        if 0 <= t - 2 < count:
            end(todo[t - 2])
        if 0 <= t - 3 < count:
            pair(todo[t - 3])
    for c in todo:
        for k in ("x", "xd", "own", "y", "z", "c0", "fz", "c1", "fy", "c2", "c3"):
            c[k].wait_send()
        for cp in c["out"]:
            cp.wait()
    gains[1].wait_recv()
    gains[2].wait_recv()
    for g in gains:
        g.wait_send()
    gain_keep.wait()


def gather_all(groups, gains, n_rep, n_shard):
    tile = 16
    fits = n_shard == 4 and n_rep >= 4 and all(w.shape[0] % (4 * tile) == 0 for g in groups for w in g)
    if not fits:
        full = [lax.all_gather(jnp.concatenate(g, axis=1), "shard", axis=0, tiled=True) for g in groups]
        return full, lax.all_gather(gains, "shard", axis=0)
    items, ins = [], []
    for o, group in enumerate(groups):
        dst = 0
        for w in group:
            rows, cols = w.shape
            big = w.size > 2 * 256 * 1024
            row_cut = 3 if big and rows > cols and rows % (12 * tile) == 0 else 1
            col_cut = 3 if big and row_cut == 1 and cols % 384 == 0 else 1
            step, width = rows // row_cut, cols // col_cut
            for a in range(row_cut):
                for b in range(col_cut):
                    units = step // 4 // tile
                    third = units // 3
                    rest = units - 3 * third
                    turn = len(items) % 2
                    parts = [third, third + (rest > turn), third + (rest > 1 - turn)]
                    parts[0] = units - parts[1] - parts[2]
                    items.append({
                        "in": len(ins), "out": o, "row": a * step, "rows": step, "src": b * width,
                        "dst": dst + b * width, "cols": width, "parts": tuple(p * tile for p in parts)})
            ins.append(w)
            dst += cols
    outs = [
        jax.ShapeDtypeStruct((n_shard, g[0].shape[0], sum(w.shape[1] for w in g)), g[0].dtype) for g in groups]
    outs.append(jax.ShapeDtypeStruct((n_shard,) + gains.shape, gains.dtype))
    n = len(items)
    dma = pltpu.SemaphoreType.DMA
    hbm = pl.BlockSpec(memory_space=pltpu.HBM)
    got = pl.pallas_call(
        functools.partial(gather_kernel, {"items": items, "n_in": len(ins) + 1, "n_out": len(outs)}),
        name="gather_weights",
        out_shape=tuple(outs),
        in_specs=[hbm] * (len(ins) + 1),
        out_specs=[hbm] * len(outs),
        scratch_shapes=[
            *[pltpu.VMEM(o.shape, o.dtype) for o in outs[:-1]],
            dma((n, 11)), dma((n, 11)), dma((n,)), dma((n, 4)), dma((3,)), dma((3,)), dma,
        ],
        compiler_params=pltpu.CompilerParams(
            collective_id=1, has_side_effects=True, vmem_limit_bytes=44_000_000),
    )(*ins, gains)
    return [g.reshape(-1, g.shape[-1]) for g in got[:-1]], got[-1]


def sum_kernel(cfg, lt_ref, r_ref, g_ref, *refs):
    n_sets = len(cfg["sets"])
    out_refs, gout_ref, scratch = refs[:n_sets], refs[n_sets], refs[n_sets + 1 :]
    n_rep, n_shard, tok = cfg["n_rep"], cfg["n_shard"], cfg["tok"]
    sub, cols, pr, pc = cfg["sub"], cfg["cols"], cfg["pr"], cfg["pc"]
    depth, n_down, n_mid, n_qkv, n_all = (cfg[k] for k in ("depth", "n_down", "n_mid", "n_qkv", "n_all"))
    lsegs, rsegs = cfg["lsegs"], cfg["rsegs"]
    s_bits, r_bits = bit_count(n_shard), bit_count(n_rep)
    n_half = n_shard // 2
    steps = [("shard", i) for i in reversed(range(1, s_bits))] + [("rep", i) for i in range(r_bits)]
    back = [("rep", i) for i in reversed(range(r_bits))]
    n_down_steps, n_back = len(steps), len(back)
    ltf, rf, dsend = scratch[:3]
    recv = scratch[3 : 3 + n_down_steps]
    outb, gacc, grecv = scratch[3 + n_down_steps : 6 + n_down_steps]
    (ex_send, ex_recv, ex_own, send_sem, recv_sem, out_sem, g_send, g_recv, g_out) = scratch[6 + n_down_steps :]
    slots = dsend.shape[0]

    me_s, me_r = lax.axis_index("shard"), lax.axis_index("rep")
    core = me_s & 1

    def bit_of(axis, bit):
        return ((me_s if axis == "shard" else me_r) >> bit) & 1

    def peer(axis, bit):
        return {axis: (me_s if axis == "shard" else me_r) ^ (1 << bit)}

    everyone = [("shard", i) for i in range(s_bits)] + [("rep", i) for i in range(r_bits)]
    barrier = pltpu.get_barrier_semaphore()
    for axis, bit in everyone:
        pl.semaphore_signal(barrier, inc=1, device_id=peer(axis, bit), device_id_type=MESH)
    pl.semaphore_wait(barrier, len(everyone))

    def exchange(i):
        (l0, l1), (r0, r1) = lsegs[i], rsegs[i]
        remote = [
            pltpu.make_async_remote_copy(
                src_ref=lt_ref.at[1 - core, :, pl.ds(l0, l1 - l0)],
                dst_ref=ltf.at[:, pl.ds(l0, l1 - l0), pl.ds(tok, tok)],
                send_sem=ex_send.at[i, 0], recv_sem=ex_recv.at[i, 0],
                device_id=peer("shard", 0), device_id_type=MESH),
            pltpu.make_async_remote_copy(
                src_ref=r_ref.at[:, pl.ds(r0, r1 - r0)],
                dst_ref=rf.at[pl.ds(tok, tok), pl.ds(r0, r1 - r0)],
                send_sem=ex_send.at[i, 1], recv_sem=ex_recv.at[i, 1],
                device_id=peer("shard", 0), device_id_type=MESH),
        ]
        local = [
            pltpu.make_async_copy(
                lt_ref.at[core, :, pl.ds(l0, l1 - l0)],
                ltf.at[:, pl.ds(l0, l1 - l0), pl.ds(0, tok)], ex_own.at[i, 0]),
            pltpu.make_async_copy(
                r_ref.at[:, pl.ds(r0, r1 - r0)], rf.at[pl.ds(0, tok), pl.ds(r0, r1 - r0)], ex_own.at[i, 1]),
        ]
        return remote + local

    for i in range(3):
        for cp in exchange(i):
            cp.start()

    gacc[0] = g_ref[...]

    def gain_copy(i):
        axis, bit = everyone[i]
        return pltpu.make_async_remote_copy(
            src_ref=gacc.at[i], dst_ref=grecv.at[i], send_sem=g_send.at[i], recv_sem=g_recv.at[i],
            device_id=peer(axis, bit), device_id_type=MESH)

    def place(k, j):
        kk = k - n_down
        down = k < n_down
        off = jnp.where(kk < n_mid, lsegs[1][0], jnp.where(kk < n_mid + n_qkv, lsegs[2][0], cfg["lout"]))
        lrow = jnp.where(down, k * sub, off + j * sub)
        rcol = jnp.where(down, j * cols, depth + kk * cols)
        return pl.multiple_of(lrow, sub), pl.multiple_of(rcol, cols)

    def product(blk, k, j):
        lrow, rcol = place(k, j)
        return jnp.dot(
            ltf[blk, pl.ds(lrow, sub), :], rf[:, pl.ds(rcol, cols)], preferred_element_type=jnp.float32)

    rows_p, cols_p = sub // pr, cols // pc

    def pieces(j):
        for a in range(rows_p):
            for b in range(cols_p):
                yield (j * rows_p + a) * cols_p + b, a * pr, b * pc

    nb = n_half // 2
    top = bit_of(*steps[0])

    def rs_copy(i, k):
        axis, bit = steps[i]
        if i == 0:
            src = dsend.at[k % slots]
        else:
            half = recv[i - 1].shape[1] // 2
            src = recv[i - 1].at[k, pl.ds((1 - bit_of(axis, bit)) * half, half)]
        return pltpu.make_async_remote_copy(
            src_ref=src, dst_ref=recv[i].at[k], send_sem=send_sem.at[i, k], recv_sem=recv_sem.at[i, k],
            device_id=peer(axis, bit), device_id_type=MESH)

    def own_start(size):
        at = 0
        for n, (axis, bit) in enumerate(steps[s_bits - 1 :]):
            block = n_rep >> (n + 1)
            if block >= size:
                at = at + bit_of(axis, bit) * block
        return at

    def ag_copy(i, k):
        axis, bit = back[i]
        size = 1 << i
        at = pl.ds(own_start(size), size)
        n = n_down_steps + i
        return pltpu.make_async_remote_copy(
            src_ref=outb.at[k, at], dst_ref=outb.at[k, at], send_sem=send_sem.at[n, k], recv_sem=recv_sem.at[n, k],
            device_id=peer(axis, bit), device_id_type=MESH)

    def out_copies(n, k):
        lo = cfg["sets"][n][0]
        made = []
        for j in range(2):
            for b in range(cols_p):
                if n == 0:
                    dst = out_refs[n].at[k, :, :, pl.ds(j * cols + b * pc, pc)]
                else:
                    at = pl.multiple_of((k - lo) * cols, cols) + b * pc
                    dst = out_refs[n].at[pl.ds(j * rows_p, rows_p), :, pl.ds(at, pc)]
                if cols_p == 1:
                    made.append((outb.at[k, pl.ds(j * rows_p, rows_p)], dst))
                else:
                    made += [
                        (outb.at[k, (j * rows_p + a) * cols_p + b], dst.at[a]) for a in range(rows_p)]
        return [pltpu.make_async_copy(src, dst, out_sem.at[k, i]) for i, (src, dst) in enumerate(made)]

    def each_set(k, act):
        for n, (lo, hi) in enumerate(cfg["sets"]):
            @pl.when((k >= lo) & (k < hi))
            def _(n=n):
                for cp in out_copies(n, k):
                    act(cp)

    def first(k):
        for i in range(nb):
            for j in range(2):
                part = product((1 - top) * nb + i, k, j).astype(jnp.bfloat16)
                for p, a, b in pieces(j):
                    dsend[k % slots, i * n_rep + p] = part[a : a + pr, b : b + pc]

    def join(i, k):
        rs_copy(i, k).wait()
        if i == 0:
            for n in range(nb):
                for j in range(2):
                    part = product(top * nb + n, k, j)
                    for p, a, b in pieces(j):
                        q = n * n_rep + p
                        got = recv[0][k, q].astype(jnp.float32)
                        recv[0][k, q] = (part[a : a + pr, b : b + pc] + got).astype(jnp.bfloat16)
            return
        half = recv[i].shape[1]
        base = bit_of(*steps[i]) * half
        for q in range(half):
            kept = recv[i - 1][k, base + q].astype(jnp.float32)
            both = (kept + recv[i][k, q].astype(jnp.float32)).astype(jnp.bfloat16)
            if i == n_down_steps - 1:
                outb[k, own_start(1)] = both
            else:
                recv[i][k, q] = both

    lag = [0, 2]
    for _ in range(n_down_steps - 1 + n_back):
        lag.append(lag[-1] + 2)
    last = lag[-1]

    def during(t, n, do):
        k = t - lag[n]

        @pl.when((k >= 0) & (k < n_all))
        def _():
            do(k)

    def body(t, carry):
        for i, when in ((0, 0), (1, n_down), (2, n_down + n_mid)):
            @pl.when(t == when)
            def _(i=i):
                for n, cp in enumerate(exchange(i)):
                    cp.wait()

        during(t, 0, first)
        for i in range(n_down_steps):
            during(t, 1 + i, functools.partial(join, i))
        for i in range(n_back):
            during(t, 1 + n_down_steps + i, lambda k, i=i: ag_copy(i, k).wait())
        for g in range(len(everyone)):
            @pl.when(t == 3 + 2 * g)
            def _(g=g):
                gain_copy(g).wait()
                gacc[g + 1] = gacc[g] + grecv[g]

        for i in range(n_down_steps):
            during(t, i, lambda k, i=i: rs_copy(i, k).start())
        for i in range(n_back):
            during(t, n_down_steps + i, lambda k, i=i: ag_copy(i, k).start())
        during(t, n_down_steps + n_back, lambda k: each_set(k, lambda cp: cp.start()))
        for g in range(len(everyone)):
            @pl.when(t == 1 + 2 * g)
            def _(g=g):
                gain_copy(g).start()

        return carry

    lax.fori_loop(0, n_all + last, body, 0)
    gout = pltpu.make_async_copy(gacc.at[len(everyone)], gout_ref, g_out)
    gout.start()

    def finish(k, carry):
        each_set(k, lambda cp: cp.wait())
        return carry

    lax.fori_loop(0, n_all, finish, 0)
    gout.wait()


def reduce_grads(hid, h2, h1, ob, dyb, dgate, dup, dqkv, dx2b, gains, n_rep, n_shard):
    tok, ff = hid.shape
    depth = h1.shape[1]
    qkv = dqkv.shape[1]
    n_half = n_shard // 2
    sub = depth // n_shard // 2
    cols = depth // 2
    pr = max(16, 2 * sub // n_rep)
    pc = cols * (2 * sub // pr) // n_rep
    n_down, n_mid, n_qkv, n_out = ff // cols, 2 * ff // cols, qkv // cols, depth // cols
    n_all = n_down + n_mid + n_qkv + n_out
    fs, ds = ff // n_shard, depth // n_shard
    lt = jnp.concatenate([v.T.reshape(n_shard, -1, tok) for v in (hid, h2, h1, ob)], axis=1)
    lt = lt.reshape(n_half, 2, -1, tok).transpose(1, 0, 2, 3)
    right = jnp.concatenate([dyb, dgate, dup, dqkv, dx2b], axis=1)
    lrows, rcols = lt.shape[2], right.shape[1]
    cfg = dict(
        n_rep=n_rep, n_shard=n_shard, tok=tok, sub=sub, cols=cols, pr=pr, pc=pc, depth=depth,
        n_down=n_down, n_mid=n_mid, n_qkv=n_qkv, n_all=n_all, lout=fs + 2 * ds,
        lsegs=((0, fs), (fs, fs + ds), (fs + ds, lrows)),
        rsegs=((0, depth), (depth, depth + 2 * ff), (depth + 2 * ff, rcols)),
    )
    g_rows = gains.shape[0]
    ends = [n_down, n_down + n_mid // 2, n_down + n_mid, n_down + n_mid + n_qkv, n_all]
    cfg["sets"] = tuple(zip([0] + ends[:-1], ends))
    rp, cp = sub // pr, cols // pc
    shapes = [(n_down, rp, pr, depth)] + [(2 * rp, pr, n) for n in (ff, ff, qkv, depth)]
    s_bits, r_bits = bit_count(n_shard), bit_count(n_rep)
    n_hops = s_bits + r_bits
    n_steps = s_bits - 1 + r_bits
    slots = 4
    sizes = [n_half * n_rep >> (i + 1) for i in range(n_steps)]
    bf = jnp.bfloat16
    dma = pltpu.SemaphoreType.DMA
    *outs, gsum = pl.pallas_call(
        functools.partial(sum_kernel, cfg),
        name="sum_grads",
        out_shape=(
            *[jax.ShapeDtypeStruct(shape, bf) for shape in shapes],
            jax.ShapeDtypeStruct((g_rows, 128), jnp.float32),
        ),
        in_specs=[pl.BlockSpec(memory_space=pltpu.VMEM)] * 3,
        out_specs=[pl.BlockSpec(memory_space=pltpu.HBM)] * (len(shapes) + 1),
        scratch_shapes=[
            pltpu.VMEM((n_half, lrows, 2 * tok), bf),
            pltpu.VMEM((2 * tok, rcols), bf),
            pltpu.VMEM((slots, sizes[0], pr, pc), bf),
            *[pltpu.VMEM((n_all, size, pr, pc), bf) for size in sizes],
            pltpu.VMEM((n_all, n_rep, pr, pc), bf),
            pltpu.VMEM((n_hops + 1, g_rows, 128), jnp.float32),
            pltpu.VMEM((n_hops, g_rows, 128), jnp.float32),
            dma((3, 2)), dma((3, 2)), dma((3, 2)),
            dma((n_steps + r_bits, n_all)), dma((n_steps + r_bits, n_all)), dma((n_all, 2 if cp == 1 else n_rep)),
            dma((n_hops,)), dma((n_hops,)), dma,
        ],
        compiler_params=pltpu.CompilerParams(
            collective_id=0, has_side_effects=True, vmem_limit_bytes=60_000_000),
    )(lt, right, gains)

    return [v.reshape(-1, v.shape[-1]).astype(jnp.float32) for v in outs], gsum


def local(
    n_rep,
    n_shard,
    tokens,
    cotangent,
    doc_ids,
    w_query,
    w_key,
    w_value,
    w_out,
    w_gate,
    w_up,
    w_down,
    gain_attn,
    gain_ffn,
    gain_query,
    gain_key,
):
    tok_rows, width = tokens.shape
    ff = w_gate.shape[1]
    q_width, k_width = w_query.shape[1], w_key.shape[1]
    head_share = QH // KVH
    score_scale = 1.0 / math.sqrt(HEAD_DIM)
    gains = (gain_attn, gain_ffn, gain_query, gain_key)
    gain_sizes = [g.shape[0] for g in gains]
    gain_ends = [sum(gain_sizes[: i + 1]) for i in range(len(gains))]
    flat_gains = jnp.concatenate(gains)
    n_gain = flat_gains.shape[0]
    flat_gains = jnp.pad(flat_gains, (0, -n_gain % 2048)).reshape(-1, 128)
    (qkv_set, out_set, gate_set, up_set, down_set), all_gains = gather_all(
        [[w_query, w_key, w_value], [w_out], [w_gate], [w_up], [w_down]], flat_gains, n_rep, n_shard
    )
    all_gains = all_gains.reshape(n_shard, -1)
    full_gattn, full_gffn, full_gquery, full_gkey = (
        all_gains[:, end - size : end].reshape(-1) for size, end in zip(gain_sizes, gain_ends)
    )

    doc_rows = doc_ids[None, :]
    allowed, positions = doc_tables(doc_rows)
    key_mask = allowed[:, None, None]
    cos_tab, sin_tab = rope_tables(positions, HEAD_DIM)
    resid_in = tokens.astype(jnp.float32)
    normed_in, unit_in, rms_in = norm_rows(resid_in, full_gattn)
    normed_bf = normed_in.astype(jnp.bfloat16)
    qkv = matmul(normed_bf, qkv_set)
    query_raw = qkv[:, :q_width].reshape(1, tok_rows, QH, HEAD_DIM)
    key_raw = qkv[:, q_width : q_width + k_width].reshape(1, tok_rows, KVH, HEAD_DIM)
    value_bf = qkv[:, q_width + k_width :].astype(jnp.bfloat16).reshape(1, tok_rows, KVH, HEAD_DIM)
    query_normed, query_unit, query_rms = norm_rows(query_raw, full_gquery)
    key_normed, key_unit, key_rms = norm_rows(key_raw, full_gkey)
    query_bf = (
        rotate(query_normed, cos_tab, sin_tab)
        .astype(jnp.bfloat16)
        .reshape(1, tok_rows, KVH, head_share, HEAD_DIM)
    )
    key_bf = rotate(key_normed, cos_tab, sin_tab).astype(jnp.bfloat16)
    attn_probs, log_total = attn_probs_of(query_bf, key_bf, key_mask, None, score_scale)
    probs_bf = attn_probs.astype(jnp.bfloat16)
    mixed_bf = (
        jnp.einsum("gkrqs,gskd->gqkrd", probs_bf, value_bf, preferred_element_type=jnp.float32)
        .astype(jnp.bfloat16)
        .reshape(tok_rows, QH * HEAD_DIM)
    )
    resid_mid = resid_in + matmul(mixed_bf, out_set)
    normed_mid, unit_mid, rms_mid = norm_rows(resid_mid, full_gffn)
    hidden_in = normed_mid.astype(jnp.bfloat16)
    gate_proj = matmul(hidden_in, gate_set)
    up_proj = matmul(hidden_in, up_set)
    gate_sig = jax.nn.sigmoid(gate_proj)
    gate_act = gate_proj * gate_sig
    hidden_bf = (gate_act * up_proj).astype(jnp.bfloat16)

    live_rows = (doc_ids >= 0).astype(jnp.float32)[:, None]
    grad_y = cotangent.astype(jnp.float32) * live_rows
    grad_y_bf = grad_y.astype(jnp.bfloat16)
    block_out = (resid_mid + matmul(hidden_bf, down_set)).astype(jnp.bfloat16)

    grad_hidden = matmul_t(grad_y_bf, down_set)
    grad_gate_bf = (grad_hidden * up_proj * gate_sig * (1.0 + gate_proj * (1.0 - gate_sig))).astype(
        jnp.bfloat16
    )
    grad_up_bf = (grad_hidden * gate_act).astype(jnp.bfloat16)
    grad_norm_mid = matmul_t(grad_gate_bf, gate_set) + matmul_t(grad_up_bf, up_set)
    back_mid, part_gffn = norm_back(grad_norm_mid, unit_mid, rms_mid, full_gffn)
    grad_mid = grad_y + back_mid
    grad_mid_bf = grad_mid.astype(jnp.bfloat16)
    grad_mixed_bf = (
        matmul_t(grad_mid_bf, out_set)
        .astype(jnp.bfloat16)
        .reshape(1, tok_rows, KVH, head_share, HEAD_DIM)
    )
    grad_scores = jnp.einsum(
        "gqkrd,gskd->gkrqs", grad_mixed_bf, value_bf, preferred_element_type=jnp.float32
    )
    grad_value_bf = (
        jnp.einsum("gkrqs,gqkrd->gskd", probs_bf, grad_mixed_bf, preferred_element_type=jnp.float32)
        .astype(jnp.bfloat16)
        .reshape(tok_rows, KVH * HEAD_DIM)
    )
    row_dot = jnp.sum(attn_probs * grad_scores, axis=-1, keepdims=True)
    grad_logits = (attn_probs * (grad_scores - row_dot) * score_scale).astype(jnp.bfloat16)
    grad_query_rot = jnp.einsum(
        "gkrqs,gskd->gqkrd", grad_logits, key_bf, preferred_element_type=jnp.float32
    ).reshape(1, tok_rows, QH, HEAD_DIM)
    grad_key_rot = jnp.einsum(
        "gkrqs,gqkrd->gskd", grad_logits, query_bf, preferred_element_type=jnp.float32
    )
    grad_query_raw, part_gquery = norm_back(
        rotate_back(grad_query_rot, cos_tab, sin_tab), query_unit, query_rms, full_gquery
    )
    grad_key_raw, part_gkey = norm_back(
        rotate_back(grad_key_rot, cos_tab, sin_tab), key_unit, key_rms, full_gkey
    )
    grad_query_bf = grad_query_raw.astype(jnp.bfloat16).reshape(tok_rows, QH * HEAD_DIM)
    grad_key_bf = grad_key_raw.astype(jnp.bfloat16).reshape(tok_rows, KVH * HEAD_DIM)
    grad_qkv_bf = jnp.concatenate([grad_query_bf, grad_key_bf, grad_value_bf], axis=1)
    grad_norm_in = matmul_t(grad_qkv_bf, qkv_set)
    back_in, part_gattn = norm_back(grad_norm_in, unit_in, rms_in, full_gattn)
    grad_tokens = grad_mid + back_in
    part_gains = jnp.concatenate(
        [
            p.reshape(n_shard, -1)
            for p in (part_gattn, part_gffn, part_gquery, part_gkey)
        ],
        axis=1,
    )
    part_gains = part_gains.astype(jnp.bfloat16).astype(jnp.float32)
    flat = part_gains.reshape(-1)
    flat = jnp.pad(flat, (0, -flat.shape[0] % 1024)).reshape(-1, 128)
    (grad_down, grad_gate, grad_up, grad_qkv, grad_out), sum_gains = reduce_grads(
        hidden_bf, hidden_in, normed_bf, mixed_bf,
        grad_y_bf, grad_gate_bf, grad_up_bf, grad_qkv_bf, grad_mid_bf,
        flat, n_rep, n_shard,
    )
    ends = [q_width, q_width + k_width]
    grad_query, grad_key, grad_value = jnp.split(grad_qkv, ends, axis=1)
    sum_gains = sum_gains.reshape(-1)[: part_gains.size].reshape(part_gains.shape)
    own_gains = lax.dynamic_index_in_dim(sum_gains, lax.axis_index("shard"), axis=0, keepdims=False)
    grad_gattn, grad_gffn, grad_gquery, grad_gkey = (
        own_gains[end - size : end] for size, end in zip(gain_sizes, gain_ends)
    )
    return (
        block_out,
        grad_tokens,
        grad_query,
        grad_key,
        grad_value,
        grad_out,
        grad_gate,
        grad_up,
        grad_down,
        grad_gattn,
        grad_gffn,
        grad_gquery,
        grad_gkey,
    )


def solution(mesh):
    return jax.shard_map(
        functools.partial(local, mesh.shape["rep"], mesh.shape["shard"]),
        mesh=mesh,
        in_specs=(
            P(("rep", "shard"), None),
            P(("rep", "shard"), None),
            P(("rep", "shard")),
            P("shard", None),
            P("shard", None),
            P("shard", None),
            P("shard", None),
            P("shard", None),
            P("shard", None),
            P("shard", None),
            P("shard"),
            P("shard"),
            P("shard"),
            P("shard"),
        ),
        out_specs=(
            P(("rep", "shard"), None),
            P(("rep", "shard"), None),
            P("shard", None),
            P("shard", None),
            P("shard", None),
            P("shard", None),
            P("shard", None),
            P("shard", None),
            P("shard", None),
            P("shard"),
            P("shard"),
            P("shard"),
            P("shard"),
        ),
        check_vma=False,
    )
```

```python
import functools
import math

import jax
import jax.numpy as jnp
from jax import lax
from jax.experimental import pallas as pl
from jax.experimental.pallas import tpu as pltpu
from jax.sharding import PartitionSpec as P

MESH = pl.DeviceIdType.MESH

QH = 16
KVH = 8
HEAD_DIM = 64


NORM_EPSILON = 1e-05
ROPE_BASE = 1000000.0


def matmul(left, right):
    return jnp.dot(left, right, preferred_element_type=jnp.float32)


def matmul_t(left, right):
    return lax.dot_general(left, right, (((1,), (1,)), ((), ())), preferred_element_type=jnp.float32)


def norm_rows(values, gain_vec):
    inv_rms = lax.rsqrt(jnp.mean(values * values, axis=-1, keepdims=True) + NORM_EPSILON)
    normed = values * inv_rms
    return (normed * gain_vec.astype(jnp.float32), normed, inv_rms)


def norm_back(grad_out, normed, inv_rms, gain_vec):
    scaled = grad_out * gain_vec.astype(jnp.float32)
    grad_in = inv_rms * (scaled - normed * jnp.mean(scaled * normed, axis=-1, keepdims=True))
    lead_axes = tuple(range(grad_out.ndim - 1))
    return (grad_in, jnp.sum(grad_out * normed, axis=lead_axes))


def doc_tables(doc_rows):
    block_len = doc_rows.shape[-1]
    row_index = jnp.arange(block_len)[:, None]
    col_index = jnp.arange(block_len)[None, :]
    same_doc = doc_rows[:, :, None] == doc_rows[:, None, :]
    allowed = same_doc & (row_index >= col_index)[None]
    earlier = same_doc & (row_index > col_index)[None]
    positions = jnp.sum(earlier.astype(jnp.int32), axis=2)
    return (allowed, positions)


def rope_tables(positions, head_dim):
    half_dim = head_dim // 2
    inv_freq = jnp.exp(
        jnp.arange(half_dim).astype(jnp.float32) * (-2.0 * math.log(ROPE_BASE) / head_dim)
    )
    angles = positions.astype(jnp.float32)[:, :, None, None] * inv_freq
    return (jnp.cos(angles), jnp.sin(angles))


def rotate(values, cos_tab, sin_tab):
    half_dim = values.shape[-1] // 2
    part_one = values[..., :half_dim]
    part_two = values[..., half_dim:]
    return jnp.concatenate(
        [part_one * cos_tab - part_two * sin_tab, part_two * cos_tab + part_one * sin_tab], axis=-1
    )


def rotate_back(values, cos_tab, sin_tab):
    half_dim = values.shape[-1] // 2
    part_one = values[..., :half_dim]
    part_two = values[..., half_dim:]
    return jnp.concatenate(
        [part_one * cos_tab + part_two * sin_tab, part_two * cos_tab - part_one * sin_tab], axis=-1
    )


def attn_probs_of(query_bf, key_bf, key_mask, log_total, score_scale):
    scores = (
        jnp.einsum("gqkrd,gskd->gkrqs", query_bf, key_bf, preferred_element_type=jnp.float32)
        * score_scale
    )
    if log_total is None:
        log_total = jnp.log(
            jnp.sum(jnp.where(key_mask, jnp.exp(scores), 0.0), axis=-1, keepdims=True)
        )
    return (jnp.where(key_mask, jnp.exp(scores - log_total), 0.0), log_total)


def bit_count(size):
    return size.bit_length() - 1


def gather_kernel(cfg, *refs):
    items, n_in, n_out = cfg["items"], cfg["n_in"], cfg["n_out"]
    ins, outs = refs[:n_in], refs[n_in : n_in + n_out]
    gain_in, gain_out = ins[-1], outs[-1]
    held = refs[n_in + n_out : n_in + 2 * n_out - 1]
    send_sem, recv_sem, own_sem, out_sem, gs_sem, gr_sem, go_sem = refs[n_in + 2 * n_out - 1 :]
    me_s, me_r = lax.axis_index("shard"), lax.axis_index("rep")
    core, y, z = me_s & 1, me_r & 1, (me_r >> 1) & 1
    peers = [{"shard": me_s ^ 1}, {"shard": me_s ^ 2}, {"rep": me_r ^ 1}, {"rep": me_r ^ 2}]
    to_core, to_x, to_y, to_z = peers
    barrier = pltpu.get_barrier_semaphore()
    for p in peers:
        pl.semaphore_signal(barrier, inc=1, device_id=p, device_id_type=MESH)
    pl.semaphore_wait(barrier, len(peers))

    other = me_s ^ 2
    mine = z * 2 + y
    from_y, from_z, diag = mine ^ 1, mine ^ 2, mine ^ 3

    def place(n, shard, row, size):
        it = items[n]
        return held[it["out"]].at[shard, pl.ds(it["row"] + row, size), pl.ds(it["dst"], it["cols"])]

    def result(n, shard, row, size):
        it = items[n]
        return outs[it["out"]].at[shard, pl.ds(it["row"] + row, size), pl.ds(it["dst"], it["cols"])]

    def fresh(n, row, size):
        it = items[n]
        return ins[it["in"]].at[pl.ds(it["row"] + row, size), pl.ds(it["src"], it["cols"])]

    def send(n, i, src, dst, to):
        return pltpu.make_async_remote_copy(
            src_ref=src, dst_ref=dst, send_sem=send_sem.at[n, i], recv_sem=recv_sem.at[n, i],
            device_id=to, device_id_type=MESH)

    def relay(n, i, row, size, to):
        ref = place(n, other, row, size)
        return send(n, i, ref, ref, to)

    def copies(n):
        it = items[n]
        rows, quarter = it["rows"], it["rows"] // 4
        dx, dy, dz = it["parts"]
        at = lambda q: pl.multiple_of(q * quarter, quarter)
        whole = lambda i, row, size, to: send(
            n, i, place(n, me_s, row, size), place(n, me_s, row, size), to)
        return dict(
            x=whole(0, at(mine), quarter, to_x),
            xd=whole(1, at(diag), dx, to_x),
            own=whole(2, 0, rows, to_core),
            y=relay(n, 3, at(mine), quarter, to_y),
            z=relay(n, 4, at(mine), quarter, to_z),
            c0=relay(n, 5, at(mine), quarter, to_core),
            fz=relay(n, 6, at(from_y) + dx + dy, dz, to_z),
            c1=relay(n, 7, at(from_y), quarter, to_core),
            fy=relay(n, 8, at(from_z) + dx, dy, to_y),
            c2=relay(n, 9, at(from_z), quarter, to_core),
            c3=relay(n, 10, at(diag), quarter, to_core),
            out=[
                pltpu.make_async_copy(
                    place(n, me_s ^ d, 0, rows), result(n, me_s ^ d, 0, rows), out_sem.at[n, d])
                for d in range(4)],
            keep=pltpu.make_async_copy(fresh(n, 0, rows), place(n, me_s, 0, rows), own_sem.at[n]),
        )

    gain_send = lambda i, shard, src, to: pltpu.make_async_remote_copy(
        src_ref=src, dst_ref=gain_out.at[shard], send_sem=gs_sem.at[i], recv_sem=gr_sem.at[i],
        device_id=to, device_id_type=MESH)
    gains = [
        gain_send(0, me_s, gain_in, to_x),
        gain_send(1, me_s, gain_in, to_core),
        gain_send(2, other, gain_out.at[other], to_core),
    ]
    gain_keep = pltpu.make_async_copy(gain_in, gain_out.at[me_s], go_sem)
    gain_keep.start()
    gains[0].start()
    gains[1].start()
    todo = [copies(n) for n in range(len(items))]
    for c in todo:
        c["keep"].start()
    for c in todo:
        c["keep"].wait()
        for k in ("x", "xd", "own"):
            c[k].start()
        c["out"][0].start()
    gains[0].wait_recv()
    gains[2].start()

    def near(c):
        c["x"].wait_recv()
        for k in ("y", "z", "c0"):
            c[k].start()

    def far(c):
        c["y"].wait_recv()
        c["fz"].start()
        c["c1"].start()
        c["z"].wait_recv()
        c["fy"].start()
        c["c2"].start()

    def end(c):
        for k in ("xd", "fy", "fz"):
            c[k].wait_recv()
        c["c3"].start()
        c["out"][2].start()
        c["own"].wait_recv()
        c["out"][1].start()

    def pair(c):
        for k in ("c0", "c1", "c2", "c3"):
            c[k].wait_recv()
        c["out"][3].start()

    count = len(todo)
    for t in range(count + 3):
        if t < count:
            near(todo[t])
        if 0 <= t - 1 < count:
            far(todo[t - 1])
        if 0 <= t - 2 < count:
            end(todo[t - 2])
        if 0 <= t - 3 < count:
            pair(todo[t - 3])
    for c in todo:
        for k in ("x", "xd", "own", "y", "z", "c0", "fz", "c1", "fy", "c2", "c3"):
            c[k].wait_send()
        for cp in c["out"]:
            cp.wait()
    gains[1].wait_recv()
    gains[2].wait_recv()
    for g in gains:
        g.wait_send()
    gain_keep.wait()


def gather_all(groups, gains, n_rep, n_shard):
    tile = 16
    fits = n_shard == 4 and n_rep >= 4 and all(w.shape[0] % (4 * tile) == 0 for g in groups for w in g)
    if not fits:
        full = [lax.all_gather(jnp.concatenate(g, axis=1), "shard", axis=0, tiled=True) for g in groups]
        return full, lax.all_gather(gains, "shard", axis=0)
    items, ins = [], []
    for o, group in enumerate(groups):
        dst = 0
        for w in group:
            rows, cols = w.shape
            big = w.size > 2 * 256 * 1024
            row_cut = 3 if big and rows > cols and rows % (12 * tile) == 0 else 1
            col_cut = 3 if big and row_cut == 1 and cols % 384 == 0 else 1
            step, width = rows // row_cut, cols // col_cut
            for a in range(row_cut):
                for b in range(col_cut):
                    units = step // 4 // tile
                    third = units // 3
                    rest = units - 3 * third
                    turn = len(items) % 2
                    parts = [third, third + (rest > turn), third + (rest > 1 - turn)]
                    parts[0] = units - parts[1] - parts[2]
                    items.append({
                        "in": len(ins), "out": o, "row": a * step, "rows": step, "src": b * width,
                        "dst": dst + b * width, "cols": width, "parts": tuple(p * tile for p in parts)})
            ins.append(w)
            dst += cols
    outs = [
        jax.ShapeDtypeStruct((n_shard, g[0].shape[0], sum(w.shape[1] for w in g)), g[0].dtype) for g in groups]
    outs.append(jax.ShapeDtypeStruct((n_shard,) + gains.shape, gains.dtype))
    n = len(items)
    dma = pltpu.SemaphoreType.DMA
    hbm = pl.BlockSpec(memory_space=pltpu.HBM)
    got = pl.pallas_call(
        functools.partial(gather_kernel, {"items": items, "n_in": len(ins) + 1, "n_out": len(outs)}),
        name="gather_weights",
        out_shape=tuple(outs),
        in_specs=[hbm] * (len(ins) + 1),
        out_specs=[hbm] * len(outs),
        scratch_shapes=[
            *[pltpu.VMEM(o.shape, o.dtype) for o in outs[:-1]],
            dma((n, 11)), dma((n, 11)), dma((n,)), dma((n, 4)), dma((3,)), dma((3,)), dma,
        ],
        compiler_params=pltpu.CompilerParams(
            collective_id=1, has_side_effects=True, vmem_limit_bytes=44_000_000),
    )(*ins, gains)
    return [g.reshape(-1, g.shape[-1]) for g in got[:-1]], got[-1]


def sum_kernel(cfg, lt_ref, r_ref, g_ref, *refs):
    n_sets = len(cfg["sets"])
    out_refs, gout_ref, scratch = refs[:n_sets], refs[n_sets], refs[n_sets + 1 :]
    n_rep, n_shard, tok = cfg["n_rep"], cfg["n_shard"], cfg["tok"]
    sub, cols, pr, pc = cfg["sub"], cfg["cols"], cfg["pr"], cfg["pc"]
    depth, n_down, n_mid, n_qkv, n_all = (cfg[k] for k in ("depth", "n_down", "n_mid", "n_qkv", "n_all"))
    lsegs, rsegs = cfg["lsegs"], cfg["rsegs"]
    s_bits, r_bits = bit_count(n_shard), bit_count(n_rep)
    n_half = n_shard // 2
    steps = [("shard", i) for i in reversed(range(1, s_bits))] + [("rep", i) for i in range(r_bits)]
    back = [("rep", i) for i in reversed(range(r_bits))]
    turned = list(steps)
    if r_bits >= 2:
        turned = [("rep", 1)] + [st for st in steps if st != ("rep", 1)]
    turned_back = [st for st in reversed(turned) if st[0] == "rep"]
    cycle = cfg["cycle"]
    n_down_steps, n_back = len(steps), len(back)
    ltf, rf, dsend = scratch[:3]
    recv = scratch[3 : 3 + n_down_steps]
    outb, gacc, grecv = scratch[3 + n_down_steps : 6 + n_down_steps]
    (ex_send, ex_recv, ex_own, send_sem, recv_sem, out_sem, g_send, g_recv, g_out) = scratch[6 + n_down_steps :]
    slots = dsend.shape[0]

    me_s, me_r = lax.axis_index("shard"), lax.axis_index("rep")
    core = me_s & 1

    def bit_of(axis, bit):
        return ((me_s if axis == "shard" else me_r) >> bit) & 1

    def peer(axis, bit):
        return {axis: (me_s if axis == "shard" else me_r) ^ (1 << bit)}

    def is_turned(k):
        return k % cycle == cycle // 2

    def bit_at(i, k):
        return jnp.where(is_turned(k), bit_of(*turned[i]), bit_of(*steps[i]))

    def peer_at(first, second, k):
        def moved(axis, me):
            ids = [me ^ (1 << bit) if name == axis else me for name, bit in (first, second)]
            return ids[0] if first == second else jnp.where(is_turned(k), ids[1], ids[0])

        return {"rep": moved("rep", me_r), "shard": moved("shard", me_s)}

    everyone = [("shard", i) for i in range(s_bits)] + [("rep", i) for i in range(r_bits)]
    barrier = pltpu.get_barrier_semaphore()
    for axis, bit in everyone:
        pl.semaphore_signal(barrier, inc=1, device_id=peer(axis, bit), device_id_type=MESH)
    pl.semaphore_wait(barrier, len(everyone))

    def exchange(i):
        (l0, l1), (r0, r1) = lsegs[i], rsegs[i]
        remote = [
            pltpu.make_async_remote_copy(
                src_ref=lt_ref.at[1 - core, :, pl.ds(l0, l1 - l0)],
                dst_ref=ltf.at[:, pl.ds(l0, l1 - l0), pl.ds(tok, tok)],
                send_sem=ex_send.at[i, 0], recv_sem=ex_recv.at[i, 0],
                device_id=peer("shard", 0), device_id_type=MESH),
            pltpu.make_async_remote_copy(
                src_ref=r_ref.at[:, pl.ds(r0, r1 - r0)],
                dst_ref=rf.at[pl.ds(tok, tok), pl.ds(r0, r1 - r0)],
                send_sem=ex_send.at[i, 1], recv_sem=ex_recv.at[i, 1],
                device_id=peer("shard", 0), device_id_type=MESH),
        ]
        local = [
            pltpu.make_async_copy(
                lt_ref.at[core, :, pl.ds(l0, l1 - l0)],
                ltf.at[:, pl.ds(l0, l1 - l0), pl.ds(0, tok)], ex_own.at[i, 0]),
            pltpu.make_async_copy(
                r_ref.at[:, pl.ds(r0, r1 - r0)], rf.at[pl.ds(0, tok), pl.ds(r0, r1 - r0)], ex_own.at[i, 1]),
        ]
        return remote + local

    for i in range(3):
        for cp in exchange(i):
            cp.start()

    gacc[0] = g_ref[...]

    def gain_copy(i):
        axis, bit = everyone[i]
        return pltpu.make_async_remote_copy(
            src_ref=gacc.at[i], dst_ref=grecv.at[i], send_sem=g_send.at[i], recv_sem=g_recv.at[i],
            device_id=peer(axis, bit), device_id_type=MESH)

    def place(k, j):
        kk = k - n_down
        down = k < n_down
        off = jnp.where(kk < n_mid, lsegs[1][0], jnp.where(kk < n_mid + n_qkv, lsegs[2][0], cfg["lout"]))
        lrow = jnp.where(down, k * sub, off + j * sub)
        rcol = jnp.where(down, j * cols, depth + kk * cols)
        return pl.multiple_of(lrow, sub), pl.multiple_of(rcol, cols)

    def product(blk, k, j):
        lrow, rcol = place(k, j)
        return jnp.dot(
            ltf[blk, pl.ds(lrow, sub), :], rf[:, pl.ds(rcol, cols)], preferred_element_type=jnp.float32)

    rows_p, cols_p = sub // pr, cols // pc

    def pieces(j):
        for a in range(rows_p):
            for b in range(cols_p):
                yield (j * rows_p + a) * cols_p + b, a * pr, b * pc

    nb = n_half // 2
    top = bit_of(*steps[0])

    def part_of(i, k, mine):
        if r_bits < 2:
            lead = top if mine else 1 - top
            return product(lead * nb + i // 2, k, i % 2)
        turn, z = is_turned(k), bit_of(*turned[0])
        lead, half = (top, z) if mine else (1 - top, 1 - z)
        return product(jnp.where(turn, i, lead * nb + i // 2), k, jnp.where(turn, half, i % 2))

    def rs_copy(i, k):
        if i == 0:
            src = dsend.at[k % slots]
        else:
            half = recv[i - 1].shape[1] // 2
            src = recv[i - 1].at[k, pl.ds((1 - bit_at(i, k)) * half, half)]
        return pltpu.make_async_remote_copy(
            src_ref=src, dst_ref=recv[i].at[k], send_sem=send_sem.at[i, k], recv_sem=recv_sem.at[i, k],
            device_id=peer_at(steps[i], turned[i], k), device_id_type=MESH)

    def own_start(size, k):
        def start(order):
            at = 0
            for n, (axis, bit) in enumerate(order):
                block = n_rep >> (n + 1)
                if block >= size:
                    at = at + bit_of(axis, bit) * block
            return at

        return jnp.where(is_turned(k), start(turned_back[::-1]), start(back[::-1]))

    def ag_copy(i, k):
        size = 1 << i
        at = pl.ds(own_start(size, k), size)
        n = n_down_steps + i
        return pltpu.make_async_remote_copy(
            src_ref=outb.at[k, at], dst_ref=outb.at[k, at], send_sem=send_sem.at[n, k], recv_sem=recv_sem.at[n, k],
            device_id=peer_at(back[i], turned_back[i], k), device_id_type=MESH)

    def out_copies(n, k):
        lo = cfg["sets"][n][0]
        made = []
        for j in range(2):
            for b in range(cols_p):
                if n == 0:
                    dst = out_refs[n].at[k, :, :, pl.ds(j * cols + b * pc, pc)]
                else:
                    at = pl.multiple_of((k - lo) * cols, cols) + b * pc
                    dst = out_refs[n].at[pl.ds(j * rows_p, rows_p), :, pl.ds(at, pc)]
                if cols_p == 1:
                    made.append((outb.at[k, pl.ds(j * rows_p, rows_p)], dst))
                else:
                    made += [
                        (outb.at[k, (j * rows_p + a) * cols_p + b], dst.at[a]) for a in range(rows_p)]
        return [pltpu.make_async_copy(src, dst, out_sem.at[k, i]) for i, (src, dst) in enumerate(made)]

    def each_set(k, act):
        for n, (lo, hi) in enumerate(cfg["sets"]):
            @pl.when((k >= lo) & (k < hi))
            def _(n=n):
                for cp in out_copies(n, k):
                    act(cp)

    def spread(i):
        for p, a, b in pieces(0):
            yield i * (n_rep // 2) + p, a, b

    def first(k):
        for i in range(n_half):
            part = part_of(i, k, False).astype(jnp.bfloat16)
            for q, a, b in spread(i):
                dsend[k % slots, q] = part[a : a + pr, b : b + pc]

    def join(i, k):
        rs_copy(i, k).wait()
        if i == 0:
            for n in range(n_half):
                part = part_of(n, k, True)
                for q, a, b in spread(n):
                    got = recv[0][k, q].astype(jnp.float32)
                    recv[0][k, q] = (part[a : a + pr, b : b + pc] + got).astype(jnp.bfloat16)
            return
        half = recv[i].shape[1]
        base = bit_at(i, k) * half
        for q in range(half):
            kept = recv[i - 1][k, base + q].astype(jnp.float32)
            both = (kept + recv[i][k, q].astype(jnp.float32)).astype(jnp.bfloat16)
            if i == n_down_steps - 1:
                outb[k, own_start(1, k)] = both
            else:
                recv[i][k, q] = both

    lag = [0, 2]
    for _ in range(n_down_steps - 1 + n_back):
        lag.append(lag[-1] + 2)
    last = lag[-1]

    def during(t, n, do):
        k = t - lag[n]

        @pl.when((k >= 0) & (k < n_all))
        def _():
            do(k)

    def body(t, carry):
        for i, when in ((0, 0), (1, n_down), (2, n_down + n_mid)):
            @pl.when(t == when)
            def _(i=i):
                for n, cp in enumerate(exchange(i)):
                    cp.wait()

        during(t, 0, first)
        for i in range(n_down_steps):
            during(t, 1 + i, functools.partial(join, i))
        for i in range(n_back):
            during(t, 1 + n_down_steps + i, lambda k, i=i: ag_copy(i, k).wait())
        for g in range(len(everyone)):
            @pl.when(t == 3 + 2 * g)
            def _(g=g):
                gain_copy(g).wait()
                gacc[g + 1] = gacc[g] + grecv[g]

        for i in range(n_down_steps):
            during(t, i, lambda k, i=i: rs_copy(i, k).start())
        for i in range(n_back):
            during(t, n_down_steps + i, lambda k, i=i: ag_copy(i, k).start())
        during(t, n_down_steps + n_back, lambda k: each_set(k, lambda cp: cp.start()))
        for g in range(len(everyone)):
            @pl.when(t == 1 + 2 * g)
            def _(g=g):
                gain_copy(g).start()

        return carry

    lax.fori_loop(0, n_all + last, body, 0)
    gout = pltpu.make_async_copy(gacc.at[len(everyone)], gout_ref, g_out)
    gout.start()

    def finish(k, carry):
        each_set(k, lambda cp: cp.wait())
        return carry

    lax.fori_loop(0, n_all, finish, 0)
    gout.wait()


def reduce_grads(hid, h2, h1, ob, dyb, dgate, dup, dqkv, dx2b, gains, n_rep, n_shard):
    tok, ff = hid.shape
    depth = h1.shape[1]
    qkv = dqkv.shape[1]
    n_half = n_shard // 2
    sub = depth // n_shard // 2
    cols = depth // 2
    pr = max(16, 2 * sub // n_rep)
    pc = cols * (2 * sub // pr) // n_rep
    n_down, n_mid, n_qkv, n_out = ff // cols, 2 * ff // cols, qkv // cols, depth // cols
    n_all = n_down + n_mid + n_qkv + n_out
    fs, ds = ff // n_shard, depth // n_shard
    lt = jnp.concatenate([v.T.reshape(n_shard, -1, tok) for v in (hid, h2, h1, ob)], axis=1)
    lt = lt.reshape(n_half, 2, -1, tok).transpose(1, 0, 2, 3)
    right = jnp.concatenate([dyb, dgate, dup, dqkv, dx2b], axis=1)
    lrows, rcols = lt.shape[2], right.shape[1]
    cfg = dict(
        n_rep=n_rep, n_shard=n_shard, tok=tok, sub=sub, cols=cols, pr=pr, pc=pc, depth=depth, cycle=6,
        n_down=n_down, n_mid=n_mid, n_qkv=n_qkv, n_all=n_all, lout=fs + 2 * ds,
        lsegs=((0, fs), (fs, fs + ds), (fs + ds, lrows)),
        rsegs=((0, depth), (depth, depth + 2 * ff), (depth + 2 * ff, rcols)),
    )
    g_rows = gains.shape[0]
    ends = [n_down, n_down + n_mid // 2, n_down + n_mid, n_down + n_mid + n_qkv, n_all]
    cfg["sets"] = tuple(zip([0] + ends[:-1], ends))
    rp, cp = sub // pr, cols // pc
    shapes = [(n_down, rp, pr, depth)] + [(2 * rp, pr, n) for n in (ff, ff, qkv, depth)]
    s_bits, r_bits = bit_count(n_shard), bit_count(n_rep)
    n_hops = s_bits + r_bits
    n_steps = s_bits - 1 + r_bits
    slots = 4
    sizes = [n_half * n_rep >> (i + 1) for i in range(n_steps)]
    bf = jnp.bfloat16
    dma = pltpu.SemaphoreType.DMA
    *outs, gsum = pl.pallas_call(
        functools.partial(sum_kernel, cfg),
        name="sum_grads",
        out_shape=(
            *[jax.ShapeDtypeStruct(shape, bf) for shape in shapes],
            jax.ShapeDtypeStruct((g_rows, 128), jnp.float32),
        ),
        in_specs=[pl.BlockSpec(memory_space=pltpu.VMEM)] * 3,
        out_specs=[pl.BlockSpec(memory_space=pltpu.HBM)] * (len(shapes) + 1),
        scratch_shapes=[
            pltpu.VMEM((n_half, lrows, 2 * tok), bf),
            pltpu.VMEM((2 * tok, rcols), bf),
            pltpu.VMEM((slots, sizes[0], pr, pc), bf),
            *[pltpu.VMEM((n_all, size, pr, pc), bf) for size in sizes],
            pltpu.VMEM((n_all, n_rep, pr, pc), bf),
            pltpu.VMEM((n_hops + 1, g_rows, 128), jnp.float32),
            pltpu.VMEM((n_hops, g_rows, 128), jnp.float32),
            dma((3, 2)), dma((3, 2)), dma((3, 2)),
            dma((n_steps + r_bits, n_all)), dma((n_steps + r_bits, n_all)), dma((n_all, 2 if cp == 1 else n_rep)),
            dma((n_hops,)), dma((n_hops,)), dma,
        ],
        compiler_params=pltpu.CompilerParams(
            collective_id=0, has_side_effects=True, vmem_limit_bytes=60_000_000),
    )(lt, right, gains)

    return [v.reshape(-1, v.shape[-1]).astype(jnp.float32) for v in outs], gsum


def local(
    n_rep,
    n_shard,
    tokens,
    cotangent,
    doc_ids,
    w_query,
    w_key,
    w_value,
    w_out,
    w_gate,
    w_up,
    w_down,
    gain_attn,
    gain_ffn,
    gain_query,
    gain_key,
):
    tok_rows, width = tokens.shape
    ff = w_gate.shape[1]
    q_width, k_width = w_query.shape[1], w_key.shape[1]
    head_share = QH // KVH
    score_scale = 1.0 / math.sqrt(HEAD_DIM)
    gains = (gain_attn, gain_ffn, gain_query, gain_key)
    gain_sizes = [g.shape[0] for g in gains]
    gain_ends = [sum(gain_sizes[: i + 1]) for i in range(len(gains))]
    flat_gains = jnp.concatenate(gains)
    n_gain = flat_gains.shape[0]
    flat_gains = jnp.pad(flat_gains, (0, -n_gain % 2048)).reshape(-1, 128)
    (qkv_set, out_set, gate_set, up_set, down_set), all_gains = gather_all(
        [[w_query, w_key, w_value], [w_out], [w_gate], [w_up], [w_down]], flat_gains, n_rep, n_shard
    )
    all_gains = all_gains.reshape(n_shard, -1)
    full_gattn, full_gffn, full_gquery, full_gkey = (
        all_gains[:, end - size : end].reshape(-1) for size, end in zip(gain_sizes, gain_ends)
    )

    doc_rows = doc_ids[None, :]
    allowed, positions = doc_tables(doc_rows)
    key_mask = allowed[:, None, None]
    cos_tab, sin_tab = rope_tables(positions, HEAD_DIM)
    resid_in = tokens.astype(jnp.float32)
    normed_in, unit_in, rms_in = norm_rows(resid_in, full_gattn)
    normed_bf = normed_in.astype(jnp.bfloat16)
    qkv = matmul(normed_bf, qkv_set)
    query_raw = qkv[:, :q_width].reshape(1, tok_rows, QH, HEAD_DIM)
    key_raw = qkv[:, q_width : q_width + k_width].reshape(1, tok_rows, KVH, HEAD_DIM)
    value_bf = qkv[:, q_width + k_width :].astype(jnp.bfloat16).reshape(1, tok_rows, KVH, HEAD_DIM)
    query_normed, query_unit, query_rms = norm_rows(query_raw, full_gquery)
    key_normed, key_unit, key_rms = norm_rows(key_raw, full_gkey)
    query_bf = (
        rotate(query_normed, cos_tab, sin_tab)
        .astype(jnp.bfloat16)
        .reshape(1, tok_rows, KVH, head_share, HEAD_DIM)
    )
    key_bf = rotate(key_normed, cos_tab, sin_tab).astype(jnp.bfloat16)
    attn_probs, log_total = attn_probs_of(query_bf, key_bf, key_mask, None, score_scale)
    probs_bf = attn_probs.astype(jnp.bfloat16)
    mixed_bf = (
        jnp.einsum("gkrqs,gskd->gqkrd", probs_bf, value_bf, preferred_element_type=jnp.float32)
        .astype(jnp.bfloat16)
        .reshape(tok_rows, QH * HEAD_DIM)
    )
    resid_mid = resid_in + matmul(mixed_bf, out_set)
    normed_mid, unit_mid, rms_mid = norm_rows(resid_mid, full_gffn)
    hidden_in = normed_mid.astype(jnp.bfloat16)
    gate_proj = matmul(hidden_in, gate_set)
    up_proj = matmul(hidden_in, up_set)
    gate_sig = jax.nn.sigmoid(gate_proj)
    gate_act = gate_proj * gate_sig
    hidden_bf = (gate_act * up_proj).astype(jnp.bfloat16)

    live_rows = (doc_ids >= 0).astype(jnp.float32)[:, None]
    grad_y = cotangent.astype(jnp.float32) * live_rows
    grad_y_bf = grad_y.astype(jnp.bfloat16)
    block_out = (resid_mid + matmul(hidden_bf, down_set)).astype(jnp.bfloat16)

    grad_hidden = matmul_t(grad_y_bf, down_set)
    grad_gate_bf = (grad_hidden * up_proj * gate_sig * (1.0 + gate_proj * (1.0 - gate_sig))).astype(
        jnp.bfloat16
    )
    grad_up_bf = (grad_hidden * gate_act).astype(jnp.bfloat16)
    grad_norm_mid = matmul_t(grad_gate_bf, gate_set) + matmul_t(grad_up_bf, up_set)
    back_mid, part_gffn = norm_back(grad_norm_mid, unit_mid, rms_mid, full_gffn)
    grad_mid = grad_y + back_mid
    grad_mid_bf = grad_mid.astype(jnp.bfloat16)
    grad_mixed_bf = (
        matmul_t(grad_mid_bf, out_set)
        .astype(jnp.bfloat16)
        .reshape(1, tok_rows, KVH, head_share, HEAD_DIM)
    )
    grad_scores = jnp.einsum(
        "gqkrd,gskd->gkrqs", grad_mixed_bf, value_bf, preferred_element_type=jnp.float32
    )
    grad_value_bf = (
        jnp.einsum("gkrqs,gqkrd->gskd", probs_bf, grad_mixed_bf, preferred_element_type=jnp.float32)
        .astype(jnp.bfloat16)
        .reshape(tok_rows, KVH * HEAD_DIM)
    )
    row_dot = jnp.sum(attn_probs * grad_scores, axis=-1, keepdims=True)
    grad_logits = (attn_probs * (grad_scores - row_dot) * score_scale).astype(jnp.bfloat16)
    grad_query_rot = jnp.einsum(
        "gkrqs,gskd->gqkrd", grad_logits, key_bf, preferred_element_type=jnp.float32
    ).reshape(1, tok_rows, QH, HEAD_DIM)
    grad_key_rot = jnp.einsum(
        "gkrqs,gqkrd->gskd", grad_logits, query_bf, preferred_element_type=jnp.float32
    )
    grad_query_raw, part_gquery = norm_back(
        rotate_back(grad_query_rot, cos_tab, sin_tab), query_unit, query_rms, full_gquery
    )
    grad_key_raw, part_gkey = norm_back(
        rotate_back(grad_key_rot, cos_tab, sin_tab), key_unit, key_rms, full_gkey
    )
    grad_query_bf = grad_query_raw.astype(jnp.bfloat16).reshape(tok_rows, QH * HEAD_DIM)
    grad_key_bf = grad_key_raw.astype(jnp.bfloat16).reshape(tok_rows, KVH * HEAD_DIM)
    grad_qkv_bf = jnp.concatenate([grad_query_bf, grad_key_bf, grad_value_bf], axis=1)
    grad_norm_in = matmul_t(grad_qkv_bf, qkv_set)
    back_in, part_gattn = norm_back(grad_norm_in, unit_in, rms_in, full_gattn)
    grad_tokens = grad_mid + back_in
    part_gains = jnp.concatenate(
        [
            p.reshape(n_shard, -1)
            for p in (part_gattn, part_gffn, part_gquery, part_gkey)
        ],
        axis=1,
    )
    part_gains = part_gains.astype(jnp.bfloat16).astype(jnp.float32)
    flat = part_gains.reshape(-1)
    flat = jnp.pad(flat, (0, -flat.shape[0] % 1024)).reshape(-1, 128)
    (grad_down, grad_gate, grad_up, grad_qkv, grad_out), sum_gains = reduce_grads(
        hidden_bf, hidden_in, normed_bf, mixed_bf,
        grad_y_bf, grad_gate_bf, grad_up_bf, grad_qkv_bf, grad_mid_bf,
        flat, n_rep, n_shard,
    )
    ends = [q_width, q_width + k_width]
    grad_query, grad_key, grad_value = jnp.split(grad_qkv, ends, axis=1)
    sum_gains = sum_gains.reshape(-1)[: part_gains.size].reshape(part_gains.shape)
    own_gains = lax.dynamic_index_in_dim(sum_gains, lax.axis_index("shard"), axis=0, keepdims=False)
    grad_gattn, grad_gffn, grad_gquery, grad_gkey = (
        own_gains[end - size : end] for size, end in zip(gain_sizes, gain_ends)
    )
    return (
        block_out,
        grad_tokens,
        grad_query,
        grad_key,
        grad_value,
        grad_out,
        grad_gate,
        grad_up,
        grad_down,
        grad_gattn,
        grad_gffn,
        grad_gquery,
        grad_gkey,
    )


def solution(mesh):
    return jax.shard_map(
        functools.partial(local, mesh.shape["rep"], mesh.shape["shard"]),
        mesh=mesh,
        in_specs=(
            P(("rep", "shard"), None),
            P(("rep", "shard"), None),
            P(("rep", "shard")),
            P("shard", None),
            P("shard", None),
            P("shard", None),
            P("shard", None),
            P("shard", None),
            P("shard", None),
            P("shard", None),
            P("shard"),
            P("shard"),
            P("shard"),
            P("shard"),
        ),
        out_specs=(
            P(("rep", "shard"), None),
            P(("rep", "shard"), None),
            P("shard", None),
            P("shard", None),
            P("shard", None),
            P("shard", None),
            P("shard", None),
            P("shard", None),
            P("shard", None),
            P("shard"),
            P("shard"),
            P("shard"),
            P("shard"),
        ),
        check_vma=False,
    )
```

```python
import functools
import math

import jax
import jax.numpy as jnp
from jax import lax
from jax.experimental import pallas as pl
from jax.experimental.pallas import tpu as pltpu
from jax.sharding import PartitionSpec as P

MESH = pl.DeviceIdType.MESH

QH = 16
KVH = 8
HEAD_DIM = 64


NORM_EPSILON = 1e-05
ROPE_BASE = 1000000.0


def matmul(left, right):
    return jnp.dot(left, right, preferred_element_type=jnp.float32)


def matmul_t(left, right):
    return lax.dot_general(left, right, (((1,), (1,)), ((), ())), preferred_element_type=jnp.float32)


def norm_rows(values, gain_vec):
    inv_rms = lax.rsqrt(jnp.mean(values * values, axis=-1, keepdims=True) + NORM_EPSILON)
    normed = values * inv_rms
    return (normed * gain_vec.astype(jnp.float32), normed, inv_rms)


def norm_back(grad_out, normed, inv_rms, gain_vec):
    scaled = grad_out * gain_vec.astype(jnp.float32)
    grad_in = inv_rms * (scaled - normed * jnp.mean(scaled * normed, axis=-1, keepdims=True))
    lead_axes = tuple(range(grad_out.ndim - 1))
    return (grad_in, jnp.sum(grad_out * normed, axis=lead_axes))


def doc_tables(doc_rows):
    block_len = doc_rows.shape[-1]
    row_index = jnp.arange(block_len)[:, None]
    col_index = jnp.arange(block_len)[None, :]
    same_doc = doc_rows[:, :, None] == doc_rows[:, None, :]
    allowed = same_doc & (row_index >= col_index)[None]
    earlier = same_doc & (row_index > col_index)[None]
    positions = jnp.sum(earlier.astype(jnp.int32), axis=2)
    return (allowed, positions)


def rope_tables(positions, head_dim):
    half_dim = head_dim // 2
    inv_freq = jnp.exp(
        jnp.arange(half_dim).astype(jnp.float32) * (-2.0 * math.log(ROPE_BASE) / head_dim)
    )
    angles = positions.astype(jnp.float32)[:, :, None, None] * inv_freq
    return (jnp.cos(angles), jnp.sin(angles))


def rotate(values, cos_tab, sin_tab):
    half_dim = values.shape[-1] // 2
    part_one = values[..., :half_dim]
    part_two = values[..., half_dim:]
    return jnp.concatenate(
        [part_one * cos_tab - part_two * sin_tab, part_two * cos_tab + part_one * sin_tab], axis=-1
    )


def rotate_back(values, cos_tab, sin_tab):
    half_dim = values.shape[-1] // 2
    part_one = values[..., :half_dim]
    part_two = values[..., half_dim:]
    return jnp.concatenate(
        [part_one * cos_tab + part_two * sin_tab, part_two * cos_tab - part_one * sin_tab], axis=-1
    )


def attn_probs_of(query_bf, key_bf, key_mask, log_total, score_scale):
    scores = (
        jnp.einsum("gqkrd,gskd->gkrqs", query_bf, key_bf, preferred_element_type=jnp.float32)
        * score_scale
    )
    if log_total is None:
        log_total = jnp.log(
            jnp.sum(jnp.where(key_mask, jnp.exp(scores), 0.0), axis=-1, keepdims=True)
        )
    return (jnp.where(key_mask, jnp.exp(scores - log_total), 0.0), log_total)


def bit_count(size):
    return size.bit_length() - 1


def gather_kernel(cfg, *refs):
    items, n_in, n_out = cfg["items"], cfg["n_in"], cfg["n_out"]
    ins, outs = refs[:n_in], refs[n_in : n_in + n_out]
    gain_in, gain_out = ins[-1], outs[-1]
    held = refs[n_in + n_out : n_in + 2 * n_out - 1]
    send_sem, recv_sem, own_sem, out_sem, gs_sem, gr_sem, go_sem = refs[n_in + 2 * n_out - 1 :]
    me_s, me_r = lax.axis_index("shard"), lax.axis_index("rep")
    core, y, z = me_s & 1, me_r & 1, (me_r >> 1) & 1
    peers = [{"shard": me_s ^ 1}, {"shard": me_s ^ 2}, {"rep": me_r ^ 1}, {"rep": me_r ^ 2}]
    to_core, to_x, to_y, to_z = peers
    barrier = pltpu.get_barrier_semaphore()
    for p in peers:
        pl.semaphore_signal(barrier, inc=1, device_id=p, device_id_type=MESH)
    pl.semaphore_wait(barrier, len(peers))

    other = me_s ^ 2
    mine = z * 2 + y
    from_y, from_z, diag = mine ^ 1, mine ^ 2, mine ^ 3

    def place(n, shard, row, size):
        it = items[n]
        return held[it["out"]].at[shard, pl.ds(it["row"] + row, size), pl.ds(it["dst"], it["cols"])]

    def result(n, shard, row, size):
        it = items[n]
        return outs[it["out"]].at[shard, pl.ds(it["row"] + row, size), pl.ds(it["dst"], it["cols"])]

    def fresh(n, row, size):
        it = items[n]
        return ins[it["in"]].at[pl.ds(it["row"] + row, size), pl.ds(it["src"], it["cols"])]

    def send(n, i, src, dst, to):
        return pltpu.make_async_remote_copy(
            src_ref=src, dst_ref=dst, send_sem=send_sem.at[n, i], recv_sem=recv_sem.at[n, i],
            device_id=to, device_id_type=MESH)

    def relay(n, i, row, size, to):
        ref = place(n, other, row, size)
        return send(n, i, ref, ref, to)

    def copies(n):
        it = items[n]
        rows, quarter = it["rows"], it["rows"] // 4
        dx, dy, dz = it["parts"]
        at = lambda q: pl.multiple_of(q * quarter, quarter)
        whole = lambda i, row, size, to: send(
            n, i, place(n, me_s, row, size), place(n, me_s, row, size), to)
        return dict(
            x=whole(0, at(mine), quarter, to_x),
            xd=whole(1, at(diag), dx, to_x),
            own=whole(2, 0, rows, to_core),
            y=relay(n, 3, at(mine), quarter, to_y),
            z=relay(n, 4, at(mine), quarter, to_z),
            c0=relay(n, 5, at(mine), quarter, to_core),
            fz=relay(n, 6, at(from_y) + dx + dy, dz, to_z),
            c1=relay(n, 7, at(from_y), quarter, to_core),
            fy=relay(n, 8, at(from_z) + dx, dy, to_y),
            c2=relay(n, 9, at(from_z), quarter, to_core),
            c3=relay(n, 10, at(diag), quarter, to_core),
            out=[
                pltpu.make_async_copy(
                    place(n, me_s ^ d, 0, rows), result(n, me_s ^ d, 0, rows), out_sem.at[n, d])
                for d in range(4)],
            keep=pltpu.make_async_copy(fresh(n, 0, rows), place(n, me_s, 0, rows), own_sem.at[n]),
        )

    gain_send = lambda i, shard, src, to: pltpu.make_async_remote_copy(
        src_ref=src, dst_ref=gain_out.at[shard], send_sem=gs_sem.at[i], recv_sem=gr_sem.at[i],
        device_id=to, device_id_type=MESH)
    gains = [
        gain_send(0, me_s, gain_in, to_x),
        gain_send(1, me_s, gain_in, to_core),
        gain_send(2, other, gain_out.at[other], to_core),
    ]
    gain_keep = pltpu.make_async_copy(gain_in, gain_out.at[me_s], go_sem)
    gain_keep.start()
    gains[0].start()
    gains[1].start()
    todo = [copies(n) for n in range(len(items))]
    for c in todo:
        c["keep"].start()
    for c in todo:
        c["keep"].wait()
        for k in ("x", "xd", "own"):
            c[k].start()
        c["out"][0].start()
    gains[0].wait_recv()
    gains[2].start()

    def near(c):
        c["x"].wait_recv()
        for k in ("y", "z", "c0"):
            c[k].start()

    def far(c):
        c["y"].wait_recv()
        c["fz"].start()
        c["c1"].start()
        c["z"].wait_recv()
        c["fy"].start()
        c["c2"].start()

    def end(c):
        for k in ("xd", "fy", "fz"):
            c[k].wait_recv()
        c["c3"].start()
        c["out"][2].start()
        c["own"].wait_recv()
        c["out"][1].start()

    def pair(c):
        for k in ("c0", "c1", "c2", "c3"):
            c[k].wait_recv()
        c["out"][3].start()

    count = len(todo)
    for t in range(count + 3):
        if t < count:
            near(todo[t])
        if 0 <= t - 1 < count:
            far(todo[t - 1])
        if 0 <= t - 2 < count:
            end(todo[t - 2])
        if 0 <= t - 3 < count:
            pair(todo[t - 3])
    for c in todo:
        for k in ("x", "xd", "own", "y", "z", "c0", "fz", "c1", "fy", "c2", "c3"):
            c[k].wait_send()
        for cp in c["out"]:
            cp.wait()
    gains[1].wait_recv()
    gains[2].wait_recv()
    for g in gains:
        g.wait_send()
    gain_keep.wait()


def gather_all(groups, gains, n_rep, n_shard):
    tile = 16
    fits = n_shard == 4 and n_rep >= 4 and all(w.shape[0] % (4 * tile) == 0 for g in groups for w in g)
    if not fits:
        full = [lax.all_gather(jnp.concatenate(g, axis=1), "shard", axis=0, tiled=True) for g in groups]
        return full, lax.all_gather(gains, "shard", axis=0)
    items, ins = [], []
    for o, group in enumerate(groups):
        dst = 0
        for w in group:
            rows, cols = w.shape
            big = w.size > 2 * 256 * 1024
            row_cut = 3 if big and rows > cols and rows % (12 * tile) == 0 else 1
            col_cut = 3 if big and row_cut == 1 and cols % 384 == 0 else 1
            step, width = rows // row_cut, cols // col_cut
            for a in range(row_cut):
                for b in range(col_cut):
                    units = step // 4 // tile
                    third = units // 3
                    rest = units - 3 * third
                    turn = len(items) % 2
                    parts = [third, third + (rest > turn), third + (rest > 1 - turn)]
                    parts[0] = units - parts[1] - parts[2]
                    items.append({
                        "in": len(ins), "out": o, "row": a * step, "rows": step, "src": b * width,
                        "dst": dst + b * width, "cols": width, "parts": tuple(p * tile for p in parts)})
            ins.append(w)
            dst += cols
    outs = [
        jax.ShapeDtypeStruct((n_shard, g[0].shape[0], sum(w.shape[1] for w in g)), g[0].dtype) for g in groups]
    outs.append(jax.ShapeDtypeStruct((n_shard,) + gains.shape, gains.dtype))
    n = len(items)
    dma = pltpu.SemaphoreType.DMA
    hbm = pl.BlockSpec(memory_space=pltpu.HBM)
    got = pl.pallas_call(
        functools.partial(gather_kernel, {"items": items, "n_in": len(ins) + 1, "n_out": len(outs)}),
        name="gather_weights",
        out_shape=tuple(outs),
        in_specs=[hbm] * (len(ins) + 1),
        out_specs=[hbm] * len(outs),
        scratch_shapes=[
            *[pltpu.VMEM(o.shape, o.dtype) for o in outs[:-1]],
            dma((n, 11)), dma((n, 11)), dma((n,)), dma((n, 4)), dma((3,)), dma((3,)), dma,
        ],
        compiler_params=pltpu.CompilerParams(
            collective_id=1, has_side_effects=True, vmem_limit_bytes=65_000_000),
    )(*ins, gains)
    return [g.reshape(-1, g.shape[-1]) for g in got[:-1]], got[-1]


def sum_kernel(cfg, *refs):
    n_left, n_right = cfg["n_left"], cfg["n_right"]
    left_refs, right_refs = refs[:n_left], refs[n_left : n_left + n_right]
    g_ref, refs = refs[n_left + n_right], refs[n_left + n_right + 1 :]
    n_sets = len(cfg["sets"])
    out_refs, gout_ref, scratch = refs[:n_sets], refs[n_sets], refs[n_sets + 1 :]
    n_rep, n_shard, tok = cfg["n_rep"], cfg["n_shard"], cfg["tok"]
    sub, cols, pr, pc = cfg["sub"], cfg["cols"], cfg["pr"], cfg["pc"]
    depth, n_down, n_mid, n_qkv, n_all = (cfg[k] for k in ("depth", "n_down", "n_mid", "n_qkv", "n_all"))
    lsegs, rsegs = cfg["lsegs"], cfg["rsegs"]
    s_bits, r_bits = bit_count(n_shard), bit_count(n_rep)
    n_half = n_shard // 2
    steps = [("shard", i) for i in reversed(range(1, s_bits))] + [("rep", i) for i in range(r_bits)]
    back = [("rep", i) for i in reversed(range(r_bits))]
    turned = list(steps)
    if r_bits >= 2:
        turned = [("rep", 1)] + [st for st in steps if st != ("rep", 1)]
    turned_back = [st for st in reversed(turned) if st[0] == "rep"]
    cycle = cfg["cycle"]
    n_down_steps, n_back = len(steps), len(back)
    ltf, rf, dsend = scratch[:3]
    recv = scratch[3 : 3 + n_down_steps]
    outb, gacc, grecv = scratch[3 + n_down_steps : 6 + n_down_steps]
    (ex_send, ex_recv, ex_own, send_sem, recv_sem, out_sem, g_send, g_recv, g_out) = scratch[6 + n_down_steps :]
    slots = dsend.shape[0]

    me_s, me_r = lax.axis_index("shard"), lax.axis_index("rep")
    core = me_s & 1

    def bit_of(axis, bit):
        return ((me_s if axis == "shard" else me_r) >> bit) & 1

    def peer(axis, bit):
        return {axis: (me_s if axis == "shard" else me_r) ^ (1 << bit)}

    def is_turned(k):
        return k % cycle == cycle // 2

    def bit_at(i, k):
        return jnp.where(is_turned(k), bit_of(*turned[i]), bit_of(*steps[i]))

    def peer_at(first, second, k):
        def moved(axis, me):
            ids = [me ^ (1 << bit) if name == axis else me for name, bit in (first, second)]
            return ids[0] if first == second else jnp.where(is_turned(k), ids[1], ids[0])

        return {"rep": moved("rep", me_r), "shard": moved("shard", me_s)}

    everyone = [("shard", i) for i in range(s_bits)] + [("rep", i) for i in range(r_bits)]
    barrier = pltpu.get_barrier_semaphore()
    for axis, bit in everyone:
        pl.semaphore_signal(barrier, inc=1, device_id=peer(axis, bit), device_id_type=MESH)
    pl.semaphore_wait(barrier, len(everyone))

    def exchange(i):
        made, n = [], 0
        for which, refs_of, span, target in ((0, left_refs, lsegs[i], ltf), (1, right_refs, rsegs[i], rf)):
            at = 0
            for ref in refs_of:
                size = ref.shape[1] // n_shard if which == 0 else ref.shape[1]
                if span[0] <= at < span[1]:
                    for half in range(n_half if which == 0 else 1):
                        def source(c):
                            first = pl.multiple_of((half * 2 + c) * size, size)
                            return ref.at[:, pl.ds(first, size)] if which == 0 else ref

                        def place_at(row):
                            held = target.at[half] if which == 0 else target
                            return held.at[pl.ds(row, tok), pl.ds(at, size)]

                        made.append(pltpu.make_async_remote_copy(
                            src_ref=source(1 - core), dst_ref=place_at(tok),
                            send_sem=ex_send.at[i, n], recv_sem=ex_recv.at[i, n],
                            device_id=peer("shard", 0), device_id_type=MESH))
                        made.append(pltpu.make_async_copy(source(core), place_at(0), ex_own.at[i, n]))
                        n += 1
                at += size
        return made

    for i in range(3):
        for cp in exchange(i):
            cp.start()

    gacc[0] = g_ref[...]

    def gain_copy(i):
        axis, bit = everyone[i]
        return pltpu.make_async_remote_copy(
            src_ref=gacc.at[i], dst_ref=grecv.at[i], send_sem=g_send.at[i], recv_sem=g_recv.at[i],
            device_id=peer(axis, bit), device_id_type=MESH)

    def place(k, j):
        kk = k - n_down
        down = k < n_down
        off = jnp.where(kk < n_mid, lsegs[1][0], jnp.where(kk < n_mid + n_qkv, lsegs[2][0], cfg["lout"]))
        lrow = jnp.where(down, k * sub, off + j * sub)
        rcol = jnp.where(down, j * cols, depth + kk * cols)
        return pl.multiple_of(lrow, sub), pl.multiple_of(rcol, cols)

    def product(blk, k, j):
        lrow, rcol = place(k, j)
        return lax.dot_general(
            ltf[blk, :, pl.ds(lrow, sub)], rf[:, pl.ds(rcol, cols)], (((0,), (0,)), ((), ())),
            preferred_element_type=jnp.float32)

    rows_p, cols_p = sub // pr, cols // pc

    def pieces(j):
        for a in range(rows_p):
            for b in range(cols_p):
                yield (j * rows_p + a) * cols_p + b, a * pr, b * pc

    nb = n_half // 2
    top = bit_of(*steps[0])

    def part_of(i, k, mine):
        if r_bits < 2:
            lead = top if mine else 1 - top
            return product(lead * nb + i // 2, k, i % 2)
        turn, z = is_turned(k), bit_of(*turned[0])
        lead, half = (top, z) if mine else (1 - top, 1 - z)
        return product(jnp.where(turn, i, lead * nb + i // 2), k, jnp.where(turn, half, i % 2))

    def rs_copy(i, k):
        if i == 0:
            src = dsend.at[k % slots]
        else:
            half = recv[i - 1].shape[1] // 2
            src = recv[i - 1].at[k, pl.ds((1 - bit_at(i, k)) * half, half)]
        return pltpu.make_async_remote_copy(
            src_ref=src, dst_ref=recv[i].at[k], send_sem=send_sem.at[i, k], recv_sem=recv_sem.at[i, k],
            device_id=peer_at(steps[i], turned[i], k), device_id_type=MESH)

    def own_start(size, k):
        def start(order):
            at = 0
            for n, (axis, bit) in enumerate(order):
                block = n_rep >> (n + 1)
                if block >= size:
                    at = at + bit_of(axis, bit) * block
            return at

        return jnp.where(is_turned(k), start(turned_back[::-1]), start(back[::-1]))

    def ag_copy(i, k):
        size = 1 << i
        at = pl.ds(own_start(size, k), size)
        n = n_down_steps + i
        return pltpu.make_async_remote_copy(
            src_ref=outb.at[k, at], dst_ref=outb.at[k, at], send_sem=send_sem.at[n, k], recv_sem=recv_sem.at[n, k],
            device_id=peer_at(back[i], turned_back[i], k), device_id_type=MESH)

    def out_copies(n, k):
        lo = cfg["sets"][n][0]
        made = []
        for j in range(2):
            for b in range(cols_p):
                if n == 0:
                    dst = out_refs[n].at[k, :, :, pl.ds(j * cols + b * pc, pc)]
                else:
                    at = pl.multiple_of((k - lo) * cols, cols) + b * pc
                    dst = out_refs[n].at[pl.ds(j * rows_p, rows_p), :, pl.ds(at, pc)]
                if cols_p == 1:
                    made.append((outb.at[k, pl.ds(j * rows_p, rows_p)], dst))
                else:
                    made += [
                        (outb.at[k, (j * rows_p + a) * cols_p + b], dst.at[a]) for a in range(rows_p)]
        return [pltpu.make_async_copy(src, dst, out_sem.at[k, i]) for i, (src, dst) in enumerate(made)]

    def each_set(k, act):
        for n, (lo, hi) in enumerate(cfg["sets"]):
            @pl.when((k >= lo) & (k < hi))
            def _(n=n):
                for cp in out_copies(n, k):
                    act(cp)

    def spread(i):
        for p, a, b in pieces(0):
            yield i * (n_rep // 2) + p, a, b

    def first(k):
        for i in range(n_half):
            part = part_of(i, k, False).astype(jnp.bfloat16)
            for q, a, b in spread(i):
                dsend[k % slots, q] = part[a : a + pr, b : b + pc]

    def join(i, k):
        rs_copy(i, k).wait()
        if i == 0:
            for n in range(n_half):
                part = part_of(n, k, True)
                for q, a, b in spread(n):
                    got = recv[0][k, q].astype(jnp.float32)
                    recv[0][k, q] = (part[a : a + pr, b : b + pc] + got).astype(jnp.bfloat16)
            return
        half = recv[i].shape[1]
        base = bit_at(i, k) * half
        for q in range(half):
            kept = recv[i - 1][k, base + q].astype(jnp.float32)
            both = (kept + recv[i][k, q].astype(jnp.float32)).astype(jnp.bfloat16)
            if i == n_down_steps - 1:
                outb[k, own_start(1, k)] = both
            else:
                recv[i][k, q] = both

    lag = [0, 2]
    for _ in range(n_down_steps - 1 + n_back):
        lag.append(lag[-1] + 2)
    last = lag[-1]

    def during(t, n, do):
        k = t - lag[n]

        @pl.when((k >= 0) & (k < n_all))
        def _():
            do(k)

    def body(t, carry):
        for i, when in ((0, 0), (1, n_down), (2, n_down + n_mid)):
            @pl.when(t == when)
            def _(i=i):
                for n, cp in enumerate(exchange(i)):
                    cp.wait()

        during(t, 0, first)
        for i in range(n_down_steps):
            during(t, 1 + i, functools.partial(join, i))
        for i in range(n_back):
            during(t, 1 + n_down_steps + i, lambda k, i=i: ag_copy(i, k).wait())
        for g in range(len(everyone)):
            @pl.when(t == 3 + 2 * g)
            def _(g=g):
                gain_copy(g).wait()
                gacc[g + 1] = gacc[g] + grecv[g]

        for i in range(n_down_steps):
            during(t, i, lambda k, i=i: rs_copy(i, k).start())
        for i in range(n_back):
            during(t, n_down_steps + i, lambda k, i=i: ag_copy(i, k).start())
        during(t, n_down_steps + n_back, lambda k: each_set(k, lambda cp: cp.start()))
        for g in range(len(everyone)):
            @pl.when(t == 1 + 2 * g)
            def _(g=g):
                gain_copy(g).start()

        return carry

    lax.fori_loop(0, n_all + last, body, 0)
    gout = pltpu.make_async_copy(gacc.at[len(everyone)], gout_ref, g_out)
    gout.start()

    def finish(k, carry):
        each_set(k, lambda cp: cp.wait())
        return carry

    lax.fori_loop(0, n_all, finish, 0)
    gout.wait()


def plain_sums(pairs, gains):
    sums = []
    for left, right in pairs:
        part = lax.dot_general(left, right, (((0,), (0,)), ((), ())), preferred_element_type=jnp.float32)
        part = part.astype(jnp.bfloat16).astype(jnp.float32)
        part = lax.psum_scatter(part, "shard", scatter_dimension=0, tiled=True)
        sums.append(lax.psum(part, "rep"))
    return sums, lax.psum(gains, ("rep", "shard"))


def reduce_grads(hid, h2, h1, ob, dyb, dgate, dup, dqkv, dx2b, gains, n_rep, n_shard):
    tok, ff = hid.shape
    depth = h1.shape[1]
    qkv = dqkv.shape[1]
    n_half = n_shard // 2
    sub = depth // n_shard // 2
    if n_shard < 4 or sub % 128 or ff // n_shard % 128:
        pairs = ((hid, dyb), (h2, dgate), (h2, dup), (h1, dqkv), (ob, dx2b))
        return plain_sums(pairs, gains)
    cols = depth // 2
    pr = max(16, 2 * sub // n_rep)
    pc = cols * (2 * sub // pr) // n_rep
    n_down, n_mid, n_qkv, n_out = ff // cols, 2 * ff // cols, qkv // cols, depth // cols
    n_all = n_down + n_mid + n_qkv + n_out
    fs, ds = ff // n_shard, depth // n_shard
    lefts, rights = (hid, h2, h1, ob), (dyb, dgate, dup, dqkv, dx2b)
    lrows, rcols = sum(v.shape[1] // n_shard for v in lefts), sum(v.shape[1] for v in rights)
    cfg = dict(
        n_rep=n_rep, n_shard=n_shard, tok=tok, sub=sub, cols=cols, pr=pr, pc=pc, depth=depth, n_left=len(lefts), n_right=len(rights),
        cycle=6,
        n_down=n_down, n_mid=n_mid, n_qkv=n_qkv, n_all=n_all, lout=fs + 2 * ds,
        lsegs=((0, fs), (fs, fs + ds), (fs + ds, lrows)),
        rsegs=((0, depth), (depth, depth + 2 * ff), (depth + 2 * ff, rcols)),
    )
    g_rows = gains.shape[0]
    ends = [n_down, n_down + n_mid // 2, n_down + n_mid, n_down + n_mid + n_qkv, n_all]
    cfg["sets"] = tuple(zip([0] + ends[:-1], ends))
    rp, cp = sub // pr, cols // pc
    shapes = [(n_down, rp, pr, depth)] + [(2 * rp, pr, n) for n in (ff, ff, qkv, depth)]
    s_bits, r_bits = bit_count(n_shard), bit_count(n_rep)
    n_hops = s_bits + r_bits
    n_steps = s_bits - 1 + r_bits
    slots = 4
    sizes = [n_half * n_rep >> (i + 1) for i in range(n_steps)]
    bf = jnp.bfloat16
    dma = pltpu.SemaphoreType.DMA
    *outs, gsum = pl.pallas_call(
        functools.partial(sum_kernel, cfg),
        name="sum_grads",
        out_shape=(
            *[jax.ShapeDtypeStruct(shape, bf) for shape in shapes],
            jax.ShapeDtypeStruct((g_rows, 128), jnp.float32),
        ),
        in_specs=[pl.BlockSpec(memory_space=pltpu.VMEM)] * (len(lefts) + len(rights) + 1),
        out_specs=[pl.BlockSpec(memory_space=pltpu.HBM)] * (len(shapes) + 1),
        scratch_shapes=[
            pltpu.VMEM((n_half, 2 * tok, lrows), bf),
            pltpu.VMEM((2 * tok, rcols), bf),
            pltpu.VMEM((slots, sizes[0], pr, pc), bf),
            *[pltpu.VMEM((n_all, size, pr, pc), bf) for size in sizes],
            pltpu.VMEM((n_all, n_rep, pr, pc), bf),
            pltpu.VMEM((n_hops + 1, g_rows, 128), jnp.float32),
            pltpu.VMEM((n_hops, g_rows, 128), jnp.float32),
            *[dma((3, 2 * n_half + 4))] * 3,
            dma((n_steps + r_bits, n_all)), dma((n_steps + r_bits, n_all)), dma((n_all, 2 if cp == 1 else n_rep)),
            dma((n_hops,)), dma((n_hops,)), dma,
        ],
        compiler_params=pltpu.CompilerParams(
            collective_id=0, has_side_effects=True, vmem_limit_bytes=60_000_000),
    )(*lefts, *rights, gains)

    return [v.reshape(-1, v.shape[-1]).astype(jnp.float32) for v in outs], gsum


def local(
    n_rep,
    n_shard,
    tokens,
    cotangent,
    doc_ids,
    w_query,
    w_key,
    w_value,
    w_out,
    w_gate,
    w_up,
    w_down,
    gain_attn,
    gain_ffn,
    gain_query,
    gain_key,
):
    tok_rows, width = tokens.shape
    ff = w_gate.shape[1]
    q_width, k_width = w_query.shape[1], w_key.shape[1]
    head_share = QH // KVH
    score_scale = 1.0 / math.sqrt(HEAD_DIM)
    gains = (gain_attn, gain_ffn, gain_query, gain_key)
    gain_sizes = [g.shape[0] for g in gains]
    gain_ends = [sum(gain_sizes[: i + 1]) for i in range(len(gains))]
    flat_gains = jnp.concatenate(gains)
    n_gain = flat_gains.shape[0]
    flat_gains = jnp.pad(flat_gains, (0, -n_gain % 2048)).reshape(-1, 128)
    (qkv_set, out_set, gate_set, up_set, down_set), all_gains = gather_all(
        [[w_query, w_key, w_value], [w_out], [w_gate], [w_up], [w_down]], flat_gains, n_rep, n_shard
    )
    all_gains = all_gains.reshape(n_shard, -1)
    full_gattn, full_gffn, full_gquery, full_gkey = (
        all_gains[:, end - size : end].reshape(-1) for size, end in zip(gain_sizes, gain_ends)
    )

    doc_rows = doc_ids[None, :]
    allowed, positions = doc_tables(doc_rows)
    key_mask = allowed[:, None, None]
    cos_tab, sin_tab = rope_tables(positions, HEAD_DIM)
    resid_in = tokens.astype(jnp.float32)
    normed_in, unit_in, rms_in = norm_rows(resid_in, full_gattn)
    normed_bf = normed_in.astype(jnp.bfloat16)
    qkv = matmul(normed_bf, qkv_set)
    query_raw = qkv[:, :q_width].reshape(1, tok_rows, QH, HEAD_DIM)
    key_raw = qkv[:, q_width : q_width + k_width].reshape(1, tok_rows, KVH, HEAD_DIM)
    value_bf = qkv[:, q_width + k_width :].astype(jnp.bfloat16).reshape(1, tok_rows, KVH, HEAD_DIM)
    query_normed, query_unit, query_rms = norm_rows(query_raw, full_gquery)
    key_normed, key_unit, key_rms = norm_rows(key_raw, full_gkey)
    query_bf = (
        rotate(query_normed, cos_tab, sin_tab)
        .astype(jnp.bfloat16)
        .reshape(1, tok_rows, KVH, head_share, HEAD_DIM)
    )
    key_bf = rotate(key_normed, cos_tab, sin_tab).astype(jnp.bfloat16)
    attn_probs, log_total = attn_probs_of(query_bf, key_bf, key_mask, None, score_scale)
    probs_bf = attn_probs.astype(jnp.bfloat16)
    mixed_bf = (
        jnp.einsum("gkrqs,gskd->gqkrd", probs_bf, value_bf, preferred_element_type=jnp.float32)
        .astype(jnp.bfloat16)
        .reshape(tok_rows, QH * HEAD_DIM)
    )
    resid_mid = resid_in + matmul(mixed_bf, out_set)
    normed_mid, unit_mid, rms_mid = norm_rows(resid_mid, full_gffn)
    hidden_in = normed_mid.astype(jnp.bfloat16)
    gate_proj = matmul(hidden_in, gate_set)
    up_proj = matmul(hidden_in, up_set)
    gate_sig = jax.nn.sigmoid(gate_proj)
    gate_act = gate_proj * gate_sig
    hidden_bf = (gate_act * up_proj).astype(jnp.bfloat16)

    live_rows = (doc_ids >= 0).astype(jnp.float32)[:, None]
    grad_y = cotangent.astype(jnp.float32) * live_rows
    grad_y_bf = grad_y.astype(jnp.bfloat16)
    block_out = (resid_mid + matmul(hidden_bf, down_set)).astype(jnp.bfloat16)

    grad_hidden = matmul_t(grad_y_bf, down_set)
    grad_gate_bf = (grad_hidden * up_proj * gate_sig * (1.0 + gate_proj * (1.0 - gate_sig))).astype(
        jnp.bfloat16
    )
    grad_up_bf = (grad_hidden * gate_act).astype(jnp.bfloat16)
    grad_norm_mid = matmul_t(grad_gate_bf, gate_set) + matmul_t(grad_up_bf, up_set)
    back_mid, part_gffn = norm_back(grad_norm_mid, unit_mid, rms_mid, full_gffn)
    grad_mid = grad_y + back_mid
    grad_mid_bf = grad_mid.astype(jnp.bfloat16)
    grad_mixed_bf = (
        matmul_t(grad_mid_bf, out_set)
        .astype(jnp.bfloat16)
        .reshape(1, tok_rows, KVH, head_share, HEAD_DIM)
    )
    grad_scores = jnp.einsum(
        "gqkrd,gskd->gkrqs", grad_mixed_bf, value_bf, preferred_element_type=jnp.float32
    )
    grad_value_bf = (
        jnp.einsum("gkrqs,gqkrd->gskd", probs_bf, grad_mixed_bf, preferred_element_type=jnp.float32)
        .astype(jnp.bfloat16)
        .reshape(tok_rows, KVH * HEAD_DIM)
    )
    row_dot = jnp.sum(attn_probs * grad_scores, axis=-1, keepdims=True)
    grad_logits = (attn_probs * (grad_scores - row_dot) * score_scale).astype(jnp.bfloat16)
    grad_query_rot = jnp.einsum(
        "gkrqs,gskd->gqkrd", grad_logits, key_bf, preferred_element_type=jnp.float32
    ).reshape(1, tok_rows, QH, HEAD_DIM)
    grad_key_rot = jnp.einsum(
        "gkrqs,gqkrd->gskd", grad_logits, query_bf, preferred_element_type=jnp.float32
    )
    grad_query_raw, part_gquery = norm_back(
        rotate_back(grad_query_rot, cos_tab, sin_tab), query_unit, query_rms, full_gquery
    )
    grad_key_raw, part_gkey = norm_back(
        rotate_back(grad_key_rot, cos_tab, sin_tab), key_unit, key_rms, full_gkey
    )
    grad_query_bf = grad_query_raw.astype(jnp.bfloat16).reshape(tok_rows, QH * HEAD_DIM)
    grad_key_bf = grad_key_raw.astype(jnp.bfloat16).reshape(tok_rows, KVH * HEAD_DIM)
    grad_qkv_bf = jnp.concatenate([grad_query_bf, grad_key_bf, grad_value_bf], axis=1)
    grad_norm_in = matmul_t(grad_qkv_bf, qkv_set)
    back_in, part_gattn = norm_back(grad_norm_in, unit_in, rms_in, full_gattn)
    grad_tokens = grad_mid + back_in
    part_gains = jnp.concatenate(
        [
            p.reshape(n_shard, -1)
            for p in (part_gattn, part_gffn, part_gquery, part_gkey)
        ],
        axis=1,
    )
    part_gains = part_gains.astype(jnp.bfloat16).astype(jnp.float32)
    flat = part_gains.reshape(-1)
    flat = jnp.pad(flat, (0, -flat.shape[0] % 1024)).reshape(-1, 128)
    (grad_down, grad_gate, grad_up, grad_qkv, grad_out), sum_gains = reduce_grads(
        hidden_bf, hidden_in, normed_bf, mixed_bf,
        grad_y_bf, grad_gate_bf, grad_up_bf, grad_qkv_bf, grad_mid_bf,
        flat, n_rep, n_shard,
    )
    ends = [q_width, q_width + k_width]
    grad_query, grad_key, grad_value = jnp.split(grad_qkv, ends, axis=1)
    sum_gains = sum_gains.reshape(-1)[: part_gains.size].reshape(part_gains.shape)
    own_gains = lax.dynamic_index_in_dim(sum_gains, lax.axis_index("shard"), axis=0, keepdims=False)
    grad_gattn, grad_gffn, grad_gquery, grad_gkey = (
        own_gains[end - size : end] for size, end in zip(gain_sizes, gain_ends)
    )
    return (
        block_out,
        grad_tokens,
        grad_query,
        grad_key,
        grad_value,
        grad_out,
        grad_gate,
        grad_up,
        grad_down,
        grad_gattn,
        grad_gffn,
        grad_gquery,
        grad_gkey,
    )


def solution(mesh):
    return jax.shard_map(
        functools.partial(local, mesh.shape["rep"], mesh.shape["shard"]),
        mesh=mesh,
        in_specs=(
            P(("rep", "shard"), None),
            P(("rep", "shard"), None),
            P(("rep", "shard")),
            P("shard", None),
            P("shard", None),
            P("shard", None),
            P("shard", None),
            P("shard", None),
            P("shard", None),
            P("shard", None),
            P("shard"),
            P("shard"),
            P("shard"),
            P("shard"),
        ),
        out_specs=(
            P(("rep", "shard"), None),
            P(("rep", "shard"), None),
            P("shard", None),
            P("shard", None),
            P("shard", None),
            P("shard", None),
            P("shard", None),
            P("shard", None),
            P("shard", None),
            P("shard"),
            P("shard"),
            P("shard"),
            P("shard"),
        ),
        check_vma=False,
    )
```

```python
import functools
import math

import jax
import jax.numpy as jnp
from jax import lax
from jax.experimental import pallas as pl
from jax.experimental.pallas import tpu as pltpu
from jax.sharding import PartitionSpec as P

MESH = pl.DeviceIdType.MESH

QH = 16
KVH = 8
HEAD_DIM = 64


NORM_EPSILON = 1e-05
ROPE_BASE = 1000000.0


def matmul(left, right):
    return jnp.dot(left, right, preferred_element_type=jnp.float32)


def matmul_t(left, right):
    return lax.dot_general(left, right, (((1,), (1,)), ((), ())), preferred_element_type=jnp.float32)


def norm_rows(values, gain_vec):
    inv_rms = lax.rsqrt(jnp.mean(values * values, axis=-1, keepdims=True) + NORM_EPSILON)
    normed = values * inv_rms
    return (normed * gain_vec.astype(jnp.float32), normed, inv_rms)


def norm_back(grad_out, normed, inv_rms, gain_vec):
    scaled = grad_out * gain_vec.astype(jnp.float32)
    grad_in = inv_rms * (scaled - normed * jnp.mean(scaled * normed, axis=-1, keepdims=True))
    lead_axes = tuple(range(grad_out.ndim - 1))
    return (grad_in, jnp.sum(grad_out * normed, axis=lead_axes))


def doc_tables(doc_rows):
    block_len = doc_rows.shape[-1]
    row_index = jnp.arange(block_len)[:, None]
    col_index = jnp.arange(block_len)[None, :]
    same_doc = doc_rows[:, :, None] == doc_rows[:, None, :]
    allowed = same_doc & (row_index >= col_index)[None]
    earlier = same_doc & (row_index > col_index)[None]
    positions = jnp.sum(earlier.astype(jnp.int32), axis=2)
    return (allowed, positions)


def rope_tables(positions, head_dim):
    half_dim = head_dim // 2
    inv_freq = jnp.exp(
        jnp.arange(half_dim).astype(jnp.float32) * (-2.0 * math.log(ROPE_BASE) / head_dim)
    )
    angles = positions.astype(jnp.float32)[:, :, None, None] * inv_freq
    return (jnp.cos(angles), jnp.sin(angles))


def rotate(values, cos_tab, sin_tab):
    half_dim = values.shape[-1] // 2
    part_one = values[..., :half_dim]
    part_two = values[..., half_dim:]
    return jnp.concatenate(
        [part_one * cos_tab - part_two * sin_tab, part_two * cos_tab + part_one * sin_tab], axis=-1
    )


def rotate_back(values, cos_tab, sin_tab):
    half_dim = values.shape[-1] // 2
    part_one = values[..., :half_dim]
    part_two = values[..., half_dim:]
    return jnp.concatenate(
        [part_one * cos_tab + part_two * sin_tab, part_two * cos_tab - part_one * sin_tab], axis=-1
    )


def bit_count(size):
    return size.bit_length() - 1


def gather_kernel(cfg, *refs):
    items, n_in, n_out = cfg["items"], cfg["n_in"], cfg["n_out"]
    ins, outs = refs[:n_in], refs[n_in : n_in + n_out]
    gain_in, gain_out = ins[-1], outs[-1]
    held = refs[n_in + n_out : n_in + 2 * n_out - 1]
    send_sem, recv_sem, own_sem, out_sem, gs_sem, gr_sem, go_sem = refs[n_in + 2 * n_out - 1 :]
    me_s, me_r = lax.axis_index("shard"), lax.axis_index("rep")
    core, y, z = me_s & 1, me_r & 1, (me_r >> 1) & 1
    peers = [{"shard": me_s ^ 1}, {"shard": me_s ^ 2}, {"rep": me_r ^ 1}, {"rep": me_r ^ 2}]
    to_core, to_x, to_y, to_z = peers
    barrier = pltpu.get_barrier_semaphore()
    for p in peers:
        pl.semaphore_signal(barrier, inc=1, device_id=p, device_id_type=MESH)
    pl.semaphore_wait(barrier, len(peers))

    other = me_s ^ 2
    mine = z * 2 + y
    from_y, from_z, diag = mine ^ 1, mine ^ 2, mine ^ 3

    def place(n, shard, row, size):
        it = items[n]
        return held[it["out"]].at[shard, pl.ds(it["row"] + row, size), pl.ds(it["dst"], it["cols"])]

    def result(n, shard, row, size):
        it = items[n]
        return outs[it["out"]].at[shard, pl.ds(it["row"] + row, size), pl.ds(it["dst"], it["cols"])]

    def fresh(n, row, size):
        it = items[n]
        return ins[it["in"]].at[pl.ds(it["row"] + row, size), pl.ds(it["src"], it["cols"])]

    def send(n, i, src, dst, to):
        return pltpu.make_async_remote_copy(
            src_ref=src, dst_ref=dst, send_sem=send_sem.at[n, i], recv_sem=recv_sem.at[n, i],
            device_id=to, device_id_type=MESH)

    def relay(n, i, row, size, to):
        ref = place(n, other, row, size)
        return send(n, i, ref, ref, to)

    def copies(n):
        it = items[n]
        rows, quarter = it["rows"], it["rows"] // 4
        dx, dy, dz = it["parts"]
        at = lambda q: pl.multiple_of(q * quarter, quarter)
        whole = lambda i, row, size, to: send(
            n, i, place(n, me_s, row, size), place(n, me_s, row, size), to)
        return dict(
            x=whole(0, at(mine), quarter, to_x),
            xd=whole(1, at(diag), dx, to_x),
            own=whole(2, 0, rows, to_core),
            y=relay(n, 3, at(mine), quarter, to_y),
            z=relay(n, 4, at(mine), quarter, to_z),
            c0=relay(n, 5, at(mine), quarter, to_core),
            fz=relay(n, 6, at(from_y) + dx + dy, dz, to_z),
            c1=relay(n, 7, at(from_y), quarter, to_core),
            fy=relay(n, 8, at(from_z) + dx, dy, to_y),
            c2=relay(n, 9, at(from_z), quarter, to_core),
            c3=relay(n, 10, at(diag), quarter, to_core),
            out=[
                pltpu.make_async_copy(
                    place(n, me_s ^ d, 0, rows), result(n, me_s ^ d, 0, rows), out_sem.at[n, d])
                for d in range(4)],
            keep=pltpu.make_async_copy(fresh(n, 0, rows), place(n, me_s, 0, rows), own_sem.at[n]),
        )

    gain_send = lambda i, shard, src, to: pltpu.make_async_remote_copy(
        src_ref=src, dst_ref=gain_out.at[shard], send_sem=gs_sem.at[i], recv_sem=gr_sem.at[i],
        device_id=to, device_id_type=MESH)
    gains = [
        gain_send(0, me_s, gain_in, to_x),
        gain_send(1, me_s, gain_in, to_core),
        gain_send(2, other, gain_out.at[other], to_core),
    ]
    gain_keep = pltpu.make_async_copy(gain_in, gain_out.at[me_s], go_sem)
    gain_keep.start()
    gains[0].start()
    gains[1].start()
    todo = [copies(n) for n in range(len(items))]
    for c in todo:
        c["keep"].start()
    for c in todo:
        c["keep"].wait()
        for k in ("x", "xd", "own"):
            c[k].start()
        c["out"][0].start()
    gains[0].wait_recv()
    gains[2].start()

    def near(c):
        c["x"].wait_recv()
        for k in ("y", "z", "c0"):
            c[k].start()

    def far(c):
        c["y"].wait_recv()
        c["fz"].start()
        c["c1"].start()
        c["z"].wait_recv()
        c["fy"].start()
        c["c2"].start()

    def end(c):
        for k in ("xd", "fy", "fz"):
            c[k].wait_recv()
        c["c3"].start()
        c["out"][2].start()
        c["own"].wait_recv()
        c["out"][1].start()

    def pair(c):
        for k in ("c0", "c1", "c2", "c3"):
            c[k].wait_recv()
        c["out"][3].start()

    count = len(todo)
    for t in range(count + 3):
        if t < count:
            near(todo[t])
        if 0 <= t - 1 < count:
            far(todo[t - 1])
        if 0 <= t - 2 < count:
            end(todo[t - 2])
        if 0 <= t - 3 < count:
            pair(todo[t - 3])
    for c in todo:
        for k in ("x", "xd", "own", "y", "z", "c0", "fz", "c1", "fy", "c2", "c3"):
            c[k].wait_send()
        for cp in c["out"]:
            cp.wait()
    gains[1].wait_recv()
    gains[2].wait_recv()
    for g in gains:
        g.wait_send()
    gain_keep.wait()


def gather_all(groups, gains, n_rep, n_shard):
    tile = 16
    fits = n_shard == 4 and n_rep >= 4 and all(w.shape[0] % (4 * tile) == 0 for g in groups for w in g)
    if not fits:
        full = [lax.all_gather(jnp.concatenate(g, axis=1), "shard", axis=0, tiled=True) for g in groups]
        return full, lax.all_gather(gains, "shard", axis=0)
    items, ins = [], []
    for o, group in enumerate(groups):
        dst = 0
        for w in group:
            rows, cols = w.shape
            big = w.size > 2 * 256 * 1024
            row_cut = 3 if big and rows > cols and rows % (12 * tile) == 0 else 1
            col_cut = 3 if big and row_cut == 1 and cols % 384 == 0 else 1
            step, width = rows // row_cut, cols // col_cut
            for a in range(row_cut):
                for b in range(col_cut):
                    units = step // 4 // tile
                    third = units // 3
                    rest = units - 3 * third
                    turn = len(items) % 2
                    parts = [third, third + (rest > turn), third + (rest > 1 - turn)]
                    parts[0] = units - parts[1] - parts[2]
                    items.append({
                        "in": len(ins), "out": o, "row": a * step, "rows": step, "src": b * width,
                        "dst": dst + b * width, "cols": width, "parts": tuple(p * tile for p in parts)})
            ins.append(w)
            dst += cols
    outs = [
        jax.ShapeDtypeStruct((n_shard, g[0].shape[0], sum(w.shape[1] for w in g)), g[0].dtype) for g in groups]
    outs.append(jax.ShapeDtypeStruct((n_shard,) + gains.shape, gains.dtype))
    n = len(items)
    dma = pltpu.SemaphoreType.DMA
    hbm = pl.BlockSpec(memory_space=pltpu.HBM)
    got = pl.pallas_call(
        functools.partial(gather_kernel, {"items": items, "n_in": len(ins) + 1, "n_out": len(outs)}),
        name="gather_weights",
        out_shape=tuple(outs),
        in_specs=[hbm] * (len(ins) + 1),
        out_specs=[hbm] * len(outs),
        scratch_shapes=[
            *[pltpu.VMEM(o.shape, o.dtype) for o in outs[:-1]],
            dma((n, 11)), dma((n, 11)), dma((n,)), dma((n, 4)), dma((3,)), dma((3,)), dma,
        ],
        compiler_params=pltpu.CompilerParams(
            collective_id=1, has_side_effects=True, vmem_limit_bytes=65_000_000),
    )(*ins, gains)
    return [g.reshape(-1, g.shape[-1]) for g in got[:-1]], got[-1]


def sum_kernel(cfg, *refs):
    n_left, n_right = cfg["n_left"], cfg["n_right"]
    left_refs, right_refs = refs[:n_left], refs[n_left : n_left + n_right]
    g_ref, refs = refs[n_left + n_right], refs[n_left + n_right + 1 :]
    n_sets = len(cfg["sets"])
    out_refs, gout_ref, scratch = refs[:n_sets], refs[n_sets], refs[n_sets + 1 :]
    n_rep, n_shard, tok = cfg["n_rep"], cfg["n_shard"], cfg["tok"]
    sub, cols, pr, pc = cfg["sub"], cfg["cols"], cfg["pr"], cfg["pc"]
    depth, n_down, n_mid, n_qkv, n_all = (cfg[k] for k in ("depth", "n_down", "n_mid", "n_qkv", "n_all"))
    lsegs, rsegs = cfg["lsegs"], cfg["rsegs"]
    s_bits, r_bits = bit_count(n_shard), bit_count(n_rep)
    n_half = n_shard // 2
    steps = [("shard", i) for i in reversed(range(1, s_bits))] + [("rep", i) for i in range(r_bits)]
    back = [("rep", i) for i in reversed(range(r_bits))]
    turned = list(steps)
    if r_bits >= 2:
        turned = [("rep", 1)] + [st for st in steps if st != ("rep", 1)]
    turned_back = [st for st in reversed(turned) if st[0] == "rep"]
    cycle = cfg["cycle"]
    n_down_steps, n_back = len(steps), len(back)
    ltf, rf, dsend = scratch[:3]
    recv = scratch[3 : 3 + n_down_steps]
    outb, gacc, grecv = scratch[3 + n_down_steps : 6 + n_down_steps]
    (ex_send, ex_recv, ex_own, send_sem, recv_sem, out_sem, g_send, g_recv, g_out) = scratch[6 + n_down_steps :]
    slots = dsend.shape[0]

    me_s, me_r = lax.axis_index("shard"), lax.axis_index("rep")
    core = me_s & 1

    def bit_of(axis, bit):
        return ((me_s if axis == "shard" else me_r) >> bit) & 1

    def peer(axis, bit):
        return {axis: (me_s if axis == "shard" else me_r) ^ (1 << bit)}

    def is_turned(k):
        return k % cycle == cycle // 2

    def bit_at(i, k):
        return jnp.where(is_turned(k), bit_of(*turned[i]), bit_of(*steps[i]))

    def peer_at(first, second, k):
        def moved(axis, me):
            ids = [me ^ (1 << bit) if name == axis else me for name, bit in (first, second)]
            return ids[0] if first == second else jnp.where(is_turned(k), ids[1], ids[0])

        return {"rep": moved("rep", me_r), "shard": moved("shard", me_s)}

    everyone = [("shard", i) for i in range(s_bits)] + [("rep", i) for i in range(r_bits)]
    barrier = pltpu.get_barrier_semaphore()
    for axis, bit in everyone:
        pl.semaphore_signal(barrier, inc=1, device_id=peer(axis, bit), device_id_type=MESH)
    pl.semaphore_wait(barrier, len(everyone))

    def exchange(i):
        made, n = [], 0
        for which, refs_of, span, target in ((0, left_refs, lsegs[i], ltf), (1, right_refs, rsegs[i], rf)):
            at = 0
            for ref in refs_of:
                size = ref.shape[1] // n_shard if which == 0 else ref.shape[1]
                if span[0] <= at < span[1]:
                    for half in range(n_half if which == 0 else 1):
                        def source(c):
                            first = pl.multiple_of((half * 2 + c) * size, size)
                            return ref.at[:, pl.ds(first, size)] if which == 0 else ref

                        def place_at(row):
                            held = target.at[half] if which == 0 else target
                            return held.at[pl.ds(row, tok), pl.ds(at, size)]

                        made.append(pltpu.make_async_remote_copy(
                            src_ref=source(1 - core), dst_ref=place_at(tok),
                            send_sem=ex_send.at[i, n], recv_sem=ex_recv.at[i, n],
                            device_id=peer("shard", 0), device_id_type=MESH))
                        made.append(pltpu.make_async_copy(source(core), place_at(0), ex_own.at[i, n]))
                        n += 1
                at += size
        return made

    for i in range(3):
        for cp in exchange(i):
            cp.start()

    gacc[0] = g_ref[...]

    def gain_copy(i):
        axis, bit = everyone[i]
        return pltpu.make_async_remote_copy(
            src_ref=gacc.at[i], dst_ref=grecv.at[i], send_sem=g_send.at[i], recv_sem=g_recv.at[i],
            device_id=peer(axis, bit), device_id_type=MESH)

    def place(k, j):
        kk = k - n_down
        down = k < n_down
        off = jnp.where(kk < n_mid, lsegs[1][0], jnp.where(kk < n_mid + n_qkv, lsegs[2][0], cfg["lout"]))
        lrow = jnp.where(down, k * sub, off + j * sub)
        rcol = jnp.where(down, j * cols, depth + kk * cols)
        return pl.multiple_of(lrow, sub), pl.multiple_of(rcol, cols)

    def product(blk, k, j):
        lrow, rcol = place(k, j)
        return lax.dot_general(
            ltf[blk, :, pl.ds(lrow, sub)], rf[:, pl.ds(rcol, cols)], (((0,), (0,)), ((), ())),
            preferred_element_type=jnp.float32)

    rows_p, cols_p = sub // pr, cols // pc

    def pieces(j):
        for a in range(rows_p):
            for b in range(cols_p):
                yield (j * rows_p + a) * cols_p + b, a * pr, b * pc

    nb = n_half // 2
    top = bit_of(*steps[0])

    def part_of(i, k, mine):
        if r_bits < 2:
            lead = top if mine else 1 - top
            return product(lead * nb + i // 2, k, i % 2)
        turn, z = is_turned(k), bit_of(*turned[0])
        lead, half = (top, z) if mine else (1 - top, 1 - z)
        return product(jnp.where(turn, i, lead * nb + i // 2), k, jnp.where(turn, half, i % 2))

    def rs_copy(i, k):
        if i == 0:
            src = dsend.at[k % slots]
        else:
            half = recv[i - 1].shape[1] // 2
            src = recv[i - 1].at[k, pl.ds((1 - bit_at(i, k)) * half, half)]
        return pltpu.make_async_remote_copy(
            src_ref=src, dst_ref=recv[i].at[k], send_sem=send_sem.at[i, k], recv_sem=recv_sem.at[i, k],
            device_id=peer_at(steps[i], turned[i], k), device_id_type=MESH)

    def own_start(size, k):
        def start(order):
            at = 0
            for n, (axis, bit) in enumerate(order):
                block = n_rep >> (n + 1)
                if block >= size:
                    at = at + bit_of(axis, bit) * block
            return at

        return jnp.where(is_turned(k), start(turned_back[::-1]), start(back[::-1]))

    def ag_copy(i, k):
        size = 1 << i
        at = pl.ds(own_start(size, k), size)
        n = n_down_steps + i
        return pltpu.make_async_remote_copy(
            src_ref=outb.at[k, at], dst_ref=outb.at[k, at], send_sem=send_sem.at[n, k], recv_sem=recv_sem.at[n, k],
            device_id=peer_at(back[i], turned_back[i], k), device_id_type=MESH)

    def out_copies(n, k):
        lo = cfg["sets"][n][0]
        made = []
        for j in range(2):
            for b in range(cols_p):
                if n == 0:
                    dst = out_refs[n].at[k, :, :, pl.ds(j * cols + b * pc, pc)]
                else:
                    at = pl.multiple_of((k - lo) * cols, cols) + b * pc
                    dst = out_refs[n].at[pl.ds(j * rows_p, rows_p), :, pl.ds(at, pc)]
                if cols_p == 1:
                    made.append((outb.at[k, pl.ds(j * rows_p, rows_p)], dst))
                else:
                    made += [
                        (outb.at[k, (j * rows_p + a) * cols_p + b], dst.at[a]) for a in range(rows_p)]
        return [pltpu.make_async_copy(src, dst, out_sem.at[k, i]) for i, (src, dst) in enumerate(made)]

    def each_set(k, act):
        for n, (lo, hi) in enumerate(cfg["sets"]):
            @pl.when((k >= lo) & (k < hi))
            def _(n=n):
                for cp in out_copies(n, k):
                    act(cp)

    def spread(i):
        for p, a, b in pieces(0):
            yield i * (n_rep // 2) + p, a, b

    def first(k):
        for i in range(n_half):
            part = part_of(i, k, False).astype(jnp.bfloat16)
            for q, a, b in spread(i):
                dsend[k % slots, q] = part[a : a + pr, b : b + pc]

    def join(i, k):
        rs_copy(i, k).wait()
        if i == 0:
            for n in range(n_half):
                part = part_of(n, k, True)
                for q, a, b in spread(n):
                    got = recv[0][k, q].astype(jnp.float32)
                    recv[0][k, q] = (part[a : a + pr, b : b + pc] + got).astype(jnp.bfloat16)
            return
        half = recv[i].shape[1]
        base = bit_at(i, k) * half
        for q in range(half):
            kept = recv[i - 1][k, base + q].astype(jnp.float32)
            both = (kept + recv[i][k, q].astype(jnp.float32)).astype(jnp.bfloat16)
            if i == n_down_steps - 1:
                outb[k, own_start(1, k)] = both
            else:
                recv[i][k, q] = both

    lag = [0, 2]
    for _ in range(n_down_steps - 1 + n_back):
        lag.append(lag[-1] + 2)
    last = lag[-1]

    def during(t, n, do):
        k = t - lag[n]

        @pl.when((k >= 0) & (k < n_all))
        def _():
            do(k)

    def body(t, carry):
        for i, when in ((0, 0), (1, n_down), (2, n_down + n_mid)):
            @pl.when(t == when)
            def _(i=i):
                for n, cp in enumerate(exchange(i)):
                    cp.wait()

        during(t, 0, first)
        for i in range(n_down_steps):
            during(t, 1 + i, functools.partial(join, i))
        for i in range(n_back):
            during(t, 1 + n_down_steps + i, lambda k, i=i: ag_copy(i, k).wait())
        for g in range(len(everyone)):
            @pl.when(t == 3 + 2 * g)
            def _(g=g):
                gain_copy(g).wait()
                gacc[g + 1] = gacc[g] + grecv[g]

        for i in range(n_down_steps):
            during(t, i, lambda k, i=i: rs_copy(i, k).start())
        for i in range(n_back):
            during(t, n_down_steps + i, lambda k, i=i: ag_copy(i, k).start())
        during(t, n_down_steps + n_back, lambda k: each_set(k, lambda cp: cp.start()))
        for g in range(len(everyone)):
            @pl.when(t == 1 + 2 * g)
            def _(g=g):
                gain_copy(g).start()

        return carry

    lax.fori_loop(0, n_all + last, body, 0)
    gout = pltpu.make_async_copy(gacc.at[len(everyone)], gout_ref, g_out)
    gout.start()

    def finish(k, carry):
        each_set(k, lambda cp: cp.wait())
        return carry

    lax.fori_loop(0, n_all, finish, 0)
    gout.wait()


def plain_sums(pairs, gains):
    sums = []
    for left, right in pairs:
        part = lax.dot_general(left, right, (((0,), (0,)), ((), ())), preferred_element_type=jnp.float32)
        part = part.astype(jnp.bfloat16).astype(jnp.float32)
        part = lax.psum_scatter(part, "shard", scatter_dimension=0, tiled=True)
        sums.append(lax.psum(part, "rep"))
    return sums, lax.psum(gains, ("rep", "shard"))


def reduce_grads(hid, h2, h1, ob, dyb, dgate, dup, dqkv, dx2b, gains, n_rep, n_shard):
    tok, ff = hid.shape
    depth = h1.shape[1]
    qkv = dqkv.shape[1]
    n_half = n_shard // 2
    sub = depth // n_shard // 2
    if n_shard < 4 or sub % 128 or ff // n_shard % 128:
        pairs = ((hid, dyb), (h2, dgate), (h2, dup), (h1, dqkv), (ob, dx2b))
        return plain_sums(pairs, gains)
    cols = depth // 2
    pr = max(16, 2 * sub // n_rep)
    pc = cols * (2 * sub // pr) // n_rep
    n_down, n_mid, n_qkv, n_out = ff // cols, 2 * ff // cols, qkv // cols, depth // cols
    n_all = n_down + n_mid + n_qkv + n_out
    fs, ds = ff // n_shard, depth // n_shard
    lefts, rights = (hid, h2, h1, ob), (dyb, dgate, dup, dqkv, dx2b)
    lrows, rcols = sum(v.shape[1] // n_shard for v in lefts), sum(v.shape[1] for v in rights)
    cfg = dict(
        n_rep=n_rep, n_shard=n_shard, tok=tok, sub=sub, cols=cols, pr=pr, pc=pc, depth=depth, n_left=len(lefts), n_right=len(rights),
        cycle=6,
        n_down=n_down, n_mid=n_mid, n_qkv=n_qkv, n_all=n_all, lout=fs + 2 * ds,
        lsegs=((0, fs), (fs, fs + ds), (fs + ds, lrows)),
        rsegs=((0, depth), (depth, depth + 2 * ff), (depth + 2 * ff, rcols)),
    )
    g_rows = gains.shape[0]
    ends = [n_down, n_down + n_mid // 2, n_down + n_mid, n_down + n_mid + n_qkv, n_all]
    cfg["sets"] = tuple(zip([0] + ends[:-1], ends))
    rp, cp = sub // pr, cols // pc
    shapes = [(n_down, rp, pr, depth)] + [(2 * rp, pr, n) for n in (ff, ff, qkv, depth)]
    s_bits, r_bits = bit_count(n_shard), bit_count(n_rep)
    n_hops = s_bits + r_bits
    n_steps = s_bits - 1 + r_bits
    slots = 4
    sizes = [n_half * n_rep >> (i + 1) for i in range(n_steps)]
    bf = jnp.bfloat16
    dma = pltpu.SemaphoreType.DMA
    *outs, gsum = pl.pallas_call(
        functools.partial(sum_kernel, cfg),
        name="sum_grads",
        out_shape=(
            *[jax.ShapeDtypeStruct(shape, bf) for shape in shapes],
            jax.ShapeDtypeStruct((g_rows, 128), jnp.float32),
        ),
        in_specs=[pl.BlockSpec(memory_space=pltpu.VMEM)] * (len(lefts) + len(rights) + 1),
        out_specs=[pl.BlockSpec(memory_space=pltpu.HBM)] * (len(shapes) + 1),
        scratch_shapes=[
            pltpu.VMEM((n_half, 2 * tok, lrows), bf),
            pltpu.VMEM((2 * tok, rcols), bf),
            pltpu.VMEM((slots, sizes[0], pr, pc), bf),
            *[pltpu.VMEM((n_all, size, pr, pc), bf) for size in sizes],
            pltpu.VMEM((n_all, n_rep, pr, pc), bf),
            pltpu.VMEM((n_hops + 1, g_rows, 128), jnp.float32),
            pltpu.VMEM((n_hops, g_rows, 128), jnp.float32),
            *[dma((3, 2 * n_half + 4))] * 3,
            dma((n_steps + r_bits, n_all)), dma((n_steps + r_bits, n_all)), dma((n_all, 2 if cp == 1 else n_rep)),
            dma((n_hops,)), dma((n_hops,)), dma,
        ],
        compiler_params=pltpu.CompilerParams(
            collective_id=0, has_side_effects=True, vmem_limit_bytes=60_000_000),
    )(*lefts, *rights, gains)

    return [v.reshape(-1, v.shape[-1]).astype(jnp.float32) for v in outs], gsum


def local(
    n_rep,
    n_shard,
    tokens,
    cotangent,
    doc_ids,
    w_query,
    w_key,
    w_value,
    w_out,
    w_gate,
    w_up,
    w_down,
    gain_attn,
    gain_ffn,
    gain_query,
    gain_key,
):
    tok_rows, width = tokens.shape
    ff = w_gate.shape[1]
    q_width, k_width = w_query.shape[1], w_key.shape[1]
    head_share = QH // KVH
    score_scale = 1.0 / math.sqrt(HEAD_DIM)
    gains = (gain_attn, gain_ffn, gain_query, gain_key)
    gain_sizes = [g.shape[0] for g in gains]
    gain_ends = [sum(gain_sizes[: i + 1]) for i in range(len(gains))]
    flat_gains = jnp.concatenate(gains)
    n_gain = flat_gains.shape[0]
    flat_gains = jnp.pad(flat_gains, (0, -n_gain % 2048)).reshape(-1, 128)
    (qkv_set, out_set, gate_set, up_set, down_set), all_gains = gather_all(
        [[w_query, w_key, w_value], [w_out], [w_gate], [w_up], [w_down]], flat_gains, n_rep, n_shard
    )
    all_gains = all_gains.reshape(n_shard, -1)
    full_gattn, full_gffn, full_gquery, full_gkey = (
        all_gains[:, end - size : end].reshape(-1) for size, end in zip(gain_sizes, gain_ends)
    )

    doc_rows = doc_ids[None, :]
    allowed, positions = doc_tables(doc_rows)
    key_mask = allowed
    cos_tab, sin_tab = (t.reshape(1, tok_rows, -1) for t in rope_tables(positions, HEAD_DIM))

    def by_head(values):
        return values.reshape(tok_rows, -1, HEAD_DIM).transpose(1, 0, 2)

    def by_token(values):
        return values.transpose(1, 0, 2).reshape(tok_rows, -1)

    def batched(spec, left, right):
        return jnp.einsum(spec, left, right, preferred_element_type=jnp.float32)

    resid_in = tokens.astype(jnp.float32)
    normed_in, unit_in, rms_in = norm_rows(resid_in, full_gattn)
    normed_bf = normed_in.astype(jnp.bfloat16)
    qkv = matmul(normed_bf, qkv_set)
    query_raw = by_head(qkv[:, :q_width])
    key_raw = by_head(qkv[:, q_width : q_width + k_width])
    value_bf = by_head(qkv[:, q_width + k_width :].astype(jnp.bfloat16))
    query_normed, query_unit, query_rms = norm_rows(query_raw, full_gquery)
    key_normed, key_unit, key_rms = norm_rows(key_raw, full_gkey)
    shared = (KVH, head_share * tok_rows, -1)
    query_bf = rotate(query_normed, cos_tab, sin_tab).astype(jnp.bfloat16).reshape(shared)
    key_bf = rotate(key_normed, cos_tab, sin_tab).astype(jnp.bfloat16)
    scores = batched("kmd,ksd->kms", query_bf, key_bf).reshape(QH, tok_rows, -1) * score_scale
    log_total = jnp.log(jnp.sum(jnp.where(key_mask, jnp.exp(scores), 0.0), axis=-1, keepdims=True))
    attn_probs = jnp.where(key_mask, jnp.exp(scores - log_total), 0.0)
    probs_bf = attn_probs.astype(jnp.bfloat16).reshape(shared)
    mixed = batched("kms,ksd->kmd", probs_bf, value_bf).astype(jnp.bfloat16)
    mixed_bf = by_token(mixed.reshape(QH, tok_rows, -1))
    resid_mid = resid_in + matmul(mixed_bf, out_set)
    normed_mid, unit_mid, rms_mid = norm_rows(resid_mid, full_gffn)
    hidden_in = normed_mid.astype(jnp.bfloat16)
    gate_proj = matmul(hidden_in, gate_set)
    up_proj = matmul(hidden_in, up_set)
    gate_proj, up_proj = lax.optimization_barrier((gate_proj, up_proj))
    gate_sig = jax.nn.sigmoid(gate_proj)
    gate_act = gate_proj * gate_sig
    hidden_bf = (gate_act * up_proj).astype(jnp.bfloat16)

    live_rows = (doc_ids >= 0).astype(jnp.float32)[:, None]
    grad_y = cotangent.astype(jnp.float32) * live_rows
    grad_y_bf = grad_y.astype(jnp.bfloat16)
    block_out = (resid_mid + matmul(hidden_bf, down_set)).astype(jnp.bfloat16)

    grad_hidden = lax.optimization_barrier(matmul_t(grad_y_bf, down_set))
    grad_gate_bf = (grad_hidden * up_proj * gate_sig * (1.0 + gate_proj * (1.0 - gate_sig))).astype(
        jnp.bfloat16
    )
    grad_up_bf = (grad_hidden * gate_act).astype(jnp.bfloat16)
    grad_norm_mid = matmul_t(grad_gate_bf, gate_set) + matmul_t(grad_up_bf, up_set)
    back_mid, part_gffn = norm_back(grad_norm_mid, unit_mid, rms_mid, full_gffn)
    grad_mid = grad_y + back_mid
    grad_mid_bf = grad_mid.astype(jnp.bfloat16)
    grad_mixed_bf = by_head(matmul_t(grad_mid_bf, out_set).astype(jnp.bfloat16)).reshape(shared)
    grad_scores = batched("kmd,ksd->kms", grad_mixed_bf, value_bf).reshape(attn_probs.shape)
    grad_value_bf = by_token(batched("kms,kmd->ksd", probs_bf, grad_mixed_bf).astype(jnp.bfloat16))
    row_dot = jnp.sum(attn_probs * grad_scores, axis=-1, keepdims=True)
    grad_logits = (attn_probs * (grad_scores - row_dot) * score_scale).astype(jnp.bfloat16).reshape(shared)
    grad_query_rot = batched("kms,ksd->kmd", grad_logits, key_bf).reshape(query_raw.shape)
    grad_key_rot = batched("kms,kmd->ksd", grad_logits, query_bf)
    grad_query_raw, part_gquery = norm_back(
        rotate_back(grad_query_rot, cos_tab, sin_tab), query_unit, query_rms, full_gquery
    )
    grad_key_raw, part_gkey = norm_back(
        rotate_back(grad_key_rot, cos_tab, sin_tab), key_unit, key_rms, full_gkey
    )
    grad_query_bf = by_token(grad_query_raw.astype(jnp.bfloat16))
    grad_key_bf = by_token(grad_key_raw.astype(jnp.bfloat16))
    grad_qkv_bf = jnp.concatenate([grad_query_bf, grad_key_bf, grad_value_bf], axis=1)
    grad_norm_in = matmul_t(grad_qkv_bf, qkv_set)
    back_in, part_gattn = norm_back(grad_norm_in, unit_in, rms_in, full_gattn)
    grad_tokens = grad_mid + back_in
    part_gains = jnp.concatenate(
        [
            p.reshape(n_shard, -1)
            for p in (part_gattn, part_gffn, part_gquery, part_gkey)
        ],
        axis=1,
    )
    part_gains = part_gains.astype(jnp.bfloat16).astype(jnp.float32)
    flat = part_gains.reshape(-1)
    flat = jnp.pad(flat, (0, -flat.shape[0] % 1024)).reshape(-1, 128)
    (grad_down, grad_gate, grad_up, grad_qkv, grad_out), sum_gains = reduce_grads(
        hidden_bf, hidden_in, normed_bf, mixed_bf,
        grad_y_bf, grad_gate_bf, grad_up_bf, grad_qkv_bf, grad_mid_bf,
        flat, n_rep, n_shard,
    )
    ends = [q_width, q_width + k_width]
    grad_query, grad_key, grad_value = jnp.split(grad_qkv, ends, axis=1)
    sum_gains = sum_gains.reshape(-1)[: part_gains.size].reshape(part_gains.shape)
    own_gains = lax.dynamic_index_in_dim(sum_gains, lax.axis_index("shard"), axis=0, keepdims=False)
    grad_gattn, grad_gffn, grad_gquery, grad_gkey = (
        own_gains[end - size : end] for size, end in zip(gain_sizes, gain_ends)
    )
    return (
        block_out,
        grad_tokens,
        grad_query,
        grad_key,
        grad_value,
        grad_out,
        grad_gate,
        grad_up,
        grad_down,
        grad_gattn,
        grad_gffn,
        grad_gquery,
        grad_gkey,
    )


def solution(mesh):
    return jax.shard_map(
        functools.partial(local, mesh.shape["rep"], mesh.shape["shard"]),
        mesh=mesh,
        in_specs=(
            P(("rep", "shard"), None),
            P(("rep", "shard"), None),
            P(("rep", "shard")),
            P("shard", None),
            P("shard", None),
            P("shard", None),
            P("shard", None),
            P("shard", None),
            P("shard", None),
            P("shard", None),
            P("shard"),
            P("shard"),
            P("shard"),
            P("shard"),
        ),
        out_specs=(
            P(("rep", "shard"), None),
            P(("rep", "shard"), None),
            P("shard", None),
            P("shard", None),
            P("shard", None),
            P("shard", None),
            P("shard", None),
            P("shard", None),
            P("shard", None),
            P("shard"),
            P("shard"),
            P("shard"),
            P("shard"),
        ),
        check_vma=False,
    )
```
